512 devices in a mesh: gz: 32 (over y_lo, z), gy: 16 (over y_hi, x, core).
Axes of the slice: x: 4, y: 8 (y_hi: 2, y_lo: 4; y = y_hi * 4 + y_lo), z: 8, core: 2. Of those that a mesh axis runs over, the one named last changes fastest.
Arguments:
- features: bfloat16 [64, 64, 128, 128], P(None, 'gz', 'gy'), may hold values from -6 to 6
- conv_weight: bfloat16 [3, 3, 64, 192], replicated, may hold values from -0.15625 to 0.15625
- down_weight: bfloat16 [2, 2, 128, 128], replicated, may hold values from -0.25 to 0.25
- cotangent: bfloat16 [128, 32, 4096], P(None, 'gz', 'gy'), may hold values from -6 to 6
Outputs:
- section_out: bfloat16 [128, 32, 4096], P(None, 'gz', 'gy')
- grad_field: float32 [64, 64, 128, 128], P(None, 'gz', 'gy')
- grad_conv: float32 [3, 3, 64, 192], replicated
- grad_down: float32 [2, 2, 128, 128], replicated
The draws below stay inside these ranges and needn't reach their ends.
All inputs are finite; a program needn't handle non-finite values.
Results may differ from the reference program's by a relative error of at most 0.005.
Values may be sent and summed in bfloat16 or wider, within the bound.
A program may use at most 64 MiB of HBM per device.

```python
import math
import jax
import jax.numpy as jnp

C = 64
COUT = 128
NX = 128
NZ = 64
NY = 128


def steps_of(stream_key, shape, shards, smallest, high):
    loudness, own = 1.0, jax.random.fold_in(stream_key, 6)
    for position, blocks in shards:
        draws = jnp.exp(jax.random.uniform(jax.random.fold_in(own, position), (blocks,), jnp.float32, smallest / len(shards), high / len(shards)))
        loudness = loudness * jnp.repeat(draws, shape[position] // blocks).reshape([-1 if axis == position else 1 for axis in range(len(shape))])
    return loudness


def noise(key, dims, width, bound, shards=(), dtype=jnp.bfloat16):
    values = jax.random.normal(key, dims, jnp.float32) * width
    if len(shards) > 0:
        values = steps_of(key, dims, shards, -0.22, 0.18) * values
    return jnp.clip(values, min=-bound, max=bound).astype(dtype)


def setup_inputs(seed: int = 0) -> dict:
    key_list = jax.random.split(jax.random.key(seed), 5)
    return {
        "features": noise(key_list[0], (C, NZ, NY, NX), 1.0, 6.0, ((1, 32), (2, 16))),
        "conv_weight": noise(key_list[1], (3, 3, C, 3 * C), (27 * C) ** -0.5, 0.15625),
        "down_weight": noise(key_list[2], (2, 2, COUT, 2 * C), (8 * C) ** -0.5, 0.25),
        "cotangent": noise(key_list[3], (COUT, NZ // 2, (NY // 2) * (NX // 2)), 1.0, 6.0, ((1, 32), (2, 16))),
    }


def reference(features, conv_weight, down_weight, cotangent):
    channels = features.shape[0]
    out_channels = down_weight.shape[2]
    grad_scale = 1.0 / math.sqrt(NZ * NY * NX)
    source = features.astype(jnp.float32)
    preact = jnp.zeros(features.shape, jnp.float32)
    for tap_z in range(3):
        for tap_y in range(3):
            for tap_x in range(3):
                shifted = jnp.roll(source, (1 - tap_z, 1 - tap_y, 1 - tap_x), axis=(1, 2, 3))
                tap_block = conv_weight[tap_z, tap_y][:, tap_x * channels:(tap_x + 1) * channels].astype(jnp.float32)
                preact = preact + jnp.einsum('oi,izyx->ozyx', tap_block, shifted)
    hidden = jax.nn.silu(preact).astype(jnp.bfloat16)
    blocks = hidden.astype(jnp.float32).reshape(channels, NZ // 2, 2, NY // 2, 2, NX // 2, 2)
    down_split = down_weight.astype(jnp.float32).reshape(2, 2, out_channels, 2, channels)
    coarse = jnp.einsum('aboei,iZaYbXe->oZYX', down_split, blocks)
    section_out = coarse.reshape(out_channels, NZ // 2, NY // 2 * (NX // 2)).astype(jnp.bfloat16)
    coarse_cot = cotangent.astype(jnp.float32).reshape(out_channels, NZ // 2, NY // 2, NX // 2)
    hidden_grad = jnp.einsum('aboei,oZYX->iZaYbXe', down_split, coarse_cot).reshape(channels, NZ, NY, NX)
    grad_down = jnp.einsum('oZYX,iZaYbXe->aboei', coarse_cot, blocks).reshape(2, 2, out_channels, 2 * channels) * grad_scale
    gate_sig = jax.nn.sigmoid(preact)
    gate_grad = (hidden_grad * gate_sig * (1.0 + preact * (1.0 - gate_sig))).astype(jnp.bfloat16)
    gate_wide = gate_grad.astype(jnp.float32)
    grad_field = jnp.zeros(features.shape, jnp.float32)
    kernel_rows = []
    for tap_z in range(3):
        row_list = []
        for tap_y in range(3):
            pieces = []
            for tap_x in range(3):
                shifted = jnp.roll(source, (1 - tap_z, 1 - tap_y, 1 - tap_x), axis=(1, 2, 3))
                pieces.append(jnp.einsum('ozyx,izyx->oi', gate_wide, shifted))
                tap_block = conv_weight[tap_z, tap_y][:, tap_x * channels:(tap_x + 1) * channels].astype(jnp.float32)
                contrib = jnp.einsum('oi,ozyx->izyx', tap_block, gate_wide)
                grad_field = grad_field + jnp.roll(contrib, (tap_z - 1, tap_y - 1, tap_x - 1), axis=(1, 2, 3))
            row_list.append(jnp.concatenate(pieces, axis=1))
        kernel_rows.append(jnp.stack(row_list, axis=0))
    grad_conv = jnp.stack(kernel_rows, axis=0) * grad_scale
    return (section_out, grad_field, grad_conv, grad_down)
```

```python
import functools
import math

import jax
import jax.numpy as jnp
from jax import lax
from jax.experimental import pallas as pl
from jax.experimental.pallas import tpu as pltpu
from jax.sharding import PartitionSpec as P

MESH_ID = pl.DeviceIdType.MESH
BIT_ORDER = (("gy", 0), ("gy", 1), ("gz", 0), ("gz", 3), ("gy", 2), ("gz", 1), ("gz", 4), ("gz", 2), ("gy", 3))
HALVINGS = 4


def extended(cells, sides, width):
    for axis, dim in sides:
        count = lax.axis_size(axis)
        head = lax.slice_in_dim(cells, 0, width, axis=dim)
        tail = lax.slice_in_dim(cells, cells.shape[dim] - width, cells.shape[dim], axis=dim)
        cells = jnp.concatenate(
            [
                lax.ppermute(tail, axis, [(i, (i + 1) % count) for i in range(count)]),
                cells,
                lax.ppermute(head, axis, [((i + 1) % count, i) for i in range(count)]),
            ],
            axis=dim,
        )
    return cells


def widen(framed):
    return jnp.concatenate([jnp.roll(framed, 1 - tap_x, axis=3) for tap_x in range(3)], axis=0)


def fold_along(spread, channels):
    result = jnp.roll(spread[0:channels], -1, axis=3)
    result = result + spread[channels : 2 * channels]
    result = result + jnp.roll(spread[2 * channels : 3 * channels], 1, axis=3)
    return result


def mesh_bits():
    sizes = {"gz": lax.axis_size("gz"), "gy": lax.axis_size("gy")}
    return [(axis, b) for axis, b in BIT_ORDER if (1 << b) < sizes[axis]]


def allreduce_kernel(bits, halvings, x_ref, o_ref, *scratch):
    halve_bufs = scratch[:halvings]
    work, double_buf, send_sems, recv_sems = scratch[halvings:]
    here = {"gz": lax.axis_index("gz"), "gy": lax.axis_index("gy")}

    def bit_of(axis, b):
        return (here[axis] // (1 << b)) % 2

    def partner(axis, b):
        flip = here[axis] + (1 - 2 * bit_of(axis, b)) * (1 << b)
        return (flip, here["gy"]) if axis == "gz" else (here["gz"], flip)

    barrier = pltpu.get_barrier_semaphore()
    for axis, b in bits:
        pl.semaphore_signal(barrier, inc=1, device_id=partner(axis, b), device_id_type=MESH_ID)
    pl.semaphore_wait(barrier, len(bits))

    def exchange(step, axis, b, src, dst):
        copy = pltpu.make_async_remote_copy(
            src_ref=src,
            dst_ref=dst,
            send_sem=send_sems.at[step],
            recv_sem=recv_sems.at[step],
            device_id=partner(axis, b),
            device_id_type=MESH_ID,
        )
        copy.start()
        copy.wait()

    lo, length, step = 0, o_ref.shape[0], 0
    for k in range(halvings):
        axis, b = bits[k]
        half = length // 2
        bit = bit_of(axis, b)
        keep = pl.multiple_of(lo + bit * half, 8)
        give = pl.multiple_of(lo + (1 - bit) * half, 8)
        source = x_ref if k == 0 else work
        exchange(step, axis, b, source.at[pl.ds(give, half)], halve_bufs[k])
        work[pl.ds(keep, half)] = source[pl.ds(keep, half)] + halve_bufs[k][...]
        lo, length, step = keep, half, step + 1
    for j, (axis, b) in enumerate(bits[halvings:]):
        exchange(step, axis, b, work.at[pl.ds(lo, length)], double_buf.at[j])
        work[pl.ds(lo, length)] = work[pl.ds(lo, length)] + double_buf[j]
        step += 1
    o_ref[pl.ds(lo, length)] = work[pl.ds(lo, length)]
    for k in reversed(range(halvings)):
        axis, b = bits[k]
        region = o_ref.at[pl.ds(lo, length)]
        exchange(step, axis, b, region, region)
        lo = pl.multiple_of(lo - bit_of(axis, b) * length, 8)
        length, step = length * 2, step + 1


def allreduce(flat, halvings=HALVINGS):
    bits = mesh_bits()
    halvings = min(halvings, len(bits))
    rows = flat.shape[0]
    segment = rows >> halvings
    steps = len(bits) + halvings
    scratch = [pltpu.VMEM((rows >> (k + 1), 128), jnp.float32) for k in range(halvings)]
    scratch += [
        pltpu.VMEM(flat.shape, jnp.float32),
        pltpu.VMEM((max(len(bits) - halvings, 1), segment, 128), jnp.float32),
        pltpu.SemaphoreType.DMA((steps,)),
        pltpu.SemaphoreType.DMA((steps,)),
    ]
    return pl.pallas_call(
        functools.partial(allreduce_kernel, bits, halvings),
        out_shape=jax.ShapeDtypeStruct(flat.shape, jnp.float32),
        in_specs=[pl.BlockSpec(memory_space=pltpu.VMEM)],
        out_specs=pl.BlockSpec(memory_space=pltpu.VMEM),
        scratch_shapes=scratch,
        compiler_params=pltpu.CompilerParams(collective_id=0, has_side_effects=True),
    )(flat)


def summed_gradients(local_conv, local_down):
    sizes = (local_conv.size, local_down.size)
    flat = jnp.concatenate([local_conv.reshape(-1), local_down.reshape(-1)])
    unit = 128 * 8 << HALVINGS
    padded = -(-flat.size // unit) * unit
    flat = jnp.pad(flat, (0, padded - flat.size)).reshape(-1, 128)
    total = allreduce(flat).reshape(-1)
    return (
        total[: sizes[0]].reshape(local_conv.shape),
        total[sizes[0] : sizes[0] + sizes[1]].reshape(local_down.shape),
    )


def body(features, conv_weight, down_weight, cotangent):
    channels, plane_count, row_count, breadth = features.shape
    out_channels = down_weight.shape[2]
    cell_count = plane_count * row_count * breadth * lax.axis_size("gz") * lax.axis_size("gy")
    grad_scale = 1.0 / math.sqrt(cell_count)
    framed = extended(features, (("gz", 1), ("gy", 2)), 1)
    columns = widen(framed)
    preact = jnp.zeros((channels, plane_count, row_count, breadth), jnp.float32)
    for tap_z in range(3):
        for tap_y in range(3):
            window = columns[:, tap_z : tap_z + plane_count, tap_y : tap_y + row_count]
            preact = preact + jnp.einsum(
                "oj,jzyx->ozyx",
                conv_weight[tap_z, tap_y],
                window,
                preferred_element_type=jnp.float32,
            )
    hidden = jax.nn.silu(preact).astype(jnp.bfloat16)
    blocks = hidden.reshape(channels, plane_count // 2, 2, row_count // 2, 2, breadth // 2, 2)
    down_split = down_weight.reshape(2, 2, out_channels, 2, channels)
    coarse = jnp.einsum(
        "aboei,iZaYbXe->oZYX", down_split, blocks, preferred_element_type=jnp.float32
    )
    section_out = coarse.reshape(out_channels, plane_count // 2, -1).astype(jnp.bfloat16)
    coarse_cot = cotangent.reshape(out_channels, plane_count // 2, row_count // 2, breadth // 2)
    hidden_grad = jnp.einsum(
        "aboei,oZYX->iZaYbXe", down_split, coarse_cot, preferred_element_type=jnp.float32
    )
    hidden_grad = hidden_grad.reshape(channels, plane_count, row_count, breadth)
    local_down = jnp.einsum(
        "oZYX,iZaYbXe->aboei", coarse_cot, blocks, preferred_element_type=jnp.float32
    )
    local_down = local_down.reshape(2, 2, out_channels, 2 * channels)
    gate_sig = jax.nn.sigmoid(preact)
    gate_grad = (hidden_grad * gate_sig * (1.0 + preact * (1.0 - gate_sig))).astype(jnp.bfloat16)
    kernel_rows = []
    for tap_z in range(3):
        row_list = []
        for tap_y in range(3):
            window = columns[:, tap_z : tap_z + plane_count, tap_y : tap_y + row_count]
            row_list.append(
                jnp.einsum("ozyx,jzyx->oj", gate_grad, window, preferred_element_type=jnp.float32)
            )
        kernel_rows.append(jnp.stack(row_list, axis=0))
    local_conv = jnp.stack(kernel_rows, axis=0)
    spread = jnp.zeros((3 * channels, plane_count + 2, row_count + 2, breadth), jnp.float32)
    for tap_z in range(3):
        for tap_y in range(3):
            term = jnp.einsum(
                "oj,ozyx->jzyx",
                conv_weight[tap_z, tap_y],
                gate_grad,
                preferred_element_type=jnp.float32,
            )
            spread = spread.at[:, tap_z : tap_z + plane_count, tap_y : tap_y + row_count].add(term)
    folded = fold_along(spread, channels)
    bordered = extended(folded.astype(jnp.bfloat16), (("gz", 1), ("gy", 2)), 1).astype(folded.dtype)
    plane_fold = bordered[:, 2 : plane_count + 2]
    plane_fold = plane_fold.at[:, 0].add(bordered[:, 0])
    plane_fold = plane_fold.at[:, plane_count - 1].add(bordered[:, plane_count + 3])
    row_fold = plane_fold[:, :, 2 : row_count + 2]
    row_fold = row_fold.at[:, :, 0].add(plane_fold[:, :, 0])
    row_fold = row_fold.at[:, :, row_count - 1].add(plane_fold[:, :, row_count + 3])
    summed_conv, summed_down = summed_gradients(local_conv, local_down)
    grad_conv = summed_conv * grad_scale
    grad_down = summed_down * grad_scale
    return (section_out, row_fold, grad_conv, grad_down)


def solution(mesh):
    return jax.shard_map(
        body,
        mesh=mesh,
        in_specs=(P(None, "gz", "gy", None), P(), P(), P(None, "gz", "gy")),
        out_specs=(P(None, "gz", "gy"), P(None, "gz", "gy", None), P(), P()),
        check_vma=False,
    )
```

```python
import functools
import math

import jax
import jax.numpy as jnp
from jax import lax
from jax.experimental import pallas as pl
from jax.experimental.pallas import tpu as pltpu
from jax.sharding import PartitionSpec as P

MESH_ID = pl.DeviceIdType.MESH
BIT_ORDER = (("gy", 0), ("gy", 1), ("gz", 0), ("gz", 3), ("gy", 2), ("gz", 1), ("gz", 4), ("gz", 2), ("gy", 3))
HALVINGS = 4


def extended(cells, sides, width):
    for axis, dim in sides:
        count = lax.axis_size(axis)
        head = lax.slice_in_dim(cells, 0, width, axis=dim)
        tail = lax.slice_in_dim(cells, cells.shape[dim] - width, cells.shape[dim], axis=dim)
        cells = jnp.concatenate(
            [
                lax.ppermute(tail, axis, [(i, (i + 1) % count) for i in range(count)]),
                cells,
                lax.ppermute(head, axis, [((i + 1) % count, i) for i in range(count)]),
            ],
            axis=dim,
        )
    return cells


def widen(framed):
    return jnp.concatenate([jnp.roll(framed, 1 - tap_x, axis=3) for tap_x in range(3)], axis=0)


def fold_along(spread, channels):
    result = jnp.roll(spread[0:channels], -1, axis=3)
    result = result + spread[channels : 2 * channels]
    result = result + jnp.roll(spread[2 * channels : 3 * channels], 1, axis=3)
    return result


NEIGHBOURS = ((1, 0), (-1, 0), (0, 1), (0, -1), (1, 1), (1, -1), (-1, 1), (-1, -1))


def halo_kernel(offsets, *refs):
    count = len(offsets)
    sources, targets = refs[:count], refs[count : 2 * count]
    send_sems, recv_sems = refs[2 * count :]
    sizes = (lax.axis_size("gz"), lax.axis_size("gy"))
    here = (lax.axis_index("gz"), lax.axis_index("gy"))

    def device(dz, dy):
        return ((here[0] + dz + sizes[0]) % sizes[0], (here[1] + dy + sizes[1]) % sizes[1])

    barrier = pltpu.get_barrier_semaphore()
    for dz, dy in offsets:
        pl.semaphore_signal(barrier, inc=1, device_id=device(dz, dy), device_id_type=MESH_ID)
    pl.semaphore_wait(barrier, count)
    copies = []
    for i, (dz, dy) in enumerate(offsets):
        copy = pltpu.make_async_remote_copy(
            src_ref=sources[i],
            dst_ref=targets[i],
            send_sem=send_sems.at[i],
            recv_sem=recv_sems.at[i],
            device_id=device(dz, dy),
            device_id_type=MESH_ID,
        )
        copy.start()
        copies.append(copy)
    for copy in copies:
        copy.wait()


def halo_swap(pieces, collective_id):
    flat = [p.reshape(-1, 128) for p in pieces]
    vmem = pl.BlockSpec(memory_space=pltpu.VMEM)
    got = pl.pallas_call(
        functools.partial(halo_kernel, NEIGHBOURS),
        out_shape=[jax.ShapeDtypeStruct(f.shape, f.dtype) for f in flat],
        in_specs=[vmem] * len(flat),
        out_specs=[vmem] * len(flat),
        scratch_shapes=[pltpu.SemaphoreType.DMA((len(flat),)), pltpu.SemaphoreType.DMA((len(flat),))],
        compiler_params=pltpu.CompilerParams(collective_id=collective_id, has_side_effects=True),
    )(*flat)
    return [g.reshape(p.shape) for g, p in zip(got, pieces)]


def ranges(shift, count, border):
    if shift == 1:
        return slice(border + count - 1, border + count)
    if shift == -1:
        return slice(border, border + 1)
    return slice(border, border + count)


def framed_features(features):
    _, planes, rows, _ = features.shape
    pieces = [features[:, ranges(dz, planes, 0), ranges(dy, rows, 0)] for dz, dy in NEIGHBOURS]
    got = dict(zip(NEIGHBOURS, halo_swap(pieces, 1)))
    lines = []
    for dz in (1, 0, -1):
        middle = features if dz == 0 else got[(dz, 0)]
        lines.append(jnp.concatenate([got[(dz, 1)], middle, got[(dz, -1)]], axis=2))
    return jnp.concatenate(lines, axis=1)


def folded_grad(spread):
    _, planes, rows, _ = spread.shape
    planes, rows = planes - 2, rows - 2
    own = spread[:, 1 : planes + 1, 1 : rows + 1]
    pieces = []
    for dz, dy in NEIGHBOURS:
        zs = slice(planes + 1, planes + 2) if dz == 1 else slice(0, 1) if dz == -1 else slice(1, planes + 1)
        ys = slice(rows + 1, rows + 2) if dy == 1 else slice(0, 1) if dy == -1 else slice(1, rows + 1)
        pieces.append(spread[:, zs, ys].astype(jnp.bfloat16))
    got = halo_swap(pieces, 2)
    for (dz, dy), piece in zip(NEIGHBOURS, got):
        own = own.at[:, ranges(-dz, planes, 0), ranges(-dy, rows, 0)].add(piece.astype(own.dtype))
    return own


def mesh_bits():
    sizes = {"gz": lax.axis_size("gz"), "gy": lax.axis_size("gy")}
    return [(axis, b) for axis, b in BIT_ORDER if (1 << b) < sizes[axis]]


def allreduce_kernel(bits, halvings, x_ref, o_ref, *scratch):
    halve_bufs = scratch[:halvings]
    work, double_buf, send_sems, recv_sems = scratch[halvings:]
    here = {"gz": lax.axis_index("gz"), "gy": lax.axis_index("gy")}

    def bit_of(axis, b):
        return (here[axis] // (1 << b)) % 2

    def partner(axis, b):
        flip = here[axis] + (1 - 2 * bit_of(axis, b)) * (1 << b)
        return (flip, here["gy"]) if axis == "gz" else (here["gz"], flip)

    barrier = pltpu.get_barrier_semaphore()
    for axis, b in bits:
        pl.semaphore_signal(barrier, inc=1, device_id=partner(axis, b), device_id_type=MESH_ID)
    pl.semaphore_wait(barrier, len(bits))

    def exchange(step, axis, b, src, dst):
        copy = pltpu.make_async_remote_copy(
            src_ref=src,
            dst_ref=dst,
            send_sem=send_sems.at[step],
            recv_sem=recv_sems.at[step],
            device_id=partner(axis, b),
            device_id_type=MESH_ID,
        )
        copy.start()
        copy.wait()

    lo, length, step = 0, o_ref.shape[0], 0
    for k in range(halvings):
        axis, b = bits[k]
        half = length // 2
        bit = bit_of(axis, b)
        keep = pl.multiple_of(lo + bit * half, 8)
        give = pl.multiple_of(lo + (1 - bit) * half, 8)
        source = x_ref if k == 0 else work
        exchange(step, axis, b, source.at[pl.ds(give, half)], halve_bufs[k])
        work[pl.ds(keep, half)] = source[pl.ds(keep, half)] + halve_bufs[k][...]
        lo, length, step = keep, half, step + 1
    for j, (axis, b) in enumerate(bits[halvings:]):
        exchange(step, axis, b, work.at[pl.ds(lo, length)], double_buf.at[j])
        work[pl.ds(lo, length)] = work[pl.ds(lo, length)] + double_buf[j]
        step += 1
    o_ref[pl.ds(lo, length)] = work[pl.ds(lo, length)]
    for k in reversed(range(halvings)):
        axis, b = bits[k]
        region = o_ref.at[pl.ds(lo, length)]
        exchange(step, axis, b, region, region)
        lo = pl.multiple_of(lo - bit_of(axis, b) * length, 8)
        length, step = length * 2, step + 1


def allreduce(flat, halvings=HALVINGS):
    bits = mesh_bits()
    halvings = min(halvings, len(bits))
    rows = flat.shape[0]
    segment = rows >> halvings
    steps = len(bits) + halvings
    scratch = [pltpu.VMEM((rows >> (k + 1), 128), jnp.float32) for k in range(halvings)]
    scratch += [
        pltpu.VMEM(flat.shape, jnp.float32),
        pltpu.VMEM((max(len(bits) - halvings, 1), segment, 128), jnp.float32),
        pltpu.SemaphoreType.DMA((steps,)),
        pltpu.SemaphoreType.DMA((steps,)),
    ]
    return pl.pallas_call(
        functools.partial(allreduce_kernel, bits, halvings),
        out_shape=jax.ShapeDtypeStruct(flat.shape, jnp.float32),
        in_specs=[pl.BlockSpec(memory_space=pltpu.VMEM)],
        out_specs=pl.BlockSpec(memory_space=pltpu.VMEM),
        scratch_shapes=scratch,
        compiler_params=pltpu.CompilerParams(collective_id=0, has_side_effects=True),
    )(flat)


def summed_gradients(local_conv, local_down):
    sizes = (local_conv.size, local_down.size)
    flat = jnp.concatenate([local_conv.reshape(-1), local_down.reshape(-1)])
    unit = 128 * 8 << HALVINGS
    padded = -(-flat.size // unit) * unit
    flat = jnp.pad(flat, (0, padded - flat.size)).reshape(-1, 128)
    total = allreduce(flat).reshape(-1)
    return (
        total[: sizes[0]].reshape(local_conv.shape),
        total[sizes[0] : sizes[0] + sizes[1]].reshape(local_down.shape),
    )


def body(features, conv_weight, down_weight, cotangent):
    channels, plane_count, row_count, breadth = features.shape
    out_channels = down_weight.shape[2]
    cell_count = plane_count * row_count * breadth * lax.axis_size("gz") * lax.axis_size("gy")
    grad_scale = 1.0 / math.sqrt(cell_count)
    framed = framed_features(features)
    columns = widen(framed)
    preact = jnp.zeros((channels, plane_count, row_count, breadth), jnp.float32)
    for tap_z in range(3):
        for tap_y in range(3):
            window = columns[:, tap_z : tap_z + plane_count, tap_y : tap_y + row_count]
            preact = preact + jnp.einsum(
                "oj,jzyx->ozyx",
                conv_weight[tap_z, tap_y],
                window,
                preferred_element_type=jnp.float32,
            )
    hidden = jax.nn.silu(preact).astype(jnp.bfloat16)
    blocks = hidden.reshape(channels, plane_count // 2, 2, row_count // 2, 2, breadth // 2, 2)
    down_split = down_weight.reshape(2, 2, out_channels, 2, channels)
    coarse = jnp.einsum(
        "aboei,iZaYbXe->oZYX", down_split, blocks, preferred_element_type=jnp.float32
    )
    section_out = coarse.reshape(out_channels, plane_count // 2, -1).astype(jnp.bfloat16)
    coarse_cot = cotangent.reshape(out_channels, plane_count // 2, row_count // 2, breadth // 2)
    hidden_grad = jnp.einsum(
        "aboei,oZYX->iZaYbXe", down_split, coarse_cot, preferred_element_type=jnp.float32
    )
    hidden_grad = hidden_grad.reshape(channels, plane_count, row_count, breadth)
    local_down = jnp.einsum(
        "oZYX,iZaYbXe->aboei", coarse_cot, blocks, preferred_element_type=jnp.float32
    )
    local_down = local_down.reshape(2, 2, out_channels, 2 * channels)
    gate_sig = jax.nn.sigmoid(preact)
    gate_grad = (hidden_grad * gate_sig * (1.0 + preact * (1.0 - gate_sig))).astype(jnp.bfloat16)
    kernel_rows = []
    for tap_z in range(3):
        row_list = []
        for tap_y in range(3):
            window = columns[:, tap_z : tap_z + plane_count, tap_y : tap_y + row_count]
            row_list.append(
                jnp.einsum("ozyx,jzyx->oj", gate_grad, window, preferred_element_type=jnp.float32)
            )
        kernel_rows.append(jnp.stack(row_list, axis=0))
    local_conv = jnp.stack(kernel_rows, axis=0)
    spread = jnp.zeros((3 * channels, plane_count + 2, row_count + 2, breadth), jnp.float32)
    for tap_z in range(3):
        for tap_y in range(3):
            term = jnp.einsum(
                "oj,ozyx->jzyx",
                conv_weight[tap_z, tap_y],
                gate_grad,
                preferred_element_type=jnp.float32,
            )
            spread = spread.at[:, tap_z : tap_z + plane_count, tap_y : tap_y + row_count].add(term)
    row_fold = folded_grad(fold_along(spread, channels))
    summed_conv, summed_down = summed_gradients(local_conv, local_down)
    grad_conv = summed_conv * grad_scale
    grad_down = summed_down * grad_scale
    return (section_out, row_fold, grad_conv, grad_down)


def solution(mesh):
    return jax.shard_map(
        body,
        mesh=mesh,
        in_specs=(P(None, "gz", "gy", None), P(), P(), P(None, "gz", "gy")),
        out_specs=(P(None, "gz", "gy"), P(None, "gz", "gy", None), P(), P()),
        check_vma=False,
    )
```

```python
import functools
import math

import jax
import jax.numpy as jnp
from jax import lax
from jax.experimental import pallas as pl
from jax.experimental.pallas import tpu as pltpu
from jax.sharding import PartitionSpec as P

MESH_ID = pl.DeviceIdType.MESH
BIT_ORDER = (("gy", 0), ("gy", 1), ("gz", 0), ("gz", 3), ("gy", 2), ("gz", 1), ("gz", 4), ("gz", 2), ("gy", 3))
HALVINGS = 4


def extended(cells, sides, width):
    for axis, dim in sides:
        count = lax.axis_size(axis)
        head = lax.slice_in_dim(cells, 0, width, axis=dim)
        tail = lax.slice_in_dim(cells, cells.shape[dim] - width, cells.shape[dim], axis=dim)
        cells = jnp.concatenate(
            [
                lax.ppermute(tail, axis, [(i, (i + 1) % count) for i in range(count)]),
                cells,
                lax.ppermute(head, axis, [((i + 1) % count, i) for i in range(count)]),
            ],
            axis=dim,
        )
    return cells


def widen(framed):
    return jnp.concatenate([jnp.roll(framed, 1 - tap_x, axis=3) for tap_x in range(3)], axis=0)


def fold_along(spread, channels):
    result = jnp.roll(spread[0:channels], -1, axis=3)
    result = result + spread[channels : 2 * channels]
    result = result + jnp.roll(spread[2 * channels : 3 * channels], 1, axis=3)
    return result


NEIGHBOURS = ((1, 0), (-1, 0), (0, 1), (0, -1), (1, 1), (1, -1), (-1, 1), (-1, -1))


def halo_kernel(offsets, *refs):
    count = len(offsets)
    sources, targets = refs[:count], refs[count : 2 * count]
    send_sems, recv_sems = refs[2 * count :]
    sizes = (lax.axis_size("gz"), lax.axis_size("gy"))
    here = (lax.axis_index("gz"), lax.axis_index("gy"))

    def device(dz, dy):
        return ((here[0] + dz + sizes[0]) % sizes[0], (here[1] + dy + sizes[1]) % sizes[1])

    barrier = pltpu.get_barrier_semaphore()
    for dz, dy in offsets:
        pl.semaphore_signal(barrier, inc=1, device_id=device(dz, dy), device_id_type=MESH_ID)
    pl.semaphore_wait(barrier, count)
    copies = []
    for i, (dz, dy) in enumerate(offsets):
        copy = pltpu.make_async_remote_copy(
            src_ref=sources[i],
            dst_ref=targets[i],
            send_sem=send_sems.at[i],
            recv_sem=recv_sems.at[i],
            device_id=device(dz, dy),
            device_id_type=MESH_ID,
        )
        copy.start()
        copies.append(copy)
    for copy in copies:
        copy.wait()


def halo_swap(pieces, collective_id):
    flat = [p.reshape(-1, 128) for p in pieces]
    vmem = pl.BlockSpec(memory_space=pltpu.VMEM)
    got = pl.pallas_call(
        functools.partial(halo_kernel, NEIGHBOURS),
        out_shape=[jax.ShapeDtypeStruct(f.shape, f.dtype) for f in flat],
        in_specs=[vmem] * len(flat),
        out_specs=[vmem] * len(flat),
        scratch_shapes=[pltpu.SemaphoreType.DMA((len(flat),)), pltpu.SemaphoreType.DMA((len(flat),))],
        compiler_params=pltpu.CompilerParams(collective_id=collective_id, has_side_effects=True),
    )(*flat)
    return [g.reshape(p.shape) for g, p in zip(got, pieces)]


def ranges(shift, count, border):
    if shift == 1:
        return slice(border + count - 1, border + count)
    if shift == -1:
        return slice(border, border + 1)
    return slice(border, border + count)


def framed_features(features):
    _, planes, rows, _ = features.shape
    pieces = [features[:, ranges(dz, planes, 0), ranges(dy, rows, 0)] for dz, dy in NEIGHBOURS]
    got = dict(zip(NEIGHBOURS, halo_swap(pieces, 1)))
    lines = []
    for dz in (1, 0, -1):
        middle = features if dz == 0 else got[(dz, 0)]
        lines.append(jnp.concatenate([got[(dz, 1)], middle, got[(dz, -1)]], axis=2))
    return jnp.concatenate(lines, axis=1)


def border_pieces(spread):
    _, planes, rows, _ = spread.shape
    planes, rows = planes - 2, rows - 2
    pieces = []
    for dz, dy in NEIGHBOURS:
        zs = slice(planes + 1, planes + 2) if dz == 1 else slice(0, 1) if dz == -1 else slice(1, planes + 1)
        ys = slice(rows + 1, rows + 2) if dy == 1 else slice(0, 1) if dy == -1 else slice(1, rows + 1)
        pieces.append(spread[:, zs, ys].astype(jnp.bfloat16))
    return pieces


def folded_grad(spread, got):
    _, planes, rows, _ = spread.shape
    planes, rows = planes - 2, rows - 2
    own = spread[:, 1 : planes + 1, 1 : rows + 1]
    for (dz, dy), piece in zip(NEIGHBOURS, got):
        own = own.at[:, ranges(-dz, planes, 0), ranges(-dy, rows, 0)].add(piece.astype(own.dtype))
    return own


def mesh_bits():
    sizes = {"gz": lax.axis_size("gz"), "gy": lax.axis_size("gy")}
    return [(axis, b) for axis, b in BIT_ORDER if (1 << b) < sizes[axis]]


def allreduce_kernel(bits, halvings, offsets, x_ref, *refs):
    count = len(offsets)
    pieces, o_ref = refs[:count], refs[count]
    landed = refs[count + 1 : 2 * count + 1]
    scratch = refs[2 * count + 1 :]
    halve_bufs = scratch[:halvings]
    work, double_buf, send_sems, recv_sems, halo_send, halo_recv = scratch[halvings:]
    here = {"gz": lax.axis_index("gz"), "gy": lax.axis_index("gy")}
    sizes = {"gz": lax.axis_size("gz"), "gy": lax.axis_size("gy")}

    def neighbour(dz, dy):
        return ((here["gz"] + dz + sizes["gz"]) % sizes["gz"], (here["gy"] + dy + sizes["gy"]) % sizes["gy"])

    def bit_of(axis, b):
        return (here[axis] // (1 << b)) % 2

    def partner(axis, b):
        flip = here[axis] + (1 - 2 * bit_of(axis, b)) * (1 << b)
        return (flip, here["gy"]) if axis == "gz" else (here["gz"], flip)

    barrier = pltpu.get_barrier_semaphore()
    for axis, b in bits:
        pl.semaphore_signal(barrier, inc=1, device_id=partner(axis, b), device_id_type=MESH_ID)
    for dz, dy in offsets:
        pl.semaphore_signal(barrier, inc=1, device_id=neighbour(dz, dy), device_id_type=MESH_ID)
    pl.semaphore_wait(barrier, len(bits) + count)
    halo = []
    for i, (dz, dy) in enumerate(offsets):
        copy = pltpu.make_async_remote_copy(
            src_ref=pieces[i],
            dst_ref=landed[i],
            send_sem=halo_send.at[i],
            recv_sem=halo_recv.at[i],
            device_id=neighbour(dz, dy),
            device_id_type=MESH_ID,
        )
        copy.start()
        halo.append(copy)

    def exchange(step, axis, b, src, dst):
        copy = pltpu.make_async_remote_copy(
            src_ref=src,
            dst_ref=dst,
            send_sem=send_sems.at[step],
            recv_sem=recv_sems.at[step],
            device_id=partner(axis, b),
            device_id_type=MESH_ID,
        )
        copy.start()
        copy.wait()

    lo, length, step = 0, o_ref.shape[0], 0
    for k in range(halvings):
        axis, b = bits[k]
        half = length // 2
        bit = bit_of(axis, b)
        keep = pl.multiple_of(lo + bit * half, 8)
        give = pl.multiple_of(lo + (1 - bit) * half, 8)
        source = x_ref if k == 0 else work
        exchange(step, axis, b, source.at[pl.ds(give, half)], halve_bufs[k])
        work[pl.ds(keep, half)] = source[pl.ds(keep, half)] + halve_bufs[k][...]
        lo, length, step = keep, half, step + 1
    for j, (axis, b) in enumerate(bits[halvings:]):
        exchange(step, axis, b, work.at[pl.ds(lo, length)], double_buf.at[j])
        work[pl.ds(lo, length)] = work[pl.ds(lo, length)] + double_buf[j]
        step += 1
    o_ref[pl.ds(lo, length)] = work[pl.ds(lo, length)]
    for k in reversed(range(halvings)):
        axis, b = bits[k]
        region = o_ref.at[pl.ds(lo, length)]
        exchange(step, axis, b, region, region)
        lo = pl.multiple_of(lo - bit_of(axis, b) * length, 8)
        length, step = length * 2, step + 1
    for copy in halo:
        copy.wait()


def allreduce(flat, pieces=(), halvings=HALVINGS):
    offsets = NEIGHBOURS[: len(pieces)]
    pieces = [p.reshape(-1, 128) for p in pieces]
    bits = mesh_bits()
    halvings = min(halvings, len(bits))
    rows = flat.shape[0]
    segment = rows >> halvings
    steps = len(bits) + halvings
    scratch = [pltpu.VMEM((rows >> (k + 1), 128), jnp.float32) for k in range(halvings)]
    scratch += [
        pltpu.VMEM(flat.shape, jnp.float32),
        pltpu.VMEM((max(len(bits) - halvings, 1), segment, 128), jnp.float32),
        pltpu.SemaphoreType.DMA((steps,)),
        pltpu.SemaphoreType.DMA((steps,)),
        pltpu.SemaphoreType.DMA((max(len(pieces), 1),)),
        pltpu.SemaphoreType.DMA((max(len(pieces), 1),)),
    ]
    vmem = pl.BlockSpec(memory_space=pltpu.VMEM)
    outs = pl.pallas_call(
        functools.partial(allreduce_kernel, bits, halvings, offsets),
        out_shape=[jax.ShapeDtypeStruct(flat.shape, jnp.float32)]
        + [jax.ShapeDtypeStruct(p.shape, p.dtype) for p in pieces],
        in_specs=[vmem] * (1 + len(pieces)),
        out_specs=[vmem] * (1 + len(pieces)),
        scratch_shapes=scratch,
        compiler_params=pltpu.CompilerParams(collective_id=0, has_side_effects=True),
    )(flat, *pieces)
    return outs[0], outs[1:]


def summed_gradients(local_conv, local_down, pieces):
    sizes = (local_conv.size, local_down.size)
    flat = jnp.concatenate([local_conv.reshape(-1), local_down.reshape(-1)])
    unit = 128 * 8 << HALVINGS
    padded = -(-flat.size // unit) * unit
    flat = jnp.pad(flat, (0, padded - flat.size)).reshape(-1, 128)
    total, got = allreduce(flat, [p.reshape(-1, 128) for p in pieces])
    total = total.reshape(-1)
    return (
        total[: sizes[0]].reshape(local_conv.shape),
        total[sizes[0] : sizes[0] + sizes[1]].reshape(local_down.shape),
        [g.reshape(p.shape) for g, p in zip(got, pieces)],
    )


def body(features, conv_weight, down_weight, cotangent):
    channels, plane_count, row_count, breadth = features.shape
    out_channels = down_weight.shape[2]
    cell_count = plane_count * row_count * breadth * lax.axis_size("gz") * lax.axis_size("gy")
    grad_scale = 1.0 / math.sqrt(cell_count)
    framed = framed_features(features)
    columns = widen(framed)
    preact = jnp.zeros((channels, plane_count, row_count, breadth), jnp.float32)
    for tap_z in range(3):
        for tap_y in range(3):
            window = columns[:, tap_z : tap_z + plane_count, tap_y : tap_y + row_count]
            preact = preact + jnp.einsum(
                "oj,jzyx->ozyx",
                conv_weight[tap_z, tap_y],
                window,
                preferred_element_type=jnp.float32,
            )
    hidden = jax.nn.silu(preact).astype(jnp.bfloat16)
    blocks = hidden.reshape(channels, plane_count // 2, 2, row_count // 2, 2, breadth // 2, 2)
    down_split = down_weight.reshape(2, 2, out_channels, 2, channels)
    coarse = jnp.einsum(
        "aboei,iZaYbXe->oZYX", down_split, blocks, preferred_element_type=jnp.float32
    )
    section_out = coarse.reshape(out_channels, plane_count // 2, -1).astype(jnp.bfloat16)
    coarse_cot = cotangent.reshape(out_channels, plane_count // 2, row_count // 2, breadth // 2)
    hidden_grad = jnp.einsum(
        "aboei,oZYX->iZaYbXe", down_split, coarse_cot, preferred_element_type=jnp.float32
    )
    hidden_grad = hidden_grad.reshape(channels, plane_count, row_count, breadth)
    local_down = jnp.einsum(
        "oZYX,iZaYbXe->aboei", coarse_cot, blocks, preferred_element_type=jnp.float32
    )
    local_down = local_down.reshape(2, 2, out_channels, 2 * channels)
    gate_sig = jax.nn.sigmoid(preact)
    gate_grad = (hidden_grad * gate_sig * (1.0 + preact * (1.0 - gate_sig))).astype(jnp.bfloat16)
    kernel_rows = []
    for tap_z in range(3):
        row_list = []
        for tap_y in range(3):
            window = columns[:, tap_z : tap_z + plane_count, tap_y : tap_y + row_count]
            row_list.append(
                jnp.einsum("ozyx,jzyx->oj", gate_grad, window, preferred_element_type=jnp.float32)
            )
        kernel_rows.append(jnp.stack(row_list, axis=0))
    local_conv = jnp.stack(kernel_rows, axis=0)
    spread = jnp.zeros((3 * channels, plane_count + 2, row_count + 2, breadth), jnp.float32)
    for tap_z in range(3):
        for tap_y in range(3):
            term = jnp.einsum(
                "oj,ozyx->jzyx",
                conv_weight[tap_z, tap_y],
                gate_grad,
                preferred_element_type=jnp.float32,
            )
            spread = spread.at[:, tap_z : tap_z + plane_count, tap_y : tap_y + row_count].add(term)
    folded = fold_along(spread, channels)
    summed_conv, summed_down, got = summed_gradients(local_conv, local_down, border_pieces(folded))
    row_fold = folded_grad(folded, got)
    grad_conv = summed_conv * grad_scale
    grad_down = summed_down * grad_scale
    return (section_out, row_fold, grad_conv, grad_down)


def solution(mesh):
    return jax.shard_map(
        body,
        mesh=mesh,
        in_specs=(P(None, "gz", "gy", None), P(), P(), P(None, "gz", "gy")),
        out_specs=(P(None, "gz", "gy"), P(None, "gz", "gy", None), P(), P()),
        check_vma=False,
    )
```

```python
import functools
import math

import jax
import jax.numpy as jnp
from jax import lax
from jax.experimental import pallas as pl
from jax.experimental.pallas import tpu as pltpu
from jax.sharding import PartitionSpec as P

MESH_ID = pl.DeviceIdType.MESH
BIT_ORDER = (
    (("gy", 0), ("gy", 0)),
    (("gy", 1), ("gz", 0)),
    (("gz", 0), ("gz", 3)),
    (("gz", 3), ("gy", 1)),
    (("gy", 2), ("gz", 1)),
    (("gz", 1), ("gy", 2)),
    (("gz", 4), ("gz", 2)),
    (("gz", 2), ("gz", 4)),
    (("gy", 3), ("gy", 3)),
)
HALVINGS = 4


def extended(cells, sides, width):
    for axis, dim in sides:
        count = lax.axis_size(axis)
        head = lax.slice_in_dim(cells, 0, width, axis=dim)
        tail = lax.slice_in_dim(cells, cells.shape[dim] - width, cells.shape[dim], axis=dim)
        cells = jnp.concatenate(
            [
                lax.ppermute(tail, axis, [(i, (i + 1) % count) for i in range(count)]),
                cells,
                lax.ppermute(head, axis, [((i + 1) % count, i) for i in range(count)]),
            ],
            axis=dim,
        )
    return cells


def widen(framed):
    return jnp.concatenate([jnp.roll(framed, 1 - tap_x, axis=3) for tap_x in range(3)], axis=0)


def fold_along(spread, channels):
    result = jnp.roll(spread[0:channels], -1, axis=3)
    result = result + spread[channels : 2 * channels]
    result = result + jnp.roll(spread[2 * channels : 3 * channels], 1, axis=3)
    return result


NEIGHBOURS = ((1, 0), (-1, 0), (0, 1), (0, -1), (1, 1), (1, -1), (-1, 1), (-1, -1))


def halo_kernel(offsets, *refs):
    count = len(offsets)
    sources, targets = refs[:count], refs[count : 2 * count]
    send_sems, recv_sems = refs[2 * count :]
    sizes = (lax.axis_size("gz"), lax.axis_size("gy"))
    here = (lax.axis_index("gz"), lax.axis_index("gy"))

    def device(dz, dy):
        return ((here[0] + dz + sizes[0]) % sizes[0], (here[1] + dy + sizes[1]) % sizes[1])

    barrier = pltpu.get_barrier_semaphore()
    for dz, dy in offsets:
        pl.semaphore_signal(barrier, inc=1, device_id=device(dz, dy), device_id_type=MESH_ID)
    pl.semaphore_wait(barrier, count)
    copies = []
    for i, (dz, dy) in enumerate(offsets):
        copy = pltpu.make_async_remote_copy(
            src_ref=sources[i],
            dst_ref=targets[i],
            send_sem=send_sems.at[i],
            recv_sem=recv_sems.at[i],
            device_id=device(dz, dy),
            device_id_type=MESH_ID,
        )
        copy.start()
        copies.append(copy)
    for copy in copies:
        copy.wait()


def halo_swap(pieces, collective_id):
    flat = [p.reshape(-1, 128) for p in pieces]
    vmem = pl.BlockSpec(memory_space=pltpu.VMEM)
    got = pl.pallas_call(
        functools.partial(halo_kernel, NEIGHBOURS),
        out_shape=[jax.ShapeDtypeStruct(f.shape, f.dtype) for f in flat],
        in_specs=[vmem] * len(flat),
        out_specs=[vmem] * len(flat),
        scratch_shapes=[pltpu.SemaphoreType.DMA((len(flat),)), pltpu.SemaphoreType.DMA((len(flat),))],
        compiler_params=pltpu.CompilerParams(collective_id=collective_id, has_side_effects=True),
    )(*flat)
    return [g.reshape(p.shape) for g, p in zip(got, pieces)]


def ranges(shift, count, border):
    if shift == 1:
        return slice(border + count - 1, border + count)
    if shift == -1:
        return slice(border, border + 1)
    return slice(border, border + count)


def framed_features(features):
    _, planes, rows, _ = features.shape
    pieces = [features[:, ranges(dz, planes, 0), ranges(dy, rows, 0)] for dz, dy in NEIGHBOURS]
    got = dict(zip(NEIGHBOURS, halo_swap(pieces, 1)))
    lines = []
    for dz in (1, 0, -1):
        middle = features if dz == 0 else got[(dz, 0)]
        lines.append(jnp.concatenate([got[(dz, 1)], middle, got[(dz, -1)]], axis=2))
    return jnp.concatenate(lines, axis=1)


def border_pieces(spread):
    _, planes, rows, _ = spread.shape
    planes, rows = planes - 2, rows - 2
    pieces = []
    for dz, dy in NEIGHBOURS:
        zs = slice(planes + 1, planes + 2) if dz == 1 else slice(0, 1) if dz == -1 else slice(1, planes + 1)
        ys = slice(rows + 1, rows + 2) if dy == 1 else slice(0, 1) if dy == -1 else slice(1, rows + 1)
        pieces.append(spread[:, zs, ys].astype(jnp.bfloat16))
    return pieces


def folded_grad(spread, got):
    _, planes, rows, _ = spread.shape
    planes, rows = planes - 2, rows - 2
    own = spread[:, 1 : planes + 1, 1 : rows + 1]
    for (dz, dy), piece in zip(NEIGHBOURS, got):
        own = own.at[:, ranges(-dz, planes, 0), ranges(-dy, rows, 0)].add(piece.astype(own.dtype))
    return own


def mesh_bits():
    sizes = {"gz": lax.axis_size("gz"), "gy": lax.axis_size("gy")}
    orders = [[pair[c] for pair in BIT_ORDER if (1 << pair[c][1]) < sizes[pair[c][0]]] for c in (0, 1)]
    return list(zip(*orders))


def allreduce_kernel(bits, halvings, offsets, x_ref, *refs):
    count = len(offsets)
    pieces, o_ref = refs[:count], refs[count]
    landed = refs[count + 1 : 2 * count + 1]
    scratch = refs[2 * count + 1 :]
    halve_bufs = scratch[:halvings]
    work, double_buf, send_sems, recv_sems, halo_send, halo_recv = scratch[halvings:]
    here = {"gz": lax.axis_index("gz"), "gy": lax.axis_index("gy")}
    sizes = {"gz": lax.axis_size("gz"), "gy": lax.axis_size("gy")}

    def neighbour(dz, dy):
        return ((here["gz"] + dz + sizes["gz"]) % sizes["gz"], (here["gy"] + dy + sizes["gy"]) % sizes["gy"])

    core = here["gy"] % 2

    def pick(pair):
        (axis0, b0), (axis1, b1) = pair
        a0, a1 = int(axis0 == "gy"), int(axis1 == "gy")
        return a0 + (a1 - a0) * core, (1 << b0) + ((1 << b1) - (1 << b0)) * core

    def bit_of(pair):
        which, weight = pick(pair)
        value = here["gz"] + (here["gy"] - here["gz"]) * which
        return (value // weight) % 2

    def partner(pair):
        which, weight = pick(pair)
        step = (1 - 2 * bit_of(pair)) * weight
        return (here["gz"] + step * (1 - which), here["gy"] + step * which)

    barrier = pltpu.get_barrier_semaphore()
    for pair in bits:
        pl.semaphore_signal(barrier, inc=1, device_id=partner(pair), device_id_type=MESH_ID)
    for dz, dy in offsets:
        pl.semaphore_signal(barrier, inc=1, device_id=neighbour(dz, dy), device_id_type=MESH_ID)
    pl.semaphore_wait(barrier, len(bits) + count)
    halo = []
    for i, (dz, dy) in enumerate(offsets):
        copy = pltpu.make_async_remote_copy(
            src_ref=pieces[i],
            dst_ref=landed[i],
            send_sem=halo_send.at[i],
            recv_sem=halo_recv.at[i],
            device_id=neighbour(dz, dy),
            device_id_type=MESH_ID,
        )
        copy.start()
        halo.append(copy)

    def exchange(step, pair, src, dst):
        copy = pltpu.make_async_remote_copy(
            src_ref=src,
            dst_ref=dst,
            send_sem=send_sems.at[step],
            recv_sem=recv_sems.at[step],
            device_id=partner(pair),
            device_id_type=MESH_ID,
        )
        copy.start()
        copy.wait()

    lo, length, step = 0, o_ref.shape[0], 0
    for k in range(halvings):
        pair = bits[k]
        half = length // 2
        bit = bit_of(pair)
        keep = pl.multiple_of(lo + bit * half, 8)
        give = pl.multiple_of(lo + (1 - bit) * half, 8)
        source = x_ref if k == 0 else work
        exchange(step, pair, source.at[pl.ds(give, half)], halve_bufs[k])
        work[pl.ds(keep, half)] = source[pl.ds(keep, half)] + halve_bufs[k][...]
        lo, length, step = keep, half, step + 1
    for j, pair in enumerate(bits[halvings:]):
        exchange(step, pair, work.at[pl.ds(lo, length)], double_buf.at[j])
        work[pl.ds(lo, length)] = work[pl.ds(lo, length)] + double_buf[j]
        step += 1
    o_ref[pl.ds(lo, length)] = work[pl.ds(lo, length)]
    for k in reversed(range(halvings)):
        pair = bits[k]
        region = o_ref.at[pl.ds(lo, length)]
        exchange(step, pair, region, region)
        lo = pl.multiple_of(lo - bit_of(pair) * length, 8)
        length, step = length * 2, step + 1
    for copy in halo:
        copy.wait()


def allreduce(flat, pieces=(), halvings=HALVINGS):
    offsets = NEIGHBOURS[: len(pieces)]
    pieces = [p.reshape(-1, 128) for p in pieces]
    bits = mesh_bits()
    halvings = min(halvings, len(bits))
    rows = flat.shape[0]
    segment = rows >> halvings
    steps = len(bits) + halvings
    scratch = [pltpu.VMEM((rows >> (k + 1), 128), jnp.float32) for k in range(halvings)]
    scratch += [
        pltpu.VMEM(flat.shape, jnp.float32),
        pltpu.VMEM((max(len(bits) - halvings, 1), segment, 128), jnp.float32),
        pltpu.SemaphoreType.DMA((steps,)),
        pltpu.SemaphoreType.DMA((steps,)),
        pltpu.SemaphoreType.DMA((max(len(pieces), 1),)),
        pltpu.SemaphoreType.DMA((max(len(pieces), 1),)),
    ]
    vmem = pl.BlockSpec(memory_space=pltpu.VMEM)
    outs = pl.pallas_call(
        functools.partial(allreduce_kernel, bits, halvings, offsets),
        out_shape=[jax.ShapeDtypeStruct(flat.shape, jnp.float32)]
        + [jax.ShapeDtypeStruct(p.shape, p.dtype) for p in pieces],
        in_specs=[vmem] * (1 + len(pieces)),
        out_specs=[vmem] * (1 + len(pieces)),
        scratch_shapes=scratch,
        compiler_params=pltpu.CompilerParams(collective_id=0, has_side_effects=True),
    )(flat, *pieces)
    return outs[0], outs[1:]


def summed_gradients(local_conv, local_down, pieces):
    sizes = (local_conv.size, local_down.size)
    flat = jnp.concatenate([local_conv.reshape(-1), local_down.reshape(-1)])
    unit = 128 * 8 << HALVINGS
    padded = -(-flat.size // unit) * unit
    flat = jnp.pad(flat, (0, padded - flat.size)).reshape(-1, 128)
    total, got = allreduce(flat, [p.reshape(-1, 128) for p in pieces])
    total = total.reshape(-1)
    return (
        total[: sizes[0]].reshape(local_conv.shape),
        total[sizes[0] : sizes[0] + sizes[1]].reshape(local_down.shape),
        [g.reshape(p.shape) for g, p in zip(got, pieces)],
    )


def body(features, conv_weight, down_weight, cotangent):
    channels, plane_count, row_count, breadth = features.shape
    out_channels = down_weight.shape[2]
    cell_count = plane_count * row_count * breadth * lax.axis_size("gz") * lax.axis_size("gy")
    grad_scale = 1.0 / math.sqrt(cell_count)
    framed = framed_features(features)
    columns = widen(framed)
    preact = jnp.zeros((channels, plane_count, row_count, breadth), jnp.float32)
    for tap_z in range(3):
        for tap_y in range(3):
            window = columns[:, tap_z : tap_z + plane_count, tap_y : tap_y + row_count]
            preact = preact + jnp.einsum(
                "oj,jzyx->ozyx",
                conv_weight[tap_z, tap_y],
                window,
                preferred_element_type=jnp.float32,
            )
    hidden = jax.nn.silu(preact).astype(jnp.bfloat16)
    blocks = hidden.reshape(channels, plane_count // 2, 2, row_count // 2, 2, breadth // 2, 2)
    down_split = down_weight.reshape(2, 2, out_channels, 2, channels)
    coarse = jnp.einsum(
        "aboei,iZaYbXe->oZYX", down_split, blocks, preferred_element_type=jnp.float32
    )
    section_out = coarse.reshape(out_channels, plane_count // 2, -1).astype(jnp.bfloat16)
    coarse_cot = cotangent.reshape(out_channels, plane_count // 2, row_count // 2, breadth // 2)
    hidden_grad = jnp.einsum(
        "aboei,oZYX->iZaYbXe", down_split, coarse_cot, preferred_element_type=jnp.float32
    )
    hidden_grad = hidden_grad.reshape(channels, plane_count, row_count, breadth)
    local_down = jnp.einsum(
        "oZYX,iZaYbXe->aboei", coarse_cot, blocks, preferred_element_type=jnp.float32
    )
    local_down = local_down.reshape(2, 2, out_channels, 2 * channels)
    gate_sig = jax.nn.sigmoid(preact)
    gate_grad = (hidden_grad * gate_sig * (1.0 + preact * (1.0 - gate_sig))).astype(jnp.bfloat16)
    kernel_rows = []
    for tap_z in range(3):
        row_list = []
        for tap_y in range(3):
            window = columns[:, tap_z : tap_z + plane_count, tap_y : tap_y + row_count]
            row_list.append(
                jnp.einsum("ozyx,jzyx->oj", gate_grad, window, preferred_element_type=jnp.float32)
            )
        kernel_rows.append(jnp.stack(row_list, axis=0))
    local_conv = jnp.stack(kernel_rows, axis=0)
    spread = jnp.zeros((3 * channels, plane_count + 2, row_count + 2, breadth), jnp.float32)
    for tap_z in range(3):
        for tap_y in range(3):
            term = jnp.einsum(
                "oj,ozyx->jzyx",
                conv_weight[tap_z, tap_y],
                gate_grad,
                preferred_element_type=jnp.float32,
            )
            spread = spread.at[:, tap_z : tap_z + plane_count, tap_y : tap_y + row_count].add(term)
    folded = fold_along(spread, channels)
    summed_conv, summed_down, got = summed_gradients(local_conv, local_down, border_pieces(folded))
    row_fold = folded_grad(folded, got)
    grad_conv = summed_conv * grad_scale
    grad_down = summed_down * grad_scale
    return (section_out, row_fold, grad_conv, grad_down)


def solution(mesh):
    return jax.shard_map(
        body,
        mesh=mesh,
        in_specs=(P(None, "gz", "gy", None), P(), P(), P(None, "gz", "gy")),
        out_specs=(P(None, "gz", "gy"), P(None, "gz", "gy", None), P(), P()),
        check_vma=False,
    )
```

```python
import functools
import math

import jax
import jax.numpy as jnp
from jax import lax
from jax.experimental import pallas as pl
from jax.experimental.pallas import tpu as pltpu
from jax.sharding import PartitionSpec as P

MESH_ID = pl.DeviceIdType.MESH
BIT_ORDER = (
    (("gy", 0), ("gy", 0)),
    (("gy", 1), ("gz", 0)),
    (("gz", 0), ("gz", 3)),
    (("gz", 3), ("gy", 1)),
    (("gy", 2), ("gz", 1)),
    (("gz", 1), ("gy", 2)),
    (("gz", 4), ("gz", 2)),
    (("gz", 2), ("gz", 4)),
    (("gy", 3), ("gy", 3)),
)
HALVINGS = 4


def extended(cells, sides, width):
    for axis, dim in sides:
        count = lax.axis_size(axis)
        head = lax.slice_in_dim(cells, 0, width, axis=dim)
        tail = lax.slice_in_dim(cells, cells.shape[dim] - width, cells.shape[dim], axis=dim)
        cells = jnp.concatenate(
            [
                lax.ppermute(tail, axis, [(i, (i + 1) % count) for i in range(count)]),
                cells,
                lax.ppermute(head, axis, [((i + 1) % count, i) for i in range(count)]),
            ],
            axis=dim,
        )
    return cells


def widen(framed):
    return jnp.concatenate([jnp.roll(framed, 1 - tap_x, axis=3) for tap_x in range(3)], axis=0)


def fold_along(spread, channels):
    result = jnp.roll(spread[0:channels], -1, axis=3)
    result = result + spread[channels : 2 * channels]
    result = result + jnp.roll(spread[2 * channels : 3 * channels], 1, axis=3)
    return result


NEIGHBOURS = ((1, 0), (-1, 0), (0, 1), (0, -1), (1, 1), (1, -1), (-1, 1), (-1, -1))


def halo_kernel(offsets, *refs):
    count = len(offsets)
    sources, targets = refs[:count], refs[count : 2 * count]
    send_sems, recv_sems = refs[2 * count :]
    sizes = (lax.axis_size("gz"), lax.axis_size("gy"))
    here = (lax.axis_index("gz"), lax.axis_index("gy"))

    def device(dz, dy):
        return ((here[0] + dz + sizes[0]) % sizes[0], (here[1] + dy + sizes[1]) % sizes[1])

    barrier = pltpu.get_barrier_semaphore()
    for dz, dy in offsets:
        pl.semaphore_signal(barrier, inc=1, device_id=device(dz, dy), device_id_type=MESH_ID)
    pl.semaphore_wait(barrier, count)
    copies = []
    for i, (dz, dy) in enumerate(offsets):
        copy = pltpu.make_async_remote_copy(
            src_ref=sources[i],
            dst_ref=targets[i],
            send_sem=send_sems.at[i],
            recv_sem=recv_sems.at[i],
            device_id=device(dz, dy),
            device_id_type=MESH_ID,
        )
        copy.start()
        copies.append(copy)
    for copy in copies:
        copy.wait()


def halo_swap(pieces, collective_id):
    flat = [p.reshape(-1, 128) for p in pieces]
    vmem = pl.BlockSpec(memory_space=pltpu.VMEM)
    got = pl.pallas_call(
        functools.partial(halo_kernel, NEIGHBOURS),
        out_shape=[jax.ShapeDtypeStruct(f.shape, f.dtype) for f in flat],
        in_specs=[vmem] * len(flat),
        out_specs=[vmem] * len(flat),
        scratch_shapes=[pltpu.SemaphoreType.DMA((len(flat),)), pltpu.SemaphoreType.DMA((len(flat),))],
        compiler_params=pltpu.CompilerParams(collective_id=collective_id, has_side_effects=True),
    )(*flat)
    return [g.reshape(p.shape) for g, p in zip(got, pieces)]


def ranges(shift, count, border):
    if shift == 1:
        return slice(border + count - 1, border + count)
    if shift == -1:
        return slice(border, border + 1)
    return slice(border, border + count)


def framed_features(features):
    _, planes, rows, _ = features.shape
    pieces = [features[:, ranges(dz, planes, 0), ranges(dy, rows, 0)] for dz, dy in NEIGHBOURS]
    got = dict(zip(NEIGHBOURS, halo_swap(pieces, 1)))
    lines = []
    for dz in (1, 0, -1):
        middle = features if dz == 0 else got[(dz, 0)]
        lines.append(jnp.concatenate([got[(dz, 1)], middle, got[(dz, -1)]], axis=2))
    return jnp.concatenate(lines, axis=1)


def border_pieces(spread):
    _, planes, rows, _ = spread.shape
    planes, rows = planes - 2, rows - 2
    pieces = []
    for dz, dy in NEIGHBOURS:
        zs = slice(planes + 1, planes + 2) if dz == 1 else slice(0, 1) if dz == -1 else slice(1, planes + 1)
        ys = slice(rows + 1, rows + 2) if dy == 1 else slice(0, 1) if dy == -1 else slice(1, rows + 1)
        pieces.append(spread[:, zs, ys].astype(jnp.bfloat16))
    return pieces


def folded_grad(spread, got):
    _, planes, rows, _ = spread.shape
    planes, rows = planes - 2, rows - 2
    own = spread[:, 1 : planes + 1, 1 : rows + 1]
    for (dz, dy), piece in zip(NEIGHBOURS, got):
        own = own.at[:, ranges(-dz, planes, 0), ranges(-dy, rows, 0)].add(piece.astype(own.dtype))
    return own


def mesh_bits():
    sizes = {"gz": lax.axis_size("gz"), "gy": lax.axis_size("gy")}
    orders = [[pair[c] for pair in BIT_ORDER if (1 << pair[c][1]) < sizes[pair[c][0]]] for c in (0, 1)]
    return list(zip(*orders))


def allreduce_kernel(bits, halvings, offsets, x_ref, *refs):
    count = len(offsets)
    pieces, o_ref = refs[:count], refs[count]
    landed = refs[count + 1 : 2 * count + 1]
    scratch = refs[2 * count + 1 :]
    halve_bufs = scratch[:halvings]
    work, double_buf, send_sems, recv_sems, halo_send, halo_recv = scratch[halvings:]
    here = {"gz": lax.axis_index("gz"), "gy": lax.axis_index("gy")}
    sizes = {"gz": lax.axis_size("gz"), "gy": lax.axis_size("gy")}

    def neighbour(dz, dy):
        return ((here["gz"] + dz + sizes["gz"]) % sizes["gz"], (here["gy"] + dy + sizes["gy"]) % sizes["gy"])

    core = here["gy"] % 2

    def pick(pair):
        (axis0, b0), (axis1, b1) = pair
        a0, a1 = int(axis0 == "gy"), int(axis1 == "gy")
        return a0 + (a1 - a0) * core, (1 << b0) + ((1 << b1) - (1 << b0)) * core

    def bit_of(pair):
        which, weight = pick(pair)
        value = here["gz"] + (here["gy"] - here["gz"]) * which
        return (value // weight) % 2

    def partner(*pairs):
        device = [here["gz"], here["gy"]]
        for pair in pairs:
            which, weight = pick(pair)
            step = (1 - 2 * bit_of(pair)) * weight
            device = [device[0] + step * (1 - which), device[1] + step * which]
        return tuple(device)

    groups = [bits[i : i + 2] for i in range(halvings, len(bits), 2)]
    reach = [(pair,) for pair in bits] + [tuple(g) for g in groups if len(g) == 2]

    barrier = pltpu.get_barrier_semaphore()
    for pairs in reach:
        pl.semaphore_signal(barrier, inc=1, device_id=partner(*pairs), device_id_type=MESH_ID)
    for dz, dy in offsets:
        pl.semaphore_signal(barrier, inc=1, device_id=neighbour(dz, dy), device_id_type=MESH_ID)
    pl.semaphore_wait(barrier, len(reach) + count)
    halo = []
    for i, (dz, dy) in enumerate(offsets):
        copy = pltpu.make_async_remote_copy(
            src_ref=pieces[i],
            dst_ref=landed[i],
            send_sem=halo_send.at[i],
            recv_sem=halo_recv.at[i],
            device_id=neighbour(dz, dy),
            device_id_type=MESH_ID,
        )
        copy.start()
        halo.append(copy)

    def exchange(step, pair, src, dst):
        start_copy(step, (pair,), src, dst).wait()

    def start_copy(step, pairs, src, dst):
        copy = pltpu.make_async_remote_copy(
            src_ref=src,
            dst_ref=dst,
            send_sem=send_sems.at[step],
            recv_sem=recv_sems.at[step],
            device_id=partner(*pairs),
            device_id_type=MESH_ID,
        )
        copy.start()
        return copy

    lo, length, step = 0, o_ref.shape[0], 0
    for k in range(halvings):
        pair = bits[k]
        half = length // 2
        bit = bit_of(pair)
        keep = pl.multiple_of(lo + bit * half, 8)
        give = pl.multiple_of(lo + (1 - bit) * half, 8)
        source = x_ref if k == 0 else work
        exchange(step, pair, source.at[pl.ds(give, half)], halve_bufs[k])
        work[pl.ds(keep, half)] = source[pl.ds(keep, half)] + halve_bufs[k][...]
        lo, length, step = keep, half, step + 1
    slot = 0
    for group in groups:
        own = work.at[pl.ds(lo, length)]
        if len(group) == 1:
            exchange(step, group[0], own, double_buf.at[slot])
            work[pl.ds(lo, length)] = own[...] + double_buf[slot]
            slot, step = slot + 1, step + 1
            continue
        flips = [(group[0],), (group[1],), (group[0], group[1])]
        copies = [start_copy(step + m, f, own, double_buf.at[slot + m]) for m, f in enumerate(flips)]
        for copy in copies:
            copy.wait()
        near, far = double_buf[slot] + own[...], double_buf[slot + 1] + double_buf[slot + 2]
        work[pl.ds(lo, length)] = near + far
        slot, step = slot + 3, step + 3
    o_ref[pl.ds(lo, length)] = work[pl.ds(lo, length)]
    for k in reversed(range(halvings)):
        pair = bits[k]
        region = o_ref.at[pl.ds(lo, length)]
        exchange(step, pair, region, region)
        lo = pl.multiple_of(lo - bit_of(pair) * length, 8)
        length, step = length * 2, step + 1
    for copy in halo:
        copy.wait()


def allreduce(flat, pieces=(), halvings=HALVINGS):
    offsets = NEIGHBOURS[: len(pieces)]
    pieces = [p.reshape(-1, 128) for p in pieces]
    bits = mesh_bits()
    halvings = min(halvings, len(bits))
    rows = flat.shape[0]
    segment = rows >> halvings
    far = len(bits) - halvings
    slots = 3 * (far // 2) + far % 2
    steps = 2 * halvings + slots
    scratch = [pltpu.VMEM((rows >> (k + 1), 128), jnp.float32) for k in range(halvings)]
    scratch += [
        pltpu.VMEM(flat.shape, jnp.float32),
        pltpu.VMEM((max(slots, 1), segment, 128), jnp.float32),
        pltpu.SemaphoreType.DMA((steps,)),
        pltpu.SemaphoreType.DMA((steps,)),
        pltpu.SemaphoreType.DMA((max(len(pieces), 1),)),
        pltpu.SemaphoreType.DMA((max(len(pieces), 1),)),
    ]
    vmem = pl.BlockSpec(memory_space=pltpu.VMEM)
    outs = pl.pallas_call(
        functools.partial(allreduce_kernel, bits, halvings, offsets),
        out_shape=[jax.ShapeDtypeStruct(flat.shape, jnp.float32)]
        + [jax.ShapeDtypeStruct(p.shape, p.dtype) for p in pieces],
        in_specs=[vmem] * (1 + len(pieces)),
        out_specs=[vmem] * (1 + len(pieces)),
        scratch_shapes=scratch,
        compiler_params=pltpu.CompilerParams(collective_id=0, has_side_effects=True),
    )(flat, *pieces)
    return outs[0], outs[1:]


def summed_gradients(local_conv, local_down, pieces):
    sizes = (local_conv.size, local_down.size)
    flat = jnp.concatenate([local_conv.reshape(-1), local_down.reshape(-1)])
    unit = 128 * 8 << HALVINGS
    padded = -(-flat.size // unit) * unit
    flat = jnp.pad(flat, (0, padded - flat.size)).reshape(-1, 128)
    total, got = allreduce(flat, [p.reshape(-1, 128) for p in pieces])
    total = total.reshape(-1)
    return (
        total[: sizes[0]].reshape(local_conv.shape),
        total[sizes[0] : sizes[0] + sizes[1]].reshape(local_down.shape),
        [g.reshape(p.shape) for g, p in zip(got, pieces)],
    )


def body(features, conv_weight, down_weight, cotangent):
    channels, plane_count, row_count, breadth = features.shape
    out_channels = down_weight.shape[2]
    cell_count = plane_count * row_count * breadth * lax.axis_size("gz") * lax.axis_size("gy")
    grad_scale = 1.0 / math.sqrt(cell_count)
    framed = framed_features(features)
    columns = widen(framed)
    preact = jnp.zeros((channels, plane_count, row_count, breadth), jnp.float32)
    for tap_z in range(3):
        for tap_y in range(3):
            window = columns[:, tap_z : tap_z + plane_count, tap_y : tap_y + row_count]
            preact = preact + jnp.einsum(
                "oj,jzyx->ozyx",
                conv_weight[tap_z, tap_y],
                window,
                preferred_element_type=jnp.float32,
            )
    hidden = jax.nn.silu(preact).astype(jnp.bfloat16)
    blocks = hidden.reshape(channels, plane_count // 2, 2, row_count // 2, 2, breadth // 2, 2)
    down_split = down_weight.reshape(2, 2, out_channels, 2, channels)
    coarse = jnp.einsum(
        "aboei,iZaYbXe->oZYX", down_split, blocks, preferred_element_type=jnp.float32
    )
    section_out = coarse.reshape(out_channels, plane_count // 2, -1).astype(jnp.bfloat16)
    coarse_cot = cotangent.reshape(out_channels, plane_count // 2, row_count // 2, breadth // 2)
    hidden_grad = jnp.einsum(
        "aboei,oZYX->iZaYbXe", down_split, coarse_cot, preferred_element_type=jnp.float32
    )
    hidden_grad = hidden_grad.reshape(channels, plane_count, row_count, breadth)
    local_down = jnp.einsum(
        "oZYX,iZaYbXe->aboei", coarse_cot, blocks, preferred_element_type=jnp.float32
    )
    local_down = local_down.reshape(2, 2, out_channels, 2 * channels)
    gate_sig = jax.nn.sigmoid(preact)
    gate_grad = (hidden_grad * gate_sig * (1.0 + preact * (1.0 - gate_sig))).astype(jnp.bfloat16)
    kernel_rows = []
    for tap_z in range(3):
        row_list = []
        for tap_y in range(3):
            window = columns[:, tap_z : tap_z + plane_count, tap_y : tap_y + row_count]
            row_list.append(
                jnp.einsum("ozyx,jzyx->oj", gate_grad, window, preferred_element_type=jnp.float32)
            )
        kernel_rows.append(jnp.stack(row_list, axis=0))
    local_conv = jnp.stack(kernel_rows, axis=0)
    spread = jnp.zeros((3 * channels, plane_count + 2, row_count + 2, breadth), jnp.float32)
    for tap_z in range(3):
        for tap_y in range(3):
            term = jnp.einsum(
                "oj,ozyx->jzyx",
                conv_weight[tap_z, tap_y],
                gate_grad,
                preferred_element_type=jnp.float32,
            )
            spread = spread.at[:, tap_z : tap_z + plane_count, tap_y : tap_y + row_count].add(term)
    folded = fold_along(spread, channels)
    summed_conv, summed_down, got = summed_gradients(local_conv, local_down, border_pieces(folded))
    row_fold = folded_grad(folded, got)
    grad_conv = summed_conv * grad_scale
    grad_down = summed_down * grad_scale
    return (section_out, row_fold, grad_conv, grad_down)


def solution(mesh):
    return jax.shard_map(
        body,
        mesh=mesh,
        in_specs=(P(None, "gz", "gy", None), P(), P(), P(None, "gz", "gy")),
        out_specs=(P(None, "gz", "gy"), P(None, "gz", "gy", None), P(), P()),
        check_vma=False,
    )
```

```python
import functools
import math

import jax
import jax.numpy as jnp
from jax import lax
from jax.experimental import pallas as pl
from jax.experimental.pallas import tpu as pltpu
from jax.sharding import PartitionSpec as P

MESH_ID = pl.DeviceIdType.MESH
BIT_ORDER = (
    (("gy", 0), ("gy", 0)),
    (("gy", 1), ("gz", 0)),
    (("gz", 0), ("gz", 3)),
    (("gz", 3), ("gy", 1)),
    (("gy", 2), ("gz", 1)),
    (("gz", 1), ("gy", 2)),
    (("gz", 4), ("gz", 2)),
    (("gz", 2), ("gz", 4)),
    (("gy", 3), ("gy", 3)),
)
HALVINGS = 4


def extended(cells, sides, width):
    for axis, dim in sides:
        count = lax.axis_size(axis)
        head = lax.slice_in_dim(cells, 0, width, axis=dim)
        tail = lax.slice_in_dim(cells, cells.shape[dim] - width, cells.shape[dim], axis=dim)
        cells = jnp.concatenate(
            [
                lax.ppermute(tail, axis, [(i, (i + 1) % count) for i in range(count)]),
                cells,
                lax.ppermute(head, axis, [((i + 1) % count, i) for i in range(count)]),
            ],
            axis=dim,
        )
    return cells


def widen(framed):
    return jnp.concatenate([jnp.roll(framed, 1 - tap_x, axis=3) for tap_x in range(3)], axis=0)


def fold_along(spread, channels):
    result = jnp.roll(spread[0:channels], -1, axis=3)
    result = result + spread[channels : 2 * channels]
    result = result + jnp.roll(spread[2 * channels : 3 * channels], 1, axis=3)
    return result


NEIGHBOURS = ((1, 0), (-1, 0), (0, 1), (0, -1), (1, 1), (1, -1), (-1, 1), (-1, -1))


def halo_kernel(offsets, *refs):
    count = len(offsets)
    sources, targets = refs[:count], refs[count : 2 * count]
    send_sems, recv_sems = refs[2 * count :]
    sizes = (lax.axis_size("gz"), lax.axis_size("gy"))
    here = (lax.axis_index("gz"), lax.axis_index("gy"))

    def device(dz, dy):
        return ((here[0] + dz + sizes[0]) % sizes[0], (here[1] + dy + sizes[1]) % sizes[1])

    barrier = pltpu.get_barrier_semaphore()
    for dz, dy in offsets:
        pl.semaphore_signal(barrier, inc=1, device_id=device(dz, dy), device_id_type=MESH_ID)
    pl.semaphore_wait(barrier, count)
    copies = []
    for i, (dz, dy) in enumerate(offsets):
        copy = pltpu.make_async_remote_copy(
            src_ref=sources[i],
            dst_ref=targets[i],
            send_sem=send_sems.at[i],
            recv_sem=recv_sems.at[i],
            device_id=device(dz, dy),
            device_id_type=MESH_ID,
        )
        copy.start()
        copies.append(copy)
    for copy in copies:
        copy.wait()


def halo_swap(pieces, collective_id):
    flat = [as_rows(p) for p in pieces]
    vmem = pl.BlockSpec(memory_space=pltpu.VMEM)
    got = pl.pallas_call(
        functools.partial(halo_kernel, NEIGHBOURS),
        out_shape=[jax.ShapeDtypeStruct(f.shape, f.dtype) for f in flat],
        in_specs=[vmem] * len(flat),
        out_specs=[vmem] * len(flat),
        scratch_shapes=[pltpu.SemaphoreType.DMA((len(flat),)), pltpu.SemaphoreType.DMA((len(flat),))],
        compiler_params=pltpu.CompilerParams(collective_id=collective_id, has_side_effects=True),
    )(*flat)
    return [from_rows(g, p.shape) for g, p in zip(got, pieces)]


def as_rows(piece):
    return jnp.transpose(piece, (1, 2, 0, 3)).reshape(-1, piece.shape[3])


def from_rows(rows, shape):
    channels, planes, lines, breadth = shape
    return jnp.transpose(rows.reshape(planes, lines, channels, breadth), (2, 0, 1, 3))


def ranges(shift, count, border):
    if shift == 1:
        return slice(border + count - 1, border + count)
    if shift == -1:
        return slice(border, border + 1)
    return slice(border, border + count)


def framed_features(features):
    _, planes, rows, _ = features.shape
    pieces = [features[:, ranges(dz, planes, 0), ranges(dy, rows, 0)] for dz, dy in NEIGHBOURS]
    got = dict(zip(NEIGHBOURS, halo_swap(pieces, 1)))
    lines = []
    for dz in (1, 0, -1):
        middle = features if dz == 0 else got[(dz, 0)]
        lines.append(jnp.concatenate([got[(dz, 1)], middle, got[(dz, -1)]], axis=2))
    return jnp.concatenate(lines, axis=1)


def border_pieces(spread):
    _, planes, rows, _ = spread.shape
    planes, rows = planes - 2, rows - 2
    pieces = []
    for dz, dy in NEIGHBOURS:
        zs = slice(planes + 1, planes + 2) if dz == 1 else slice(0, 1) if dz == -1 else slice(1, planes + 1)
        ys = slice(rows + 1, rows + 2) if dy == 1 else slice(0, 1) if dy == -1 else slice(1, rows + 1)
        pieces.append(spread[:, zs, ys].astype(jnp.bfloat16))
    return pieces


def folded_grad(spread, got):
    _, planes, rows, _ = spread.shape
    planes, rows = planes - 2, rows - 2
    own = spread[:, 1 : planes + 1, 1 : rows + 1]
    for (dz, dy), piece in zip(NEIGHBOURS, got):
        own = own.at[:, ranges(-dz, planes, 0), ranges(-dy, rows, 0)].add(piece.astype(own.dtype))
    return own


def mesh_bits():
    sizes = {"gz": lax.axis_size("gz"), "gy": lax.axis_size("gy")}
    orders = [[pair[c] for pair in BIT_ORDER if (1 << pair[c][1]) < sizes[pair[c][0]]] for c in (0, 1)]
    return list(zip(*orders))


def allreduce_kernel(bits, halvings, offsets, x_ref, *refs):
    count = len(offsets)
    pieces, o_ref = refs[:count], refs[count]
    landed = refs[count + 1 : 2 * count + 1]
    scratch = refs[2 * count + 1 :]
    halve_bufs = scratch[:halvings]
    work, double_buf, send_sems, recv_sems, halo_send, halo_recv = scratch[halvings:]
    here = {"gz": lax.axis_index("gz"), "gy": lax.axis_index("gy")}
    sizes = {"gz": lax.axis_size("gz"), "gy": lax.axis_size("gy")}

    def neighbour(dz, dy):
        return ((here["gz"] + dz + sizes["gz"]) % sizes["gz"], (here["gy"] + dy + sizes["gy"]) % sizes["gy"])

    core = here["gy"] % 2

    def pick(pair):
        (axis0, b0), (axis1, b1) = pair
        a0, a1 = int(axis0 == "gy"), int(axis1 == "gy")
        return a0 + (a1 - a0) * core, (1 << b0) + ((1 << b1) - (1 << b0)) * core

    def bit_of(pair):
        which, weight = pick(pair)
        value = here["gz"] + (here["gy"] - here["gz"]) * which
        return (value // weight) % 2

    def partner(*pairs):
        device = [here["gz"], here["gy"]]
        for pair in pairs:
            which, weight = pick(pair)
            step = (1 - 2 * bit_of(pair)) * weight
            device = [device[0] + step * (1 - which), device[1] + step * which]
        return tuple(device)

    groups = [bits[i : i + 2] for i in range(halvings, len(bits), 2)]
    reach = [(pair,) for pair in bits] + [tuple(g) for g in groups if len(g) == 2]

    barrier = pltpu.get_barrier_semaphore()
    for pairs in reach:
        pl.semaphore_signal(barrier, inc=1, device_id=partner(*pairs), device_id_type=MESH_ID)
    for dz, dy in offsets:
        pl.semaphore_signal(barrier, inc=1, device_id=neighbour(dz, dy), device_id_type=MESH_ID)
    pl.semaphore_wait(barrier, len(reach) + count)
    halo = []
    for i, (dz, dy) in enumerate(offsets):
        copy = pltpu.make_async_remote_copy(
            src_ref=pieces[i],
            dst_ref=landed[i],
            send_sem=halo_send.at[i],
            recv_sem=halo_recv.at[i],
            device_id=neighbour(dz, dy),
            device_id_type=MESH_ID,
        )
        copy.start()
        halo.append(copy)

    def exchange(step, pair, src, dst):
        start_copy(step, (pair,), src, dst).wait()

    def start_copy(step, pairs, src, dst):
        copy = pltpu.make_async_remote_copy(
            src_ref=src,
            dst_ref=dst,
            send_sem=send_sems.at[step],
            recv_sem=recv_sems.at[step],
            device_id=partner(*pairs),
            device_id_type=MESH_ID,
        )
        copy.start()
        return copy

    lo, length, step = 0, o_ref.shape[0], 0
    for k in range(halvings):
        pair = bits[k]
        half = length // 2
        bit = bit_of(pair)
        keep = pl.multiple_of(lo + bit * half, 8)
        give = pl.multiple_of(lo + (1 - bit) * half, 8)
        source = x_ref if k == 0 else work
        exchange(step, pair, source.at[pl.ds(give, half)], halve_bufs[k])
        work[pl.ds(keep, half)] = source[pl.ds(keep, half)] + halve_bufs[k][...]
        lo, length, step = keep, half, step + 1
    slot = 0
    for group in groups:
        own = work.at[pl.ds(lo, length)]
        if len(group) == 1:
            exchange(step, group[0], own, double_buf.at[slot])
            work[pl.ds(lo, length)] = own[...] + double_buf[slot]
            slot, step = slot + 1, step + 1
            continue
        flips = [(group[0],), (group[1],), (group[0], group[1])]
        copies = [start_copy(step + m, f, own, double_buf.at[slot + m]) for m, f in enumerate(flips)]
        for copy in copies:
            copy.wait()
        near, far = double_buf[slot] + own[...], double_buf[slot + 1] + double_buf[slot + 2]
        work[pl.ds(lo, length)] = near + far
        slot, step = slot + 3, step + 3
    o_ref[pl.ds(lo, length)] = work[pl.ds(lo, length)]
    for k in reversed(range(halvings)):
        pair = bits[k]
        region = o_ref.at[pl.ds(lo, length)]
        exchange(step, pair, region, region)
        lo = pl.multiple_of(lo - bit_of(pair) * length, 8)
        length, step = length * 2, step + 1
    for copy in halo:
        copy.wait()


def allreduce(flat, pieces=(), halvings=HALVINGS):
    offsets = NEIGHBOURS[: len(pieces)]
    pieces = [p.reshape(-1, 128) for p in pieces]
    bits = mesh_bits()
    halvings = min(halvings, len(bits))
    rows = flat.shape[0]
    segment = rows >> halvings
    far = len(bits) - halvings
    slots = 3 * (far // 2) + far % 2
    steps = 2 * halvings + slots
    scratch = [pltpu.VMEM((rows >> (k + 1), 128), jnp.float32) for k in range(halvings)]
    scratch += [
        pltpu.VMEM(flat.shape, jnp.float32),
        pltpu.VMEM((max(slots, 1), segment, 128), jnp.float32),
        pltpu.SemaphoreType.DMA((steps,)),
        pltpu.SemaphoreType.DMA((steps,)),
        pltpu.SemaphoreType.DMA((max(len(pieces), 1),)),
        pltpu.SemaphoreType.DMA((max(len(pieces), 1),)),
    ]
    vmem = pl.BlockSpec(memory_space=pltpu.VMEM)
    outs = pl.pallas_call(
        functools.partial(allreduce_kernel, bits, halvings, offsets),
        out_shape=[jax.ShapeDtypeStruct(flat.shape, jnp.float32)]
        + [jax.ShapeDtypeStruct(p.shape, p.dtype) for p in pieces],
        in_specs=[vmem] * (1 + len(pieces)),
        out_specs=[vmem] * (1 + len(pieces)),
        scratch_shapes=scratch,
        compiler_params=pltpu.CompilerParams(collective_id=0, has_side_effects=True),
    )(flat, *pieces)
    return outs[0], outs[1:]


def summed_gradients(local_conv, local_down, pieces):
    sizes = (local_conv.size, local_down.size)
    flat = jnp.concatenate([local_conv.reshape(-1), local_down.reshape(-1)])
    unit = 128 * 8 << HALVINGS
    padded = -(-flat.size // unit) * unit
    flat = jnp.pad(flat, (0, padded - flat.size)).reshape(-1, 128)
    total, got = allreduce(flat, [as_rows(p) for p in pieces])
    total = total.reshape(-1)
    return (
        total[: sizes[0]].reshape(local_conv.shape),
        total[sizes[0] : sizes[0] + sizes[1]].reshape(local_down.shape),
        [from_rows(g, p.shape) for g, p in zip(got, pieces)],
    )


def body(features, conv_weight, down_weight, cotangent):
    channels, plane_count, row_count, breadth = features.shape
    out_channels = down_weight.shape[2]
    cell_count = plane_count * row_count * breadth * lax.axis_size("gz") * lax.axis_size("gy")
    grad_scale = 1.0 / math.sqrt(cell_count)
    framed = framed_features(features)
    columns = widen(framed)
    preact = jnp.zeros((channels, plane_count, row_count, breadth), jnp.float32)
    for tap_z in range(3):
        for tap_y in range(3):
            window = columns[:, tap_z : tap_z + plane_count, tap_y : tap_y + row_count]
            preact = preact + jnp.einsum(
                "oj,jzyx->ozyx",
                conv_weight[tap_z, tap_y],
                window,
                preferred_element_type=jnp.float32,
            )
    hidden = jax.nn.silu(preact).astype(jnp.bfloat16)
    blocks = hidden.reshape(channels, plane_count // 2, 2, row_count // 2, 2, breadth // 2, 2)
    down_split = down_weight.reshape(2, 2, out_channels, 2, channels)
    coarse = jnp.einsum(
        "aboei,iZaYbXe->oZYX", down_split, blocks, preferred_element_type=jnp.float32
    )
    section_out = coarse.reshape(out_channels, plane_count // 2, -1).astype(jnp.bfloat16)
    coarse_cot = cotangent.reshape(out_channels, plane_count // 2, row_count // 2, breadth // 2)
    hidden_grad = jnp.einsum(
        "aboei,oZYX->iZaYbXe", down_split, coarse_cot, preferred_element_type=jnp.float32
    )
    hidden_grad = hidden_grad.reshape(channels, plane_count, row_count, breadth)
    local_down = jnp.einsum(
        "oZYX,iZaYbXe->aboei", coarse_cot, blocks, preferred_element_type=jnp.float32
    )
    local_down = local_down.reshape(2, 2, out_channels, 2 * channels)
    gate_sig = jax.nn.sigmoid(preact)
    gate_grad = (hidden_grad * gate_sig * (1.0 + preact * (1.0 - gate_sig))).astype(jnp.bfloat16)
    kernel_rows = []
    for tap_z in range(3):
        row_list = []
        for tap_y in range(3):
            window = columns[:, tap_z : tap_z + plane_count, tap_y : tap_y + row_count]
            row_list.append(
                jnp.einsum("ozyx,jzyx->oj", gate_grad, window, preferred_element_type=jnp.float32)
            )
        kernel_rows.append(jnp.stack(row_list, axis=0))
    local_conv = jnp.stack(kernel_rows, axis=0)
    spread = jnp.zeros((3 * channels, plane_count + 2, row_count + 2, breadth), jnp.float32)
    for tap_z in range(3):
        for tap_y in range(3):
            term = jnp.einsum(
                "oj,ozyx->jzyx",
                conv_weight[tap_z, tap_y],
                gate_grad,
                preferred_element_type=jnp.float32,
            )
            spread = spread.at[:, tap_z : tap_z + plane_count, tap_y : tap_y + row_count].add(term)
    folded = fold_along(spread, channels)
    summed_conv, summed_down, got = summed_gradients(local_conv, local_down, border_pieces(folded))
    row_fold = folded_grad(folded, got)
    grad_conv = summed_conv * grad_scale
    grad_down = summed_down * grad_scale
    return (section_out, row_fold, grad_conv, grad_down)


def solution(mesh):
    return jax.shard_map(
        body,
        mesh=mesh,
        in_specs=(P(None, "gz", "gy", None), P(), P(), P(None, "gz", "gy")),
        out_specs=(P(None, "gz", "gy"), P(None, "gz", "gy", None), P(), P()),
        check_vma=False,
    )
```

```python
import functools
import math

import jax
import jax.numpy as jnp
from jax import lax
from jax.experimental import pallas as pl
from jax.experimental.pallas import tpu as pltpu
from jax.sharding import PartitionSpec as P

MESH_ID = pl.DeviceIdType.MESH
BIT_ORDER = (
    (("gy", 0), ("gy", 0)),
    (("gy", 1), ("gz", 0)),
    (("gz", 0), ("gz", 3)),
    (("gz", 3), ("gy", 1)),
    (("gy", 2), ("gz", 1)),
    (("gz", 1), ("gy", 2)),
    (("gz", 4), ("gz", 2)),
    (("gz", 2), ("gz", 4)),
    (("gy", 3), ("gy", 3)),
)
HALVINGS = 4


def extended(cells, sides, width):
    for axis, dim in sides:
        count = lax.axis_size(axis)
        head = lax.slice_in_dim(cells, 0, width, axis=dim)
        tail = lax.slice_in_dim(cells, cells.shape[dim] - width, cells.shape[dim], axis=dim)
        cells = jnp.concatenate(
            [
                lax.ppermute(tail, axis, [(i, (i + 1) % count) for i in range(count)]),
                cells,
                lax.ppermute(head, axis, [((i + 1) % count, i) for i in range(count)]),
            ],
            axis=dim,
        )
    return cells


def widen(framed):
    return jnp.concatenate([jnp.roll(framed, 1 - tap_x, axis=3) for tap_x in range(3)], axis=0)


def fold_along(spread, channels):
    result = jnp.roll(spread[0:channels], -1, axis=3)
    result = result + spread[channels : 2 * channels]
    result = result + jnp.roll(spread[2 * channels : 3 * channels], 1, axis=3)
    return result


NEIGHBOURS = ((1, 0), (-1, 0), (0, 1), (0, -1), (1, 1), (1, -1), (-1, 1), (-1, -1))


def halo_kernel(offsets, *refs):
    count = len(offsets)
    sources, targets = refs[:count], refs[count : 2 * count]
    send_sems, recv_sems = refs[2 * count :]
    sizes = (lax.axis_size("gz"), lax.axis_size("gy"))
    here = (lax.axis_index("gz"), lax.axis_index("gy"))

    def device(dz, dy):
        return ((here[0] + dz + sizes[0]) % sizes[0], (here[1] + dy + sizes[1]) % sizes[1])

    barrier = pltpu.get_barrier_semaphore()
    for dz, dy in offsets:
        pl.semaphore_signal(barrier, inc=1, device_id=device(dz, dy), device_id_type=MESH_ID)
    pl.semaphore_wait(barrier, count)
    copies = []
    for i, (dz, dy) in enumerate(offsets):
        copy = pltpu.make_async_remote_copy(
            src_ref=sources[i],
            dst_ref=targets[i],
            send_sem=send_sems.at[i],
            recv_sem=recv_sems.at[i],
            device_id=device(dz, dy),
            device_id_type=MESH_ID,
        )
        copy.start()
        copies.append(copy)
    for copy in copies:
        copy.wait()


def halo_swap(pieces, collective_id):
    flat = [as_rows(p) for p in pieces]
    vmem = pl.BlockSpec(memory_space=pltpu.VMEM)
    got = pl.pallas_call(
        functools.partial(halo_kernel, NEIGHBOURS),
        out_shape=[jax.ShapeDtypeStruct(f.shape, f.dtype) for f in flat],
        in_specs=[vmem] * len(flat),
        out_specs=[vmem] * len(flat),
        scratch_shapes=[pltpu.SemaphoreType.DMA((len(flat),)), pltpu.SemaphoreType.DMA((len(flat),))],
        compiler_params=pltpu.CompilerParams(collective_id=collective_id, has_side_effects=True),
    )(*flat)
    return [from_rows(g, p.shape) for g, p in zip(got, pieces)]


def as_rows(piece):
    return jnp.transpose(piece, (1, 2, 0, 3)).reshape(-1, piece.shape[3])


def from_rows(rows, shape):
    channels, planes, lines, breadth = shape
    return jnp.transpose(rows.reshape(planes, lines, channels, breadth), (2, 0, 1, 3))


def ranges(shift, count, border):
    if shift == 1:
        return slice(border + count - 1, border + count)
    if shift == -1:
        return slice(border, border + 1)
    return slice(border, border + count)


def framed_features(features):
    _, planes, rows, _ = features.shape
    pieces = [features[:, ranges(dz, planes, 0), ranges(dy, rows, 0)] for dz, dy in NEIGHBOURS]
    got = dict(zip(NEIGHBOURS, halo_swap(pieces, 1)))
    lines = []
    for dz in (1, 0, -1):
        middle = features if dz == 0 else got[(dz, 0)]
        lines.append(jnp.concatenate([got[(dz, 1)], middle, got[(dz, -1)]], axis=2))
    return jnp.concatenate(lines, axis=1)


def border_pieces(spread):
    _, planes, rows, _ = spread.shape
    planes, rows = planes - 2, rows - 2
    pieces = []
    for dz, dy in NEIGHBOURS:
        zs = slice(planes + 1, planes + 2) if dz == 1 else slice(0, 1) if dz == -1 else slice(1, planes + 1)
        ys = slice(rows + 1, rows + 2) if dy == 1 else slice(0, 1) if dy == -1 else slice(1, rows + 1)
        pieces.append(spread[:, zs, ys].astype(jnp.bfloat16))
    return pieces


def folded_grad(spread, got):
    _, planes, rows, _ = spread.shape
    planes, rows = planes - 2, rows - 2
    own = spread[:, 1 : planes + 1, 1 : rows + 1]
    for (dz, dy), piece in zip(NEIGHBOURS, got):
        own = own.at[:, ranges(-dz, planes, 0), ranges(-dy, rows, 0)].add(piece.astype(own.dtype))
    return own


def mesh_bits():
    sizes = {"gz": lax.axis_size("gz"), "gy": lax.axis_size("gy")}
    orders = [[pair[c] for pair in BIT_ORDER if (1 << pair[c][1]) < sizes[pair[c][0]]] for c in (0, 1)]
    return list(zip(*orders))


def allreduce_kernel(bits, halvings, offsets, x_ref, *refs):
    count = len(offsets)
    pieces, o_ref = refs[:count], refs[count]
    landed = refs[count + 1 : 2 * count + 1]
    scratch = refs[2 * count + 1 :]
    halve_bufs = scratch[:halvings]
    work, double_buf, send_sems, recv_sems, halo_send, halo_recv = scratch[halvings:]
    here = {"gz": lax.axis_index("gz"), "gy": lax.axis_index("gy")}
    sizes = {"gz": lax.axis_size("gz"), "gy": lax.axis_size("gy")}

    def neighbour(dz, dy):
        return ((here["gz"] + dz + sizes["gz"]) % sizes["gz"], (here["gy"] + dy + sizes["gy"]) % sizes["gy"])

    core = here["gy"] % 2

    def pick(pair):
        (axis0, b0), (axis1, b1) = pair
        a0, a1 = int(axis0 == "gy"), int(axis1 == "gy")
        return a0 + (a1 - a0) * core, (1 << b0) + ((1 << b1) - (1 << b0)) * core

    def bit_of(pair):
        which, weight = pick(pair)
        value = here["gz"] + (here["gy"] - here["gz"]) * which
        return (value // weight) % 2

    def partner(*pairs):
        device = [here["gz"], here["gy"]]
        for pair in pairs:
            which, weight = pick(pair)
            step = (1 - 2 * bit_of(pair)) * weight
            device = [device[0] + step * (1 - which), device[1] + step * which]
        return tuple(device)

    groups = [bits[i : i + 2] for i in range(halvings, len(bits), 2)]
    reach = [(pair,) for pair in bits] + [tuple(g) for g in groups if len(g) == 2]

    barrier = pltpu.get_barrier_semaphore()
    for pairs in reach:
        pl.semaphore_signal(barrier, inc=1, device_id=partner(*pairs), device_id_type=MESH_ID)
    for dz, dy in offsets:
        pl.semaphore_signal(barrier, inc=1, device_id=neighbour(dz, dy), device_id_type=MESH_ID)
    pl.semaphore_wait(barrier, len(reach) + count)
    halo = []
    for i, (dz, dy) in enumerate(offsets):
        copy = pltpu.make_async_remote_copy(
            src_ref=pieces[i],
            dst_ref=landed[i],
            send_sem=halo_send.at[i],
            recv_sem=halo_recv.at[i],
            device_id=neighbour(dz, dy),
            device_id_type=MESH_ID,
        )
        copy.start()
        halo.append(copy)

    def exchange(step, pair, src, dst):
        start_copy(step, (pair,), src, dst).wait()

    def start_copy(step, pairs, src, dst):
        copy = pltpu.make_async_remote_copy(
            src_ref=src,
            dst_ref=dst,
            send_sem=send_sems.at[step],
            recv_sem=recv_sems.at[step],
            device_id=partner(*pairs),
            device_id_type=MESH_ID,
        )
        copy.start()
        return copy

    lo, length, step = 0, o_ref.shape[0], 0
    for k in range(halvings):
        pair = bits[k]
        half = length // 2
        bit = bit_of(pair)
        keep = pl.multiple_of(lo + bit * half, 8)
        give = pl.multiple_of(lo + (1 - bit) * half, 8)
        source = x_ref if k == 0 else work
        exchange(step, pair, source.at[pl.ds(give, half)], halve_bufs[k])
        work[pl.ds(keep, half)] = source[pl.ds(keep, half)] + halve_bufs[k][...]
        lo, length, step = keep, half, step + 1
    slot = 0
    for group in groups:
        own = work.at[pl.ds(lo, length)]
        if len(group) == 1:
            exchange(step, group[0], own, double_buf.at[slot])
            work[pl.ds(lo, length)] = own[...] + double_buf[slot]
            slot, step = slot + 1, step + 1
            continue
        flips = [(group[0],), (group[1],), (group[0], group[1])]
        copies = [start_copy(step + m, f, own, double_buf.at[slot + m]) for m, f in enumerate(flips)]
        for copy in copies:
            copy.wait()
        near, far = double_buf[slot] + own[...], double_buf[slot + 1] + double_buf[slot + 2]
        work[pl.ds(lo, length)] = near + far
        slot, step = slot + 3, step + 3
    o_ref[pl.ds(lo, length)] = work[pl.ds(lo, length)]
    for k in reversed(range(halvings)):
        pair = bits[k]
        region = o_ref.at[pl.ds(lo, length)]
        exchange(step, pair, region, region)
        lo = pl.multiple_of(lo - bit_of(pair) * length, 8)
        length, step = length * 2, step + 1
    for copy in halo:
        copy.wait()


def allreduce(flat, pieces=(), halvings=HALVINGS):
    offsets = NEIGHBOURS[: len(pieces)]
    pieces = [p.reshape(-1, 128) for p in pieces]
    bits = mesh_bits()
    halvings = min(halvings, len(bits))
    rows = flat.shape[0]
    segment = rows >> halvings
    far = len(bits) - halvings
    slots = 3 * (far // 2) + far % 2
    steps = 2 * halvings + slots
    scratch = [pltpu.VMEM((rows >> (k + 1), 128), jnp.float32) for k in range(halvings)]
    scratch += [
        pltpu.VMEM(flat.shape, jnp.float32),
        pltpu.VMEM((max(slots, 1), segment, 128), jnp.float32),
        pltpu.SemaphoreType.DMA((steps,)),
        pltpu.SemaphoreType.DMA((steps,)),
        pltpu.SemaphoreType.DMA((max(len(pieces), 1),)),
        pltpu.SemaphoreType.DMA((max(len(pieces), 1),)),
    ]
    vmem = pl.BlockSpec(memory_space=pltpu.VMEM)
    outs = pl.pallas_call(
        functools.partial(allreduce_kernel, bits, halvings, offsets),
        out_shape=[jax.ShapeDtypeStruct(flat.shape, jnp.float32)]
        + [jax.ShapeDtypeStruct(p.shape, p.dtype) for p in pieces],
        in_specs=[vmem] * (1 + len(pieces)),
        out_specs=[vmem] * (1 + len(pieces)),
        scratch_shapes=scratch,
        compiler_params=pltpu.CompilerParams(collective_id=0, has_side_effects=True),
    )(flat, *pieces)
    return outs[0], outs[1:]


def summed_gradients(local_conv, local_down, pieces, scale):
    sizes = (local_conv.size, local_down.size)
    flat = jnp.concatenate([local_conv.reshape(-1), local_down.reshape(-1)]) * scale
    unit = 128 * 8 << HALVINGS
    padded = -(-flat.size // unit) * unit
    flat = jnp.pad(flat, (0, padded - flat.size)).reshape(-1, 128)
    total, got = allreduce(flat, [as_rows(p) for p in pieces])
    total = total.reshape(-1)
    return (
        total[: sizes[0]].reshape(local_conv.shape),
        total[sizes[0] : sizes[0] + sizes[1]].reshape(local_down.shape),
        [from_rows(g, p.shape) for g, p in zip(got, pieces)],
    )


def body(features, conv_weight, down_weight, cotangent):
    channels, plane_count, row_count, breadth = features.shape
    out_channels = down_weight.shape[2]
    cell_count = plane_count * row_count * breadth * lax.axis_size("gz") * lax.axis_size("gy")
    grad_scale = 1.0 / math.sqrt(cell_count)
    framed = framed_features(features)
    columns = widen(framed)
    preact = jnp.zeros((channels, plane_count, row_count, breadth), jnp.float32)
    for tap_z in range(3):
        for tap_y in range(3):
            window = columns[:, tap_z : tap_z + plane_count, tap_y : tap_y + row_count]
            preact = preact + jnp.einsum(
                "oj,jzyx->ozyx",
                conv_weight[tap_z, tap_y],
                window,
                preferred_element_type=jnp.float32,
            )
    hidden = jax.nn.silu(preact).astype(jnp.bfloat16)
    blocks = hidden.reshape(channels, plane_count // 2, 2, row_count // 2, 2, breadth // 2, 2)
    down_split = down_weight.reshape(2, 2, out_channels, 2, channels)
    coarse = jnp.einsum(
        "aboei,iZaYbXe->oZYX", down_split, blocks, preferred_element_type=jnp.float32
    )
    section_out = coarse.reshape(out_channels, plane_count // 2, -1).astype(jnp.bfloat16)
    coarse_cot = cotangent.reshape(out_channels, plane_count // 2, row_count // 2, breadth // 2)
    hidden_grad = jnp.einsum(
        "aboei,oZYX->iZaYbXe", down_split, coarse_cot, preferred_element_type=jnp.float32
    )
    hidden_grad = hidden_grad.reshape(channels, plane_count, row_count, breadth)
    local_down = jnp.einsum(
        "oZYX,iZaYbXe->aboei", coarse_cot, blocks, preferred_element_type=jnp.float32
    )
    local_down = local_down.reshape(2, 2, out_channels, 2 * channels)
    gate_sig = jax.nn.sigmoid(preact)
    gate_grad = (hidden_grad * gate_sig * (1.0 + preact * (1.0 - gate_sig))).astype(jnp.bfloat16)
    kernel_rows = []
    for tap_z in range(3):
        row_list = []
        for tap_y in range(3):
            window = columns[:, tap_z : tap_z + plane_count, tap_y : tap_y + row_count]
            row_list.append(
                jnp.einsum("ozyx,jzyx->oj", gate_grad, window, preferred_element_type=jnp.float32)
            )
        kernel_rows.append(jnp.stack(row_list, axis=0))
    local_conv = jnp.stack(kernel_rows, axis=0)
    spread = jnp.zeros((3 * channels, plane_count + 2, row_count + 2, breadth), jnp.float32)
    for tap_z in range(3):
        for tap_y in range(3):
            term = jnp.einsum(
                "oj,ozyx->jzyx",
                conv_weight[tap_z, tap_y],
                gate_grad,
                preferred_element_type=jnp.float32,
            )
            spread = spread.at[:, tap_z : tap_z + plane_count, tap_y : tap_y + row_count].add(term)
    folded = fold_along(spread, channels)
    summed_conv, summed_down, got = summed_gradients(local_conv, local_down, border_pieces(folded), grad_scale)
    row_fold = folded_grad(folded, got)
    return (section_out, row_fold, summed_conv, summed_down)


def solution(mesh):
    return jax.shard_map(
        body,
        mesh=mesh,
        in_specs=(P(None, "gz", "gy", None), P(), P(), P(None, "gz", "gy")),
        out_specs=(P(None, "gz", "gy"), P(None, "gz", "gy", None), P(), P()),
        check_vma=False,
    )
```

```python
import functools
import math

import jax
import jax.numpy as jnp
from jax import lax
from jax.experimental import pallas as pl
from jax.experimental.pallas import tpu as pltpu
from jax.sharding import PartitionSpec as P

MESH_ID = pl.DeviceIdType.MESH
BIT_ORDER = (
    (("gy", 0), ("gy", 0)),
    (("gy", 1), ("gz", 0)),
    (("gz", 0), ("gz", 3)),
    (("gz", 3), ("gy", 1)),
    (("gy", 2), ("gz", 1)),
    (("gz", 1), ("gy", 2)),
    (("gz", 4), ("gz", 2)),
    (("gz", 2), ("gz", 4)),
    (("gy", 3), ("gy", 3)),
)
HALVINGS = 4


def extended(cells, sides, width):
    for axis, dim in sides:
        count = lax.axis_size(axis)
        head = lax.slice_in_dim(cells, 0, width, axis=dim)
        tail = lax.slice_in_dim(cells, cells.shape[dim] - width, cells.shape[dim], axis=dim)
        cells = jnp.concatenate(
            [
                lax.ppermute(tail, axis, [(i, (i + 1) % count) for i in range(count)]),
                cells,
                lax.ppermute(head, axis, [((i + 1) % count, i) for i in range(count)]),
            ],
            axis=dim,
        )
    return cells


def widen(framed):
    return jnp.concatenate([jnp.roll(framed, 1 - tap_x, axis=3) for tap_x in range(3)], axis=0)


def fold_along(spread, channels):
    result = jnp.roll(spread[0:channels], -1, axis=3)
    result = result + spread[channels : 2 * channels]
    result = result + jnp.roll(spread[2 * channels : 3 * channels], 1, axis=3)
    return result


NEIGHBOURS = ((1, 0), (-1, 0), (0, 1), (0, -1), (1, 1), (1, -1), (-1, 1), (-1, -1))


def halo_kernel(offsets, *refs):
    count = len(offsets)
    sources, targets = refs[:count], refs[count : 2 * count]
    send_sems, recv_sems = refs[2 * count :]
    sizes = (lax.axis_size("gz"), lax.axis_size("gy"))
    here = (lax.axis_index("gz"), lax.axis_index("gy"))

    def device(dz, dy):
        return ((here[0] + dz + sizes[0]) % sizes[0], (here[1] + dy + sizes[1]) % sizes[1])

    barrier = pltpu.get_barrier_semaphore()
    for dz, dy in offsets:
        pl.semaphore_signal(barrier, inc=1, device_id=device(dz, dy), device_id_type=MESH_ID)
    pl.semaphore_wait(barrier, count)
    copies = []
    for i, (dz, dy) in enumerate(offsets):
        copy = pltpu.make_async_remote_copy(
            src_ref=sources[i],
            dst_ref=targets[i],
            send_sem=send_sems.at[i],
            recv_sem=recv_sems.at[i],
            device_id=device(dz, dy),
            device_id_type=MESH_ID,
        )
        copy.start()
        copies.append(copy)
    for copy in copies:
        copy.wait()


def halo_swap(pieces, collective_id):
    flat = [as_rows(p) for p in pieces]
    vmem = pl.BlockSpec(memory_space=pltpu.VMEM)
    got = pl.pallas_call(
        functools.partial(halo_kernel, NEIGHBOURS),
        out_shape=[jax.ShapeDtypeStruct(f.shape, f.dtype) for f in flat],
        in_specs=[vmem] * len(flat),
        out_specs=[vmem] * len(flat),
        scratch_shapes=[pltpu.SemaphoreType.DMA((len(flat),)), pltpu.SemaphoreType.DMA((len(flat),))],
        compiler_params=pltpu.CompilerParams(collective_id=collective_id, has_side_effects=True),
    )(*flat)
    return [from_rows(g, p.shape) for g, p in zip(got, pieces)]


def as_rows(piece):
    return jnp.transpose(piece, (1, 2, 0, 3)).reshape(-1, piece.shape[3])


def from_rows(rows, shape):
    channels, planes, lines, breadth = shape
    return jnp.transpose(rows.reshape(planes, lines, channels, breadth), (2, 0, 1, 3))


def ranges(shift, count, border):
    if shift == 1:
        return slice(border + count - 1, border + count)
    if shift == -1:
        return slice(border, border + 1)
    return slice(border, border + count)


def halo_pieces(cells):
    _, planes, rows, _ = cells.shape
    return [cells[:, ranges(dz, planes, 0), ranges(dy, rows, 0)] for dz, dy in NEIGHBOURS]


def framed(cells, received):
    got = dict(zip(NEIGHBOURS, received))
    lines = []
    for dz in (1, 0, -1):
        middle = cells if dz == 0 else got[(dz, 0)]
        lines.append(jnp.concatenate([got[(dz, 1)], middle, got[(dz, -1)]], axis=2))
    return jnp.concatenate(lines, axis=1)


def conv_taps(columns, weight, shape):
    _, planes, rows, _ = shape
    total = jnp.zeros(shape, jnp.float32)
    for tap_z in range(3):
        for tap_y in range(3):
            window = columns[:, tap_z : tap_z + planes, tap_y : tap_y + rows]
            total = total + jnp.einsum(
                "oj,jzyx->ozyx", weight[tap_z, tap_y], window, preferred_element_type=jnp.float32
            )
    return total


def transposed_weight(conv_weight):
    taps_z, taps_y, channels, width = conv_weight.shape
    split = conv_weight.reshape(taps_z, taps_y, channels, width // channels, channels)
    split = split[::-1, ::-1, :, ::-1, :]
    return jnp.transpose(split, (0, 1, 4, 3, 2)).reshape(taps_z, taps_y, channels, width)


def border_pieces(spread):
    _, planes, rows, _ = spread.shape
    planes, rows = planes - 2, rows - 2
    pieces = []
    for dz, dy in NEIGHBOURS:
        zs = slice(planes + 1, planes + 2) if dz == 1 else slice(0, 1) if dz == -1 else slice(1, planes + 1)
        ys = slice(rows + 1, rows + 2) if dy == 1 else slice(0, 1) if dy == -1 else slice(1, rows + 1)
        pieces.append(spread[:, zs, ys].astype(jnp.bfloat16))
    return pieces


def folded_grad(spread, got):
    _, planes, rows, _ = spread.shape
    planes, rows = planes - 2, rows - 2
    own = spread[:, 1 : planes + 1, 1 : rows + 1]
    for (dz, dy), piece in zip(NEIGHBOURS, got):
        own = own.at[:, ranges(-dz, planes, 0), ranges(-dy, rows, 0)].add(piece.astype(own.dtype))
    return own


def mesh_bits():
    sizes = {"gz": lax.axis_size("gz"), "gy": lax.axis_size("gy")}
    orders = [[pair[c] for pair in BIT_ORDER if (1 << pair[c][1]) < sizes[pair[c][0]]] for c in (0, 1)]
    return list(zip(*orders))


def allreduce_kernel(bits, halvings, offsets, x_ref, *refs):
    count = len(offsets)
    pieces, o_ref = refs[:count], refs[count]
    landed = refs[count + 1 : 2 * count + 1]
    scratch = refs[2 * count + 1 :]
    halve_bufs = scratch[:halvings]
    work, double_buf, send_sems, recv_sems, halo_send, halo_recv = scratch[halvings:]
    here = {"gz": lax.axis_index("gz"), "gy": lax.axis_index("gy")}
    sizes = {"gz": lax.axis_size("gz"), "gy": lax.axis_size("gy")}

    def neighbour(dz, dy):
        return ((here["gz"] + dz + sizes["gz"]) % sizes["gz"], (here["gy"] + dy + sizes["gy"]) % sizes["gy"])

    core = here["gy"] % 2

    def pick(pair):
        (axis0, b0), (axis1, b1) = pair
        a0, a1 = int(axis0 == "gy"), int(axis1 == "gy")
        return a0 + (a1 - a0) * core, (1 << b0) + ((1 << b1) - (1 << b0)) * core

    def bit_of(pair):
        which, weight = pick(pair)
        value = here["gz"] + (here["gy"] - here["gz"]) * which
        return (value // weight) % 2

    def partner(*pairs):
        device = [here["gz"], here["gy"]]
        for pair in pairs:
            which, weight = pick(pair)
            step = (1 - 2 * bit_of(pair)) * weight
            device = [device[0] + step * (1 - which), device[1] + step * which]
        return tuple(device)

    groups = [bits[i : i + 2] for i in range(halvings, len(bits), 2)]
    reach = [(pair,) for pair in bits] + [tuple(g) for g in groups if len(g) == 2]

    barrier = pltpu.get_barrier_semaphore()
    for pairs in reach:
        pl.semaphore_signal(barrier, inc=1, device_id=partner(*pairs), device_id_type=MESH_ID)
    for dz, dy in offsets:
        pl.semaphore_signal(barrier, inc=1, device_id=neighbour(dz, dy), device_id_type=MESH_ID)
    pl.semaphore_wait(barrier, len(reach) + count)
    halo = []
    for i, (dz, dy) in enumerate(offsets):
        copy = pltpu.make_async_remote_copy(
            src_ref=pieces[i],
            dst_ref=landed[i],
            send_sem=halo_send.at[i],
            recv_sem=halo_recv.at[i],
            device_id=neighbour(dz, dy),
            device_id_type=MESH_ID,
        )
        copy.start()
        halo.append(copy)

    def exchange(step, pair, src, dst):
        start_copy(step, (pair,), src, dst).wait()

    def start_copy(step, pairs, src, dst):
        copy = pltpu.make_async_remote_copy(
            src_ref=src,
            dst_ref=dst,
            send_sem=send_sems.at[step],
            recv_sem=recv_sems.at[step],
            device_id=partner(*pairs),
            device_id_type=MESH_ID,
        )
        copy.start()
        return copy

    lo, length, step = 0, o_ref.shape[0], 0
    for k in range(halvings):
        pair = bits[k]
        half = length // 2
        bit = bit_of(pair)
        keep = pl.multiple_of(lo + bit * half, 8)
        give = pl.multiple_of(lo + (1 - bit) * half, 8)
        source = x_ref if k == 0 else work
        exchange(step, pair, source.at[pl.ds(give, half)], halve_bufs[k])
        work[pl.ds(keep, half)] = source[pl.ds(keep, half)] + halve_bufs[k][...]
        lo, length, step = keep, half, step + 1
    slot = 0
    for group in groups:
        own = work.at[pl.ds(lo, length)]
        if len(group) == 1:
            exchange(step, group[0], own, double_buf.at[slot])
            work[pl.ds(lo, length)] = own[...] + double_buf[slot]
            slot, step = slot + 1, step + 1
            continue
        flips = [(group[0],), (group[1],), (group[0], group[1])]
        copies = [start_copy(step + m, f, own, double_buf.at[slot + m]) for m, f in enumerate(flips)]
        for copy in copies:
            copy.wait()
        near, far = double_buf[slot] + own[...], double_buf[slot + 1] + double_buf[slot + 2]
        work[pl.ds(lo, length)] = near + far
        slot, step = slot + 3, step + 3
    o_ref[pl.ds(lo, length)] = work[pl.ds(lo, length)]
    for k in reversed(range(halvings)):
        pair = bits[k]
        region = o_ref.at[pl.ds(lo, length)]
        exchange(step, pair, region, region)
        lo = pl.multiple_of(lo - bit_of(pair) * length, 8)
        length, step = length * 2, step + 1
    for copy in halo:
        copy.wait()


def allreduce(flat, pieces=(), halvings=HALVINGS):
    offsets = NEIGHBOURS[: len(pieces)]
    pieces = [p.reshape(-1, 128) for p in pieces]
    bits = mesh_bits()
    halvings = min(halvings, len(bits))
    rows = flat.shape[0]
    segment = rows >> halvings
    far = len(bits) - halvings
    slots = 3 * (far // 2) + far % 2
    steps = 2 * halvings + slots
    scratch = [pltpu.VMEM((rows >> (k + 1), 128), jnp.float32) for k in range(halvings)]
    scratch += [
        pltpu.VMEM(flat.shape, jnp.float32),
        pltpu.VMEM((max(slots, 1), segment, 128), jnp.float32),
        pltpu.SemaphoreType.DMA((steps,)),
        pltpu.SemaphoreType.DMA((steps,)),
        pltpu.SemaphoreType.DMA((max(len(pieces), 1),)),
        pltpu.SemaphoreType.DMA((max(len(pieces), 1),)),
    ]
    vmem = pl.BlockSpec(memory_space=pltpu.VMEM)
    outs = pl.pallas_call(
        functools.partial(allreduce_kernel, bits, halvings, offsets),
        out_shape=[jax.ShapeDtypeStruct(flat.shape, jnp.float32)]
        + [jax.ShapeDtypeStruct(p.shape, p.dtype) for p in pieces],
        in_specs=[vmem] * (1 + len(pieces)),
        out_specs=[vmem] * (1 + len(pieces)),
        scratch_shapes=scratch,
        compiler_params=pltpu.CompilerParams(collective_id=0, has_side_effects=True),
    )(flat, *pieces)
    return outs[0], outs[1:]


def summed_gradients(local_conv, local_down, pieces, scale):
    sizes = (local_conv.size, local_down.size)
    flat = jnp.concatenate([local_conv.reshape(-1), local_down.reshape(-1)]) * scale
    unit = 128 * 8 << HALVINGS
    padded = -(-flat.size // unit) * unit
    flat = jnp.pad(flat, (0, padded - flat.size)).reshape(-1, 128)
    total, got = allreduce(flat, [as_rows(p) for p in pieces])
    total = total.reshape(-1)
    return (
        total[: sizes[0]].reshape(local_conv.shape),
        total[sizes[0] : sizes[0] + sizes[1]].reshape(local_down.shape),
        [from_rows(g, p.shape) for g, p in zip(got, pieces)],
    )


def body(features, conv_weight, down_weight, cotangent):
    channels, plane_count, row_count, breadth = features.shape
    out_channels = down_weight.shape[2]
    cell_count = plane_count * row_count * breadth * lax.axis_size("gz") * lax.axis_size("gy")
    grad_scale = 1.0 / math.sqrt(cell_count)
    columns = widen(framed(features, halo_swap(halo_pieces(features), 1)))
    preact = conv_taps(columns, conv_weight, features.shape)
    hidden = jax.nn.silu(preact).astype(jnp.bfloat16)
    blocks = hidden.reshape(channels, plane_count // 2, 2, row_count // 2, 2, breadth // 2, 2)
    down_split = down_weight.reshape(2, 2, out_channels, 2, channels)
    coarse = jnp.einsum(
        "aboei,iZaYbXe->oZYX", down_split, blocks, preferred_element_type=jnp.float32
    )
    section_out = coarse.reshape(out_channels, plane_count // 2, -1).astype(jnp.bfloat16)
    coarse_cot = cotangent.reshape(out_channels, plane_count // 2, row_count // 2, breadth // 2)
    hidden_grad = jnp.einsum(
        "aboei,oZYX->iZaYbXe", down_split, coarse_cot, preferred_element_type=jnp.float32
    )
    hidden_grad = hidden_grad.reshape(channels, plane_count, row_count, breadth)
    local_down = jnp.einsum(
        "oZYX,iZaYbXe->aboei", coarse_cot, blocks, preferred_element_type=jnp.float32
    )
    local_down = local_down.reshape(2, 2, out_channels, 2 * channels)
    gate_sig = jax.nn.sigmoid(preact)
    gate_grad = (hidden_grad * gate_sig * (1.0 + preact * (1.0 - gate_sig))).astype(jnp.bfloat16)
    kernel_rows = []
    for tap_z in range(3):
        row_list = []
        for tap_y in range(3):
            window = columns[:, tap_z : tap_z + plane_count, tap_y : tap_y + row_count]
            row_list.append(
                jnp.einsum("ozyx,jzyx->oj", gate_grad, window, preferred_element_type=jnp.float32)
            )
        kernel_rows.append(jnp.stack(row_list, axis=0))
    local_conv = jnp.stack(kernel_rows, axis=0)
    summed_conv, summed_down, got = summed_gradients(local_conv, local_down, halo_pieces(gate_grad), grad_scale)
    gate_columns = widen(framed(gate_grad, got))
    grad_field = conv_taps(gate_columns, transposed_weight(conv_weight), features.shape)
    return (section_out, grad_field, summed_conv, summed_down)


def solution(mesh):
    return jax.shard_map(
        body,
        mesh=mesh,
        in_specs=(P(None, "gz", "gy", None), P(), P(), P(None, "gz", "gy")),
        out_specs=(P(None, "gz", "gy"), P(None, "gz", "gy", None), P(), P()),
        check_vma=False,
    )
```

```python
import functools
import math

import jax
import jax.numpy as jnp
from jax import lax
from jax.experimental import pallas as pl
from jax.experimental.pallas import tpu as pltpu
from jax.sharding import PartitionSpec as P

MESH_ID = pl.DeviceIdType.MESH
BIT_ORDER = (
    (("gy", 0), ("gy", 0)),
    (("gy", 1), ("gz", 0)),
    (("gz", 0), ("gz", 3)),
    (("gz", 3), ("gy", 1)),
    (("gy", 2), ("gz", 1)),
    (("gz", 1), ("gy", 2)),
    (("gz", 4), ("gz", 2)),
    (("gz", 2), ("gz", 4)),
    (("gy", 3), ("gy", 3)),
)
HALVINGS = 3


def extended(cells, sides, width):
    for axis, dim in sides:
        count = lax.axis_size(axis)
        head = lax.slice_in_dim(cells, 0, width, axis=dim)
        tail = lax.slice_in_dim(cells, cells.shape[dim] - width, cells.shape[dim], axis=dim)
        cells = jnp.concatenate(
            [
                lax.ppermute(tail, axis, [(i, (i + 1) % count) for i in range(count)]),
                cells,
                lax.ppermute(head, axis, [((i + 1) % count, i) for i in range(count)]),
            ],
            axis=dim,
        )
    return cells


def widen(framed):
    return jnp.concatenate([jnp.roll(framed, 1 - tap_x, axis=3) for tap_x in range(3)], axis=0)


def fold_along(spread, channels):
    result = jnp.roll(spread[0:channels], -1, axis=3)
    result = result + spread[channels : 2 * channels]
    result = result + jnp.roll(spread[2 * channels : 3 * channels], 1, axis=3)
    return result


NEIGHBOURS = ((1, 0), (-1, 0), (0, 1), (0, -1), (1, 1), (1, -1), (-1, 1), (-1, -1))


def halo_kernel(offsets, *refs):
    count = len(offsets)
    sources, targets = refs[:count], refs[count : 2 * count]
    send_sems, recv_sems = refs[2 * count :]
    sizes = (lax.axis_size("gz"), lax.axis_size("gy"))
    here = (lax.axis_index("gz"), lax.axis_index("gy"))

    def device(dz, dy):
        return ((here[0] + dz + sizes[0]) % sizes[0], (here[1] + dy + sizes[1]) % sizes[1])

    barrier = pltpu.get_barrier_semaphore()
    for dz, dy in offsets:
        pl.semaphore_signal(barrier, inc=1, device_id=device(dz, dy), device_id_type=MESH_ID)
    pl.semaphore_wait(barrier, count)
    copies = []
    for i, (dz, dy) in enumerate(offsets):
        copy = pltpu.make_async_remote_copy(
            src_ref=sources[i],
            dst_ref=targets[i],
            send_sem=send_sems.at[i],
            recv_sem=recv_sems.at[i],
            device_id=device(dz, dy),
            device_id_type=MESH_ID,
        )
        copy.start()
        copies.append(copy)
    for copy in copies:
        copy.wait()


def halo_swap(pieces, collective_id):
    flat = [as_rows(p) for p in pieces]
    vmem = pl.BlockSpec(memory_space=pltpu.VMEM)
    got = pl.pallas_call(
        functools.partial(halo_kernel, NEIGHBOURS),
        out_shape=[jax.ShapeDtypeStruct(f.shape, f.dtype) for f in flat],
        in_specs=[vmem] * len(flat),
        out_specs=[vmem] * len(flat),
        scratch_shapes=[pltpu.SemaphoreType.DMA((len(flat),)), pltpu.SemaphoreType.DMA((len(flat),))],
        compiler_params=pltpu.CompilerParams(collective_id=collective_id, has_side_effects=True),
    )(*flat)
    return [from_rows(g, p.shape) for g, p in zip(got, pieces)]


def as_rows(piece):
    return jnp.transpose(piece, (1, 2, 0, 3)).reshape(-1, piece.shape[3])


def from_rows(rows, shape):
    channels, planes, lines, breadth = shape
    return jnp.transpose(rows.reshape(planes, lines, channels, breadth), (2, 0, 1, 3))


def ranges(shift, count, border):
    if shift == 1:
        return slice(border + count - 1, border + count)
    if shift == -1:
        return slice(border, border + 1)
    return slice(border, border + count)


def halo_pieces(cells):
    _, planes, rows, _ = cells.shape
    return [cells[:, ranges(dz, planes, 0), ranges(dy, rows, 0)] for dz, dy in NEIGHBOURS]


def framed(cells, received):
    got = dict(zip(NEIGHBOURS, received))
    lines = []
    for dz in (1, 0, -1):
        middle = cells if dz == 0 else got[(dz, 0)]
        lines.append(jnp.concatenate([got[(dz, 1)], middle, got[(dz, -1)]], axis=2))
    return jnp.concatenate(lines, axis=1)


def conv_taps(columns, weight, shape):
    _, planes, rows, _ = shape
    total = jnp.zeros(shape, jnp.float32)
    for tap_z in range(3):
        for tap_y in range(3):
            window = columns[:, tap_z : tap_z + planes, tap_y : tap_y + rows]
            total = total + jnp.einsum(
                "oj,jzyx->ozyx", weight[tap_z, tap_y], window, preferred_element_type=jnp.float32
            )
    return total


def transposed_weight(conv_weight):
    taps_z, taps_y, channels, width = conv_weight.shape
    split = conv_weight.reshape(taps_z, taps_y, channels, width // channels, channels)
    split = split[::-1, ::-1, :, ::-1, :]
    return jnp.transpose(split, (0, 1, 4, 3, 2)).reshape(taps_z, taps_y, channels, width)


def border_pieces(spread):
    _, planes, rows, _ = spread.shape
    planes, rows = planes - 2, rows - 2
    pieces = []
    for dz, dy in NEIGHBOURS:
        zs = slice(planes + 1, planes + 2) if dz == 1 else slice(0, 1) if dz == -1 else slice(1, planes + 1)
        ys = slice(rows + 1, rows + 2) if dy == 1 else slice(0, 1) if dy == -1 else slice(1, rows + 1)
        pieces.append(spread[:, zs, ys].astype(jnp.bfloat16))
    return pieces


def folded_grad(spread, got):
    _, planes, rows, _ = spread.shape
    planes, rows = planes - 2, rows - 2
    own = spread[:, 1 : planes + 1, 1 : rows + 1]
    for (dz, dy), piece in zip(NEIGHBOURS, got):
        own = own.at[:, ranges(-dz, planes, 0), ranges(-dy, rows, 0)].add(piece.astype(own.dtype))
    return own


def mesh_bits():
    sizes = {"gz": lax.axis_size("gz"), "gy": lax.axis_size("gy")}
    orders = [[pair[c] for pair in BIT_ORDER if (1 << pair[c][1]) < sizes[pair[c][0]]] for c in (0, 1)]
    return list(zip(*orders))


def allreduce_kernel(bits, halvings, offsets, x_ref, *refs):
    count = len(offsets)
    pieces, o_ref = refs[:count], refs[count]
    landed = refs[count + 1 : 2 * count + 1]
    scratch = refs[2 * count + 1 :]
    halve_bufs = scratch[:halvings]
    work, double_buf, send_sems, recv_sems, halo_send, halo_recv = scratch[halvings:]
    here = {"gz": lax.axis_index("gz"), "gy": lax.axis_index("gy")}
    sizes = {"gz": lax.axis_size("gz"), "gy": lax.axis_size("gy")}

    def neighbour(dz, dy):
        return ((here["gz"] + dz + sizes["gz"]) % sizes["gz"], (here["gy"] + dy + sizes["gy"]) % sizes["gy"])

    core = here["gy"] % 2

    def pick(pair):
        (axis0, b0), (axis1, b1) = pair
        a0, a1 = int(axis0 == "gy"), int(axis1 == "gy")
        return a0 + (a1 - a0) * core, (1 << b0) + ((1 << b1) - (1 << b0)) * core

    def bit_of(pair):
        which, weight = pick(pair)
        value = here["gz"] + (here["gy"] - here["gz"]) * which
        return (value // weight) % 2

    def partner(*pairs):
        device = [here["gz"], here["gy"]]
        for pair in pairs:
            which, weight = pick(pair)
            step = (1 - 2 * bit_of(pair)) * weight
            device = [device[0] + step * (1 - which), device[1] + step * which]
        return tuple(device)

    groups = [bits[i : i + 2] for i in range(halvings, len(bits), 2)]
    reach = [(pair,) for pair in bits] + [tuple(g) for g in groups if len(g) == 2]

    barrier = pltpu.get_barrier_semaphore()
    for pairs in reach:
        pl.semaphore_signal(barrier, inc=1, device_id=partner(*pairs), device_id_type=MESH_ID)
    for dz, dy in offsets:
        pl.semaphore_signal(barrier, inc=1, device_id=neighbour(dz, dy), device_id_type=MESH_ID)
    pl.semaphore_wait(barrier, len(reach) + count)
    halo = []
    for i, (dz, dy) in enumerate(offsets):
        copy = pltpu.make_async_remote_copy(
            src_ref=pieces[i],
            dst_ref=landed[i],
            send_sem=halo_send.at[i],
            recv_sem=halo_recv.at[i],
            device_id=neighbour(dz, dy),
            device_id_type=MESH_ID,
        )
        copy.start()
        halo.append(copy)

    def exchange(step, pair, src, dst):
        start_copy(step, (pair,), src, dst).wait()

    def start_copy(step, pairs, src, dst):
        copy = pltpu.make_async_remote_copy(
            src_ref=src,
            dst_ref=dst,
            send_sem=send_sems.at[step],
            recv_sem=recv_sems.at[step],
            device_id=partner(*pairs),
            device_id_type=MESH_ID,
        )
        copy.start()
        return copy

    lo, length, step = 0, o_ref.shape[0], 0
    for k in range(halvings):
        pair = bits[k]
        half = length // 2
        bit = bit_of(pair)
        keep = pl.multiple_of(lo + bit * half, 8)
        give = pl.multiple_of(lo + (1 - bit) * half, 8)
        source = x_ref if k == 0 else work
        exchange(step, pair, source.at[pl.ds(give, half)], halve_bufs[k])
        work[pl.ds(keep, half)] = source[pl.ds(keep, half)] + halve_bufs[k][...]
        lo, length, step = keep, half, step + 1
    slot = 0
    for group in groups:
        own = work.at[pl.ds(lo, length)]
        if len(group) == 1:
            exchange(step, group[0], own, double_buf.at[slot])
            work[pl.ds(lo, length)] = own[...] + double_buf[slot]
            slot, step = slot + 1, step + 1
            continue
        flips = [(group[0],), (group[1],), (group[0], group[1])]
        copies = [start_copy(step + m, f, own, double_buf.at[slot + m]) for m, f in enumerate(flips)]
        for copy in copies:
            copy.wait()
        near, far = double_buf[slot] + own[...], double_buf[slot + 1] + double_buf[slot + 2]
        work[pl.ds(lo, length)] = near + far
        slot, step = slot + 3, step + 3
    o_ref[pl.ds(lo, length)] = work[pl.ds(lo, length)]
    for k in reversed(range(halvings)):
        pair = bits[k]
        region = o_ref.at[pl.ds(lo, length)]
        exchange(step, pair, region, region)
        lo = pl.multiple_of(lo - bit_of(pair) * length, 8)
        length, step = length * 2, step + 1
    for copy in halo:
        copy.wait()


def allreduce(flat, pieces=(), halvings=HALVINGS):
    offsets = NEIGHBOURS[: len(pieces)]
    pieces = [p.reshape(-1, 128) for p in pieces]
    bits = mesh_bits()
    halvings = min(halvings, len(bits))
    rows = flat.shape[0]
    segment = rows >> halvings
    far = len(bits) - halvings
    slots = 3 * (far // 2) + far % 2
    steps = 2 * halvings + slots
    scratch = [pltpu.VMEM((rows >> (k + 1), 128), jnp.float32) for k in range(halvings)]
    scratch += [
        pltpu.VMEM(flat.shape, jnp.float32),
        pltpu.VMEM((max(slots, 1), segment, 128), jnp.float32),
        pltpu.SemaphoreType.DMA((steps,)),
        pltpu.SemaphoreType.DMA((steps,)),
        pltpu.SemaphoreType.DMA((max(len(pieces), 1),)),
        pltpu.SemaphoreType.DMA((max(len(pieces), 1),)),
    ]
    vmem = pl.BlockSpec(memory_space=pltpu.VMEM)
    outs = pl.pallas_call(
        functools.partial(allreduce_kernel, bits, halvings, offsets),
        out_shape=[jax.ShapeDtypeStruct(flat.shape, jnp.float32)]
        + [jax.ShapeDtypeStruct(p.shape, p.dtype) for p in pieces],
        in_specs=[vmem] * (1 + len(pieces)),
        out_specs=[vmem] * (1 + len(pieces)),
        scratch_shapes=scratch,
        compiler_params=pltpu.CompilerParams(collective_id=0, has_side_effects=True),
    )(flat, *pieces)
    return outs[0], outs[1:]


def summed_gradients(local_conv, local_down, pieces, scale):
    sizes = (local_conv.size, local_down.size)
    flat = jnp.concatenate([local_conv.reshape(-1), local_down.reshape(-1)]) * scale
    unit = 128 * 8 << HALVINGS
    padded = -(-flat.size // unit) * unit
    flat = jnp.pad(flat, (0, padded - flat.size)).reshape(-1, 128)
    total, got = allreduce(flat, [as_rows(p) for p in pieces])
    total = total.reshape(-1)
    return (
        total[: sizes[0]].reshape(local_conv.shape),
        total[sizes[0] : sizes[0] + sizes[1]].reshape(local_down.shape),
        [from_rows(g, p.shape) for g, p in zip(got, pieces)],
    )


def body(features, conv_weight, down_weight, cotangent):
    channels, plane_count, row_count, breadth = features.shape
    out_channels = down_weight.shape[2]
    cell_count = plane_count * row_count * breadth * lax.axis_size("gz") * lax.axis_size("gy")
    grad_scale = 1.0 / math.sqrt(cell_count)
    columns = widen(framed(features, halo_swap(halo_pieces(features), 1)))
    preact = conv_taps(columns, conv_weight, features.shape)
    hidden = jax.nn.silu(preact).astype(jnp.bfloat16)
    blocks = hidden.reshape(channels, plane_count // 2, 2, row_count // 2, 2, breadth // 2, 2)
    down_split = down_weight.reshape(2, 2, out_channels, 2, channels)
    coarse = jnp.einsum(
        "aboei,iZaYbXe->oZYX", down_split, blocks, preferred_element_type=jnp.float32
    )
    section_out = coarse.reshape(out_channels, plane_count // 2, -1).astype(jnp.bfloat16)
    coarse_cot = cotangent.reshape(out_channels, plane_count // 2, row_count // 2, breadth // 2)
    hidden_grad = jnp.einsum(
        "aboei,oZYX->iZaYbXe", down_split, coarse_cot, preferred_element_type=jnp.float32
    )
    hidden_grad = hidden_grad.reshape(channels, plane_count, row_count, breadth)
    local_down = jnp.einsum(
        "oZYX,iZaYbXe->aboei", coarse_cot, blocks, preferred_element_type=jnp.float32
    )
    local_down = local_down.reshape(2, 2, out_channels, 2 * channels)
    gate_sig = jax.nn.sigmoid(preact)
    gate_grad = (hidden_grad * gate_sig * (1.0 + preact * (1.0 - gate_sig))).astype(jnp.bfloat16)
    kernel_rows = []
    for tap_z in range(3):
        row_list = []
        for tap_y in range(3):
            window = columns[:, tap_z : tap_z + plane_count, tap_y : tap_y + row_count]
            row_list.append(
                jnp.einsum("ozyx,jzyx->oj", gate_grad, window, preferred_element_type=jnp.float32)
            )
        kernel_rows.append(jnp.stack(row_list, axis=0))
    local_conv = jnp.stack(kernel_rows, axis=0)
    summed_conv, summed_down, got = summed_gradients(local_conv, local_down, halo_pieces(gate_grad), grad_scale)
    gate_columns = widen(framed(gate_grad, got))
    grad_field = conv_taps(gate_columns, transposed_weight(conv_weight), features.shape)
    return (section_out, grad_field, summed_conv, summed_down)


def solution(mesh):
    return jax.shard_map(
        body,
        mesh=mesh,
        in_specs=(P(None, "gz", "gy", None), P(), P(), P(None, "gz", "gy")),
        out_specs=(P(None, "gz", "gy"), P(None, "gz", "gy", None), P(), P()),
        check_vma=False,
    )
```

```python
import functools
import math

import jax
import jax.numpy as jnp
from jax import lax
from jax.experimental import pallas as pl
from jax.experimental.pallas import tpu as pltpu
from jax.sharding import PartitionSpec as P

MESH_ID = pl.DeviceIdType.MESH
BIT_ORDER = (
    (("gy", 0), ("gy", 0)),
    (("gy", 1), ("gz", 0)),
    (("gz", 0), ("gz", 3)),
    (("gz", 3), ("gy", 1)),
    (("gy", 2), ("gz", 1)),
    (("gz", 1), ("gy", 2)),
    (("gz", 4), ("gz", 2)),
    (("gz", 2), ("gz", 4)),
    (("gy", 3), ("gy", 3)),
)
HALVINGS = 4


def extended(cells, sides, width):
    for axis, dim in sides:
        count = lax.axis_size(axis)
        head = lax.slice_in_dim(cells, 0, width, axis=dim)
        tail = lax.slice_in_dim(cells, cells.shape[dim] - width, cells.shape[dim], axis=dim)
        cells = jnp.concatenate(
            [
                lax.ppermute(tail, axis, [(i, (i + 1) % count) for i in range(count)]),
                cells,
                lax.ppermute(head, axis, [((i + 1) % count, i) for i in range(count)]),
            ],
            axis=dim,
        )
    return cells


def widen(framed):
    return jnp.concatenate([jnp.roll(framed, 1 - tap_x, axis=3) for tap_x in range(3)], axis=0)


def fold_along(spread, channels):
    result = jnp.roll(spread[0:channels], -1, axis=3)
    result = result + spread[channels : 2 * channels]
    result = result + jnp.roll(spread[2 * channels : 3 * channels], 1, axis=3)
    return result


NEIGHBOURS = ((1, 0), (-1, 0), (0, 1), (0, -1), (1, 1), (1, -1), (-1, 1), (-1, -1))


def halo_kernel(offsets, *refs):
    count = len(offsets)
    sources, targets = refs[:count], refs[count : 2 * count]
    send_sems, recv_sems = refs[2 * count :]
    sizes = (lax.axis_size("gz"), lax.axis_size("gy"))
    here = (lax.axis_index("gz"), lax.axis_index("gy"))

    def device(dz, dy):
        return ((here[0] + dz + sizes[0]) % sizes[0], (here[1] + dy + sizes[1]) % sizes[1])

    barrier = pltpu.get_barrier_semaphore()
    for dz, dy in offsets:
        pl.semaphore_signal(barrier, inc=1, device_id=device(dz, dy), device_id_type=MESH_ID)
    pl.semaphore_wait(barrier, count)
    copies = []
    for i, (dz, dy) in enumerate(offsets):
        copy = pltpu.make_async_remote_copy(
            src_ref=sources[i],
            dst_ref=targets[i],
            send_sem=send_sems.at[i],
            recv_sem=recv_sems.at[i],
            device_id=device(dz, dy),
            device_id_type=MESH_ID,
        )
        copy.start()
        copies.append(copy)
    for copy in copies:
        copy.wait()


def halo_swap(pieces, collective_id):
    flat = [as_rows(p) for p in pieces]
    vmem = pl.BlockSpec(memory_space=pltpu.VMEM)
    got = pl.pallas_call(
        functools.partial(halo_kernel, NEIGHBOURS),
        out_shape=[jax.ShapeDtypeStruct(f.shape, f.dtype) for f in flat],
        in_specs=[vmem] * len(flat),
        out_specs=[vmem] * len(flat),
        scratch_shapes=[pltpu.SemaphoreType.DMA((len(flat),)), pltpu.SemaphoreType.DMA((len(flat),))],
        compiler_params=pltpu.CompilerParams(collective_id=collective_id, has_side_effects=True),
    )(*flat)
    return [from_rows(g, p.shape) for g, p in zip(got, pieces)]


def as_rows(piece):
    return jnp.transpose(piece, (1, 2, 0, 3)).reshape(-1, piece.shape[3])


def from_rows(rows, shape):
    channels, planes, lines, breadth = shape
    return jnp.transpose(rows.reshape(planes, lines, channels, breadth), (2, 0, 1, 3))


def ranges(shift, count, border):
    if shift == 1:
        return slice(border + count - 1, border + count)
    if shift == -1:
        return slice(border, border + 1)
    return slice(border, border + count)


def halo_pieces(cells):
    _, planes, rows, _ = cells.shape
    return [cells[:, ranges(dz, planes, 0), ranges(dy, rows, 0)] for dz, dy in NEIGHBOURS]


def framed(cells, received):
    got = dict(zip(NEIGHBOURS, received))
    lines = []
    for dz in (1, 0, -1):
        middle = cells if dz == 0 else got[(dz, 0)]
        lines.append(jnp.concatenate([got[(dz, 1)], middle, got[(dz, -1)]], axis=2))
    return jnp.concatenate(lines, axis=1)


def conv_taps(columns, weight, shape):
    _, planes, rows, _ = shape
    total = jnp.zeros(shape, jnp.float32)
    for tap_z in range(3):
        for tap_y in range(3):
            window = columns[:, tap_z : tap_z + planes, tap_y : tap_y + rows]
            total = total + jnp.einsum(
                "oj,jzyx->ozyx", weight[tap_z, tap_y], window, preferred_element_type=jnp.float32
            )
    return total


def transposed_weight(conv_weight):
    taps_z, taps_y, channels, width = conv_weight.shape
    split = conv_weight.reshape(taps_z, taps_y, channels, width // channels, channels)
    split = split[::-1, ::-1, :, ::-1, :]
    return jnp.transpose(split, (0, 1, 4, 3, 2)).reshape(taps_z, taps_y, channels, width)


def border_pieces(spread):
    _, planes, rows, _ = spread.shape
    planes, rows = planes - 2, rows - 2
    pieces = []
    for dz, dy in NEIGHBOURS:
        zs = slice(planes + 1, planes + 2) if dz == 1 else slice(0, 1) if dz == -1 else slice(1, planes + 1)
        ys = slice(rows + 1, rows + 2) if dy == 1 else slice(0, 1) if dy == -1 else slice(1, rows + 1)
        pieces.append(spread[:, zs, ys].astype(jnp.bfloat16))
    return pieces


def folded_grad(spread, got):
    _, planes, rows, _ = spread.shape
    planes, rows = planes - 2, rows - 2
    own = spread[:, 1 : planes + 1, 1 : rows + 1]
    for (dz, dy), piece in zip(NEIGHBOURS, got):
        own = own.at[:, ranges(-dz, planes, 0), ranges(-dy, rows, 0)].add(piece.astype(own.dtype))
    return own


def mesh_bits():
    sizes = {"gz": lax.axis_size("gz"), "gy": lax.axis_size("gy")}
    orders = [[pair[c] for pair in BIT_ORDER if (1 << pair[c][1]) < sizes[pair[c][0]]] for c in (0, 1)]
    return list(zip(*orders))


def allreduce_kernel(bits, halvings, offsets, x_ref, *refs):
    count = len(offsets)
    pieces, o_ref = refs[:count], refs[count]
    landed = refs[count + 1 : 2 * count + 1]
    scratch = refs[2 * count + 1 :]
    halve_bufs = scratch[:halvings]
    work, double_buf, send_sems, recv_sems, halo_send, halo_recv = scratch[halvings:]
    here = {"gz": lax.axis_index("gz"), "gy": lax.axis_index("gy")}
    sizes = {"gz": lax.axis_size("gz"), "gy": lax.axis_size("gy")}

    def neighbour(dz, dy):
        return ((here["gz"] + dz + sizes["gz"]) % sizes["gz"], (here["gy"] + dy + sizes["gy"]) % sizes["gy"])

    core = here["gy"] % 2

    def pick(pair):
        (axis0, b0), (axis1, b1) = pair
        a0, a1 = int(axis0 == "gy"), int(axis1 == "gy")
        return a0 + (a1 - a0) * core, (1 << b0) + ((1 << b1) - (1 << b0)) * core

    def bit_of(pair):
        which, weight = pick(pair)
        value = here["gz"] + (here["gy"] - here["gz"]) * which
        return (value // weight) % 2

    def partner(*pairs):
        device = [here["gz"], here["gy"]]
        for pair in pairs:
            which, weight = pick(pair)
            step = (1 - 2 * bit_of(pair)) * weight
            device = [device[0] + step * (1 - which), device[1] + step * which]
        return tuple(device)

    groups = [bits[i : i + 2] for i in range(halvings, len(bits), 2)]
    reach = [(pair,) for pair in bits] + [tuple(g) for g in groups if len(g) == 2]

    barrier = pltpu.get_barrier_semaphore()
    for pairs in reach:
        pl.semaphore_signal(barrier, inc=1, device_id=partner(*pairs), device_id_type=MESH_ID)
    for dz, dy in offsets:
        pl.semaphore_signal(barrier, inc=1, device_id=neighbour(dz, dy), device_id_type=MESH_ID)
    pl.semaphore_wait(barrier, len(reach) + count)

    def exchange(step, pair, src, dst):
        start_copy(step, (pair,), src, dst).wait()

    def start_copy(step, pairs, src, dst):
        copy = pltpu.make_async_remote_copy(
            src_ref=src,
            dst_ref=dst,
            send_sem=send_sems.at[step],
            recv_sem=recv_sems.at[step],
            device_id=partner(*pairs),
            device_id_type=MESH_ID,
        )
        copy.start()
        return copy

    lo, length, step = 0, o_ref.shape[0], 0
    for k in range(halvings):
        pair = bits[k]
        half = length // 2
        bit = bit_of(pair)
        keep = pl.multiple_of(lo + bit * half, 8)
        give = pl.multiple_of(lo + (1 - bit) * half, 8)
        source = x_ref if k == 0 else work
        exchange(step, pair, source.at[pl.ds(give, half)], halve_bufs[k])
        work[pl.ds(keep, half)] = source[pl.ds(keep, half)] + halve_bufs[k][...]
        lo, length, step = keep, half, step + 1
    halo = []
    for i, (dz, dy) in enumerate(offsets):
        copy = pltpu.make_async_remote_copy(
            src_ref=pieces[i],
            dst_ref=landed[i],
            send_sem=halo_send.at[i],
            recv_sem=halo_recv.at[i],
            device_id=neighbour(dz, dy),
            device_id_type=MESH_ID,
        )
        copy.start()
        halo.append(copy)
    slot = 0
    for group in groups:
        own = work.at[pl.ds(lo, length)]
        if len(group) == 1:
            exchange(step, group[0], own, double_buf.at[slot])
            work[pl.ds(lo, length)] = own[...] + double_buf[slot]
            slot, step = slot + 1, step + 1
            continue
        flips = [(group[0],), (group[1],), (group[0], group[1])]
        copies = [start_copy(step + m, f, own, double_buf.at[slot + m]) for m, f in enumerate(flips)]
        for copy in copies:
            copy.wait()
        near, far = double_buf[slot] + own[...], double_buf[slot + 1] + double_buf[slot + 2]
        work[pl.ds(lo, length)] = near + far
        slot, step = slot + 3, step + 3
    o_ref[pl.ds(lo, length)] = work[pl.ds(lo, length)]
    for k in reversed(range(halvings)):
        pair = bits[k]
        region = o_ref.at[pl.ds(lo, length)]
        exchange(step, pair, region, region)
        lo = pl.multiple_of(lo - bit_of(pair) * length, 8)
        length, step = length * 2, step + 1
    for copy in halo:
        copy.wait()


def allreduce(flat, pieces=(), halvings=HALVINGS):
    offsets = NEIGHBOURS[: len(pieces)]
    pieces = [p.reshape(-1, 128) for p in pieces]
    bits = mesh_bits()
    halvings = min(halvings, len(bits))
    rows = flat.shape[0]
    segment = rows >> halvings
    far = len(bits) - halvings
    slots = 3 * (far // 2) + far % 2
    steps = 2 * halvings + slots
    scratch = [pltpu.VMEM((rows >> (k + 1), 128), jnp.float32) for k in range(halvings)]
    scratch += [
        pltpu.VMEM(flat.shape, jnp.float32),
        pltpu.VMEM((max(slots, 1), segment, 128), jnp.float32),
        pltpu.SemaphoreType.DMA((steps,)),
        pltpu.SemaphoreType.DMA((steps,)),
        pltpu.SemaphoreType.DMA((max(len(pieces), 1),)),
        pltpu.SemaphoreType.DMA((max(len(pieces), 1),)),
    ]
    vmem = pl.BlockSpec(memory_space=pltpu.VMEM)
    outs = pl.pallas_call(
        functools.partial(allreduce_kernel, bits, halvings, offsets),
        out_shape=[jax.ShapeDtypeStruct(flat.shape, jnp.float32)]
        + [jax.ShapeDtypeStruct(p.shape, p.dtype) for p in pieces],
        in_specs=[vmem] * (1 + len(pieces)),
        out_specs=[vmem] * (1 + len(pieces)),
        scratch_shapes=scratch,
        compiler_params=pltpu.CompilerParams(collective_id=0, has_side_effects=True),
    )(flat, *pieces)
    return outs[0], outs[1:]


def summed_gradients(local_conv, local_down, pieces, scale):
    sizes = (local_conv.size, local_down.size)
    flat = jnp.concatenate([local_conv.reshape(-1), local_down.reshape(-1)]) * scale
    unit = 128 * 8 << HALVINGS
    padded = -(-flat.size // unit) * unit
    flat = jnp.pad(flat, (0, padded - flat.size)).reshape(-1, 128)
    total, got = allreduce(flat, [as_rows(p) for p in pieces])
    total = total.reshape(-1)
    return (
        total[: sizes[0]].reshape(local_conv.shape),
        total[sizes[0] : sizes[0] + sizes[1]].reshape(local_down.shape),
        [from_rows(g, p.shape) for g, p in zip(got, pieces)],
    )


def body(features, conv_weight, down_weight, cotangent):
    channels, plane_count, row_count, breadth = features.shape
    out_channels = down_weight.shape[2]
    cell_count = plane_count * row_count * breadth * lax.axis_size("gz") * lax.axis_size("gy")
    grad_scale = 1.0 / math.sqrt(cell_count)
    columns = widen(framed(features, halo_swap(halo_pieces(features), 1)))
    preact = conv_taps(columns, conv_weight, features.shape)
    hidden = jax.nn.silu(preact).astype(jnp.bfloat16)
    blocks = hidden.reshape(channels, plane_count // 2, 2, row_count // 2, 2, breadth // 2, 2)
    down_split = down_weight.reshape(2, 2, out_channels, 2, channels)
    coarse = jnp.einsum(
        "aboei,iZaYbXe->oZYX", down_split, blocks, preferred_element_type=jnp.float32
    )
    section_out = coarse.reshape(out_channels, plane_count // 2, -1).astype(jnp.bfloat16)
    coarse_cot = cotangent.reshape(out_channels, plane_count // 2, row_count // 2, breadth // 2)
    hidden_grad = jnp.einsum(
        "aboei,oZYX->iZaYbXe", down_split, coarse_cot, preferred_element_type=jnp.float32
    )
    hidden_grad = hidden_grad.reshape(channels, plane_count, row_count, breadth)
    local_down = jnp.einsum(
        "oZYX,iZaYbXe->aboei", coarse_cot, blocks, preferred_element_type=jnp.float32
    )
    local_down = local_down.reshape(2, 2, out_channels, 2 * channels)
    gate_sig = jax.nn.sigmoid(preact)
    gate_grad = (hidden_grad * gate_sig * (1.0 + preact * (1.0 - gate_sig))).astype(jnp.bfloat16)
    kernel_rows = []
    for tap_z in range(3):
        row_list = []
        for tap_y in range(3):
            window = columns[:, tap_z : tap_z + plane_count, tap_y : tap_y + row_count]
            row_list.append(
                jnp.einsum("ozyx,jzyx->oj", gate_grad, window, preferred_element_type=jnp.float32)
            )
        kernel_rows.append(jnp.stack(row_list, axis=0))
    local_conv = jnp.stack(kernel_rows, axis=0)
    summed_conv, summed_down, got = summed_gradients(local_conv, local_down, halo_pieces(gate_grad), grad_scale)
    gate_columns = widen(framed(gate_grad, got))
    grad_field = conv_taps(gate_columns, transposed_weight(conv_weight), features.shape)
    return (section_out, grad_field, summed_conv, summed_down)


def solution(mesh):
    return jax.shard_map(
        body,
        mesh=mesh,
        in_specs=(P(None, "gz", "gy", None), P(), P(), P(None, "gz", "gy")),
        out_specs=(P(None, "gz", "gy"), P(None, "gz", "gy", None), P(), P()),
        check_vma=False,
    )
```

```python
import functools
import math

import jax
import jax.numpy as jnp
from jax import lax
from jax.experimental import pallas as pl
from jax.experimental.pallas import tpu as pltpu
from jax.sharding import PartitionSpec as P

MESH_ID = pl.DeviceIdType.MESH
BIT_ORDER = (
    (("gy", 0), ("gy", 0)),
    (("gy", 1), ("gz", 0)),
    (("gz", 0), ("gz", 3)),
    (("gz", 3), ("gy", 1)),
    (("gz", 1), ("gz", 4)),
    (("gz", 2), ("gy", 3)),
    (("gz", 4), ("gz", 1)),
    (("gy", 3), ("gz", 2)),
    (("gy", 2), ("gy", 2)),
)
HALVINGS = 4


def extended(cells, sides, width):
    for axis, dim in sides:
        count = lax.axis_size(axis)
        head = lax.slice_in_dim(cells, 0, width, axis=dim)
        tail = lax.slice_in_dim(cells, cells.shape[dim] - width, cells.shape[dim], axis=dim)
        cells = jnp.concatenate(
            [
                lax.ppermute(tail, axis, [(i, (i + 1) % count) for i in range(count)]),
                cells,
                lax.ppermute(head, axis, [((i + 1) % count, i) for i in range(count)]),
            ],
            axis=dim,
        )
    return cells


def widen(framed):
    return jnp.concatenate([jnp.roll(framed, 1 - tap_x, axis=3) for tap_x in range(3)], axis=0)


def fold_along(spread, channels):
    result = jnp.roll(spread[0:channels], -1, axis=3)
    result = result + spread[channels : 2 * channels]
    result = result + jnp.roll(spread[2 * channels : 3 * channels], 1, axis=3)
    return result


NEIGHBOURS = ((1, 0), (-1, 0), (0, 1), (0, -1), (1, 1), (1, -1), (-1, 1), (-1, -1))


def halo_kernel(offsets, *refs):
    count = len(offsets)
    sources, targets = refs[:count], refs[count : 2 * count]
    send_sems, recv_sems = refs[2 * count :]
    sizes = (lax.axis_size("gz"), lax.axis_size("gy"))
    here = (lax.axis_index("gz"), lax.axis_index("gy"))

    def device(dz, dy):
        return ((here[0] + dz + sizes[0]) % sizes[0], (here[1] + dy + sizes[1]) % sizes[1])

    barrier = pltpu.get_barrier_semaphore()
    for dz, dy in offsets:
        pl.semaphore_signal(barrier, inc=1, device_id=device(dz, dy), device_id_type=MESH_ID)
    pl.semaphore_wait(barrier, count)
    copies = []
    for i, (dz, dy) in enumerate(offsets):
        copy = pltpu.make_async_remote_copy(
            src_ref=sources[i],
            dst_ref=targets[i],
            send_sem=send_sems.at[i],
            recv_sem=recv_sems.at[i],
            device_id=device(dz, dy),
            device_id_type=MESH_ID,
        )
        copy.start()
        copies.append(copy)
    for copy in copies:
        copy.wait()


def halo_swap(pieces, collective_id):
    flat = [as_rows(p) for p in pieces]
    vmem = pl.BlockSpec(memory_space=pltpu.VMEM)
    got = pl.pallas_call(
        functools.partial(halo_kernel, NEIGHBOURS),
        out_shape=[jax.ShapeDtypeStruct(f.shape, f.dtype) for f in flat],
        in_specs=[vmem] * len(flat),
        out_specs=[vmem] * len(flat),
        scratch_shapes=[pltpu.SemaphoreType.DMA((len(flat),)), pltpu.SemaphoreType.DMA((len(flat),))],
        compiler_params=pltpu.CompilerParams(collective_id=collective_id, has_side_effects=True),
    )(*flat)
    return [from_rows(g, p.shape) for g, p in zip(got, pieces)]


def as_rows(piece):
    return jnp.transpose(piece, (1, 2, 0, 3)).reshape(-1, piece.shape[3])


def from_rows(rows, shape):
    channels, planes, lines, breadth = shape
    return jnp.transpose(rows.reshape(planes, lines, channels, breadth), (2, 0, 1, 3))


def ranges(shift, count, border):
    if shift == 1:
        return slice(border + count - 1, border + count)
    if shift == -1:
        return slice(border, border + 1)
    return slice(border, border + count)


def halo_pieces(cells):
    _, planes, rows, _ = cells.shape
    return [cells[:, ranges(dz, planes, 0), ranges(dy, rows, 0)] for dz, dy in NEIGHBOURS]


def framed(cells, received):
    got = dict(zip(NEIGHBOURS, received))
    lines = []
    for dz in (1, 0, -1):
        middle = cells if dz == 0 else got[(dz, 0)]
        lines.append(jnp.concatenate([got[(dz, 1)], middle, got[(dz, -1)]], axis=2))
    return jnp.concatenate(lines, axis=1)


def conv_taps(columns, weight, shape):
    _, planes, rows, _ = shape
    total = jnp.zeros(shape, jnp.float32)
    for tap_z in range(3):
        for tap_y in range(3):
            window = columns[:, tap_z : tap_z + planes, tap_y : tap_y + rows]
            total = total + jnp.einsum(
                "oj,jzyx->ozyx", weight[tap_z, tap_y], window, preferred_element_type=jnp.float32
            )
    return total


def transposed_weight(conv_weight):
    taps_z, taps_y, channels, width = conv_weight.shape
    split = conv_weight.reshape(taps_z, taps_y, channels, width // channels, channels)
    split = split[::-1, ::-1, :, ::-1, :]
    return jnp.transpose(split, (0, 1, 4, 3, 2)).reshape(taps_z, taps_y, channels, width)


def border_pieces(spread):
    _, planes, rows, _ = spread.shape
    planes, rows = planes - 2, rows - 2
    pieces = []
    for dz, dy in NEIGHBOURS:
        zs = slice(planes + 1, planes + 2) if dz == 1 else slice(0, 1) if dz == -1 else slice(1, planes + 1)
        ys = slice(rows + 1, rows + 2) if dy == 1 else slice(0, 1) if dy == -1 else slice(1, rows + 1)
        pieces.append(spread[:, zs, ys].astype(jnp.bfloat16))
    return pieces


def folded_grad(spread, got):
    _, planes, rows, _ = spread.shape
    planes, rows = planes - 2, rows - 2
    own = spread[:, 1 : planes + 1, 1 : rows + 1]
    for (dz, dy), piece in zip(NEIGHBOURS, got):
        own = own.at[:, ranges(-dz, planes, 0), ranges(-dy, rows, 0)].add(piece.astype(own.dtype))
    return own


def mesh_bits():
    sizes = {"gz": lax.axis_size("gz"), "gy": lax.axis_size("gy")}
    orders = [[pair[c] for pair in BIT_ORDER if (1 << pair[c][1]) < sizes[pair[c][0]]] for c in (0, 1)]
    return list(zip(*orders))


def allreduce_kernel(bits, halvings, offsets, x_ref, *refs):
    count = len(offsets)
    pieces, o_ref = refs[:count], refs[count]
    landed = refs[count + 1 : 2 * count + 1]
    scratch = refs[2 * count + 1 :]
    halve_bufs = scratch[:halvings]
    work, double_buf, send_sems, recv_sems, halo_send, halo_recv = scratch[halvings:]
    here = {"gz": lax.axis_index("gz"), "gy": lax.axis_index("gy")}
    sizes = {"gz": lax.axis_size("gz"), "gy": lax.axis_size("gy")}

    def neighbour(dz, dy):
        return ((here["gz"] + dz + sizes["gz"]) % sizes["gz"], (here["gy"] + dy + sizes["gy"]) % sizes["gy"])

    core = here["gy"] % 2

    def pick(pair):
        (axis0, b0), (axis1, b1) = pair
        a0, a1 = int(axis0 == "gy"), int(axis1 == "gy")
        return a0 + (a1 - a0) * core, (1 << b0) + ((1 << b1) - (1 << b0)) * core

    def bit_of(pair):
        which, weight = pick(pair)
        value = here["gz"] + (here["gy"] - here["gz"]) * which
        return (value // weight) % 2

    def partner(*pairs):
        device = [here["gz"], here["gy"]]
        for pair in pairs:
            which, weight = pick(pair)
            step = (1 - 2 * bit_of(pair)) * weight
            device = [device[0] + step * (1 - which), device[1] + step * which]
        return tuple(device)

    groups = [bits[i : i + 2] for i in range(halvings, len(bits), 2)]
    reach = [(pair,) for pair in bits] + [tuple(g) for g in groups if len(g) == 2]

    barrier = pltpu.get_barrier_semaphore()
    for pairs in reach:
        pl.semaphore_signal(barrier, inc=1, device_id=partner(*pairs), device_id_type=MESH_ID)
    for dz, dy in offsets:
        pl.semaphore_signal(barrier, inc=1, device_id=neighbour(dz, dy), device_id_type=MESH_ID)
    pl.semaphore_wait(barrier, len(reach) + count)
    halo = []
    for i, (dz, dy) in enumerate(offsets):
        copy = pltpu.make_async_remote_copy(
            src_ref=pieces[i],
            dst_ref=landed[i],
            send_sem=halo_send.at[i],
            recv_sem=halo_recv.at[i],
            device_id=neighbour(dz, dy),
            device_id_type=MESH_ID,
        )
        copy.start()
        halo.append(copy)

    def exchange(step, pair, src, dst):
        start_copy(step, (pair,), src, dst).wait()

    def start_copy(step, pairs, src, dst):
        copy = pltpu.make_async_remote_copy(
            src_ref=src,
            dst_ref=dst,
            send_sem=send_sems.at[step],
            recv_sem=recv_sems.at[step],
            device_id=partner(*pairs),
            device_id_type=MESH_ID,
        )
        copy.start()
        return copy

    lo, length, step = 0, o_ref.shape[0], 0
    for k in range(halvings):
        pair = bits[k]
        half = length // 2
        bit = bit_of(pair)
        keep = pl.multiple_of(lo + bit * half, 8)
        give = pl.multiple_of(lo + (1 - bit) * half, 8)
        source = x_ref if k == 0 else work
        exchange(step, pair, source.at[pl.ds(give, half)], halve_bufs[k])
        work[pl.ds(keep, half)] = source[pl.ds(keep, half)] + halve_bufs[k][...]
        lo, length, step = keep, half, step + 1
    slot = 0
    for group in groups:
        own = work.at[pl.ds(lo, length)]
        if len(group) == 1:
            exchange(step, group[0], own, double_buf.at[slot])
            work[pl.ds(lo, length)] = own[...] + double_buf[slot]
            slot, step = slot + 1, step + 1
            continue
        flips = [(group[0],), (group[1],), (group[0], group[1])]
        copies = [start_copy(step + m, f, own, double_buf.at[slot + m]) for m, f in enumerate(flips)]
        for copy in copies:
            copy.wait()
        near, far = double_buf[slot] + own[...], double_buf[slot + 1] + double_buf[slot + 2]
        work[pl.ds(lo, length)] = near + far
        slot, step = slot + 3, step + 3
    o_ref[pl.ds(lo, length)] = work[pl.ds(lo, length)]
    for k in reversed(range(halvings)):
        pair = bits[k]
        region = o_ref.at[pl.ds(lo, length)]
        exchange(step, pair, region, region)
        lo = pl.multiple_of(lo - bit_of(pair) * length, 8)
        length, step = length * 2, step + 1
    for copy in halo:
        copy.wait()


def allreduce(flat, pieces=(), halvings=HALVINGS):
    offsets = NEIGHBOURS[: len(pieces)]
    pieces = [p.reshape(-1, 128) for p in pieces]
    bits = mesh_bits()
    halvings = min(halvings, len(bits))
    rows = flat.shape[0]
    segment = rows >> halvings
    far = len(bits) - halvings
    slots = 3 * (far // 2) + far % 2
    steps = 2 * halvings + slots
    scratch = [pltpu.VMEM((rows >> (k + 1), 128), jnp.float32) for k in range(halvings)]
    scratch += [
        pltpu.VMEM(flat.shape, jnp.float32),
        pltpu.VMEM((max(slots, 1), segment, 128), jnp.float32),
        pltpu.SemaphoreType.DMA((steps,)),
        pltpu.SemaphoreType.DMA((steps,)),
        pltpu.SemaphoreType.DMA((max(len(pieces), 1),)),
        pltpu.SemaphoreType.DMA((max(len(pieces), 1),)),
    ]
    vmem = pl.BlockSpec(memory_space=pltpu.VMEM)
    outs = pl.pallas_call(
        functools.partial(allreduce_kernel, bits, halvings, offsets),
        out_shape=[jax.ShapeDtypeStruct(flat.shape, jnp.float32)]
        + [jax.ShapeDtypeStruct(p.shape, p.dtype) for p in pieces],
        in_specs=[vmem] * (1 + len(pieces)),
        out_specs=[vmem] * (1 + len(pieces)),
        scratch_shapes=scratch,
        compiler_params=pltpu.CompilerParams(collective_id=0, has_side_effects=True),
    )(flat, *pieces)
    return outs[0], outs[1:]


def summed_gradients(local_conv, local_down, pieces, scale):
    sizes = (local_conv.size, local_down.size)
    flat = jnp.concatenate([local_conv.reshape(-1), local_down.reshape(-1)]) * scale
    unit = 128 * 8 << HALVINGS
    padded = -(-flat.size // unit) * unit
    flat = jnp.pad(flat, (0, padded - flat.size)).reshape(-1, 128)
    total, got = allreduce(flat, [as_rows(p) for p in pieces])
    total = total.reshape(-1)
    return (
        total[: sizes[0]].reshape(local_conv.shape),
        total[sizes[0] : sizes[0] + sizes[1]].reshape(local_down.shape),
        [from_rows(g, p.shape) for g, p in zip(got, pieces)],
    )


def body(features, conv_weight, down_weight, cotangent):
    channels, plane_count, row_count, breadth = features.shape
    out_channels = down_weight.shape[2]
    cell_count = plane_count * row_count * breadth * lax.axis_size("gz") * lax.axis_size("gy")
    grad_scale = 1.0 / math.sqrt(cell_count)
    columns = widen(framed(features, halo_swap(halo_pieces(features), 1)))
    preact = conv_taps(columns, conv_weight, features.shape)
    hidden = jax.nn.silu(preact).astype(jnp.bfloat16)
    blocks = hidden.reshape(channels, plane_count // 2, 2, row_count // 2, 2, breadth // 2, 2)
    down_split = down_weight.reshape(2, 2, out_channels, 2, channels)
    coarse = jnp.einsum(
        "aboei,iZaYbXe->oZYX", down_split, blocks, preferred_element_type=jnp.float32
    )
    section_out = coarse.reshape(out_channels, plane_count // 2, -1).astype(jnp.bfloat16)
    coarse_cot = cotangent.reshape(out_channels, plane_count // 2, row_count // 2, breadth // 2)
    hidden_grad = jnp.einsum(
        "aboei,oZYX->iZaYbXe", down_split, coarse_cot, preferred_element_type=jnp.float32
    )
    hidden_grad = hidden_grad.reshape(channels, plane_count, row_count, breadth)
    local_down = jnp.einsum(
        "oZYX,iZaYbXe->aboei", coarse_cot, blocks, preferred_element_type=jnp.float32
    )
    local_down = local_down.reshape(2, 2, out_channels, 2 * channels)
    gate_sig = jax.nn.sigmoid(preact)
    gate_grad = (hidden_grad * gate_sig * (1.0 + preact * (1.0 - gate_sig))).astype(jnp.bfloat16)
    kernel_rows = []
    for tap_z in range(3):
        row_list = []
        for tap_y in range(3):
            window = columns[:, tap_z : tap_z + plane_count, tap_y : tap_y + row_count]
            row_list.append(
                jnp.einsum("ozyx,jzyx->oj", gate_grad, window, preferred_element_type=jnp.float32)
            )
        kernel_rows.append(jnp.stack(row_list, axis=0))
    local_conv = jnp.stack(kernel_rows, axis=0)
    summed_conv, summed_down, got = summed_gradients(local_conv, local_down, halo_pieces(gate_grad), grad_scale)
    gate_columns = widen(framed(gate_grad, got))
    grad_field = conv_taps(gate_columns, transposed_weight(conv_weight), features.shape)
    return (section_out, grad_field, summed_conv, summed_down)


def solution(mesh):
    return jax.shard_map(
        body,
        mesh=mesh,
        in_specs=(P(None, "gz", "gy", None), P(), P(), P(None, "gz", "gy")),
        out_specs=(P(None, "gz", "gy"), P(None, "gz", "gy", None), P(), P()),
        check_vma=False,
    )
```

```python
import functools
import math

import jax
import jax.numpy as jnp
from jax import lax
from jax.experimental import pallas as pl
from jax.experimental.pallas import tpu as pltpu
from jax.sharding import PartitionSpec as P

MESH_ID = pl.DeviceIdType.MESH
BIT_ORDER = (
    (("gy", 0), ("gy", 0)),
    (("gy", 1), ("gz", 0)),
    (("gz", 0), ("gz", 3)),
    (("gz", 3), ("gy", 1)),
    (("gz", 1), ("gz", 4)),
    (("gz", 2), ("gy", 3)),
    (("gz", 4), ("gz", 1)),
    (("gy", 3), ("gz", 2)),
    (("gy", 2), ("gy", 2)),
)
HALVINGS = 4


def extended(cells, sides, width):
    for axis, dim in sides:
        count = lax.axis_size(axis)
        head = lax.slice_in_dim(cells, 0, width, axis=dim)
        tail = lax.slice_in_dim(cells, cells.shape[dim] - width, cells.shape[dim], axis=dim)
        cells = jnp.concatenate(
            [
                lax.ppermute(tail, axis, [(i, (i + 1) % count) for i in range(count)]),
                cells,
                lax.ppermute(head, axis, [((i + 1) % count, i) for i in range(count)]),
            ],
            axis=dim,
        )
    return cells


def widen(framed):
    return jnp.concatenate([jnp.roll(framed, 1 - tap_x, axis=3) for tap_x in range(3)], axis=0)


def fold_along(spread, channels):
    result = jnp.roll(spread[0:channels], -1, axis=3)
    result = result + spread[channels : 2 * channels]
    result = result + jnp.roll(spread[2 * channels : 3 * channels], 1, axis=3)
    return result


NEIGHBOURS = ((1, 0), (-1, 0), (0, 1), (0, -1), (1, 1), (1, -1), (-1, 1), (-1, -1))


def halo_kernel(offsets, *refs):
    count = len(offsets)
    sources, targets = refs[:count], refs[count : 2 * count]
    send_sems, recv_sems = refs[2 * count :]
    sizes = (lax.axis_size("gz"), lax.axis_size("gy"))
    here = (lax.axis_index("gz"), lax.axis_index("gy"))

    def device(dz, dy):
        return ((here[0] + dz + sizes[0]) % sizes[0], (here[1] + dy + sizes[1]) % sizes[1])

    barrier = pltpu.get_barrier_semaphore()
    for dz, dy in offsets:
        pl.semaphore_signal(barrier, inc=1, device_id=device(dz, dy), device_id_type=MESH_ID)
    pl.semaphore_wait(barrier, count)
    copies = []
    for i, (dz, dy) in enumerate(offsets):
        copy = pltpu.make_async_remote_copy(
            src_ref=sources[i],
            dst_ref=targets[i],
            send_sem=send_sems.at[i],
            recv_sem=recv_sems.at[i],
            device_id=device(dz, dy),
            device_id_type=MESH_ID,
        )
        copy.start()
        copies.append(copy)
    for copy in copies:
        copy.wait()


def halo_swap(pieces, collective_id):
    flat = [as_rows(p) for p in pieces]
    vmem = pl.BlockSpec(memory_space=pltpu.VMEM)
    got = pl.pallas_call(
        functools.partial(halo_kernel, NEIGHBOURS),
        out_shape=[jax.ShapeDtypeStruct(f.shape, f.dtype) for f in flat],
        in_specs=[vmem] * len(flat),
        out_specs=[vmem] * len(flat),
        scratch_shapes=[pltpu.SemaphoreType.DMA((len(flat),)), pltpu.SemaphoreType.DMA((len(flat),))],
        compiler_params=pltpu.CompilerParams(collective_id=collective_id, has_side_effects=True),
    )(*flat)
    return [from_rows(g, p.shape) for g, p in zip(got, pieces)]


def as_rows(piece):
    return jnp.transpose(piece, (1, 2, 0, 3)).reshape(-1, piece.shape[3])


def from_rows(rows, shape):
    channels, planes, lines, breadth = shape
    return jnp.transpose(rows.reshape(planes, lines, channels, breadth), (2, 0, 1, 3))


def ranges(shift, count, border):
    if shift == 1:
        return slice(border + count - 1, border + count)
    if shift == -1:
        return slice(border, border + 1)
    return slice(border, border + count)


def halo_pieces(cells):
    _, planes, rows, _ = cells.shape
    return [cells[:, ranges(dz, planes, 0), ranges(dy, rows, 0)] for dz, dy in NEIGHBOURS]


def framed(cells, received):
    got = dict(zip(NEIGHBOURS, received))
    lines = []
    for dz in (1, 0, -1):
        middle = cells if dz == 0 else got[(dz, 0)]
        lines.append(jnp.concatenate([got[(dz, 1)], middle, got[(dz, -1)]], axis=2))
    return jnp.concatenate(lines, axis=1)


def conv_taps(columns, weight, shape):
    _, planes, rows, _ = shape
    total = jnp.zeros(shape, jnp.float32)
    for tap_z in range(3):
        for tap_y in range(3):
            window = columns[:, tap_z : tap_z + planes, tap_y : tap_y + rows]
            total = total + jnp.einsum(
                "oj,jzyx->ozyx", weight[tap_z, tap_y], window, preferred_element_type=jnp.float32
            )
    return total


def transposed_weight(conv_weight):
    taps_z, taps_y, channels, width = conv_weight.shape
    split = conv_weight.reshape(taps_z, taps_y, channels, width // channels, channels)
    split = split[::-1, ::-1, :, ::-1, :]
    return jnp.transpose(split, (0, 1, 4, 3, 2)).reshape(taps_z, taps_y, channels, width)


def border_pieces(spread):
    _, planes, rows, _ = spread.shape
    planes, rows = planes - 2, rows - 2
    pieces = []
    for dz, dy in NEIGHBOURS:
        zs = slice(planes + 1, planes + 2) if dz == 1 else slice(0, 1) if dz == -1 else slice(1, planes + 1)
        ys = slice(rows + 1, rows + 2) if dy == 1 else slice(0, 1) if dy == -1 else slice(1, rows + 1)
        pieces.append(spread[:, zs, ys].astype(jnp.bfloat16))
    return pieces


def folded_grad(spread, got):
    _, planes, rows, _ = spread.shape
    planes, rows = planes - 2, rows - 2
    own = spread[:, 1 : planes + 1, 1 : rows + 1]
    for (dz, dy), piece in zip(NEIGHBOURS, got):
        own = own.at[:, ranges(-dz, planes, 0), ranges(-dy, rows, 0)].add(piece.astype(own.dtype))
    return own


def mesh_bits():
    sizes = {"gz": lax.axis_size("gz"), "gy": lax.axis_size("gy")}
    orders = [[pair[c] for pair in BIT_ORDER if (1 << pair[c][1]) < sizes[pair[c][0]]] for c in (0, 1)]
    return list(zip(*orders))


def halving_groups(bits, halvings):
    if halvings < 3:
        return [(pair,) for pair in bits[:halvings]]
    return [(pair,) for pair in bits[: halvings - 2]] + [tuple(bits[halvings - 2 : halvings])]


def allreduce_kernel(bits, halvings, offsets, x_ref, *refs):
    count = len(offsets)
    pieces, o_ref = refs[:count], refs[count]
    landed = refs[count + 1 : 2 * count + 1]
    scratch = refs[2 * count + 1 :]
    halve_bufs = scratch[: len(halving_groups(bits, halvings))]
    work, double_buf, send_sems, recv_sems, halo_send, halo_recv = scratch[len(halve_bufs) :]
    here = {"gz": lax.axis_index("gz"), "gy": lax.axis_index("gy")}
    sizes = {"gz": lax.axis_size("gz"), "gy": lax.axis_size("gy")}

    def neighbour(dz, dy):
        return ((here["gz"] + dz + sizes["gz"]) % sizes["gz"], (here["gy"] + dy + sizes["gy"]) % sizes["gy"])

    core = here["gy"] % 2

    def pick(pair):
        (axis0, b0), (axis1, b1) = pair
        a0, a1 = int(axis0 == "gy"), int(axis1 == "gy")
        return a0 + (a1 - a0) * core, (1 << b0) + ((1 << b1) - (1 << b0)) * core

    def bit_of(pair):
        which, weight = pick(pair)
        value = here["gz"] + (here["gy"] - here["gz"]) * which
        return (value // weight) % 2

    def partner(*pairs):
        device = [here["gz"], here["gy"]]
        for pair in pairs:
            which, weight = pick(pair)
            step = (1 - 2 * bit_of(pair)) * weight
            device = [device[0] + step * (1 - which), device[1] + step * which]
        return tuple(device)

    groups = [bits[i : i + 2] for i in range(halvings, len(bits), 2)]
    wide = [tuple(g) for g in groups + halving_groups(bits, halvings) if len(g) == 2]
    reach = [(pair,) for pair in bits] + wide

    barrier = pltpu.get_barrier_semaphore()
    for pairs in reach:
        pl.semaphore_signal(barrier, inc=1, device_id=partner(*pairs), device_id_type=MESH_ID)
    for dz, dy in offsets:
        pl.semaphore_signal(barrier, inc=1, device_id=neighbour(dz, dy), device_id_type=MESH_ID)
    pl.semaphore_wait(barrier, len(reach) + count)
    halo = []
    for i, (dz, dy) in enumerate(offsets):
        copy = pltpu.make_async_remote_copy(
            src_ref=pieces[i],
            dst_ref=landed[i],
            send_sem=halo_send.at[i],
            recv_sem=halo_recv.at[i],
            device_id=neighbour(dz, dy),
            device_id_type=MESH_ID,
        )
        copy.start()
        halo.append(copy)

    def exchange(step, pair, src, dst):
        start_copy(step, (pair,), src, dst).wait()

    def start_copy(step, pairs, src, dst):
        copy = pltpu.make_async_remote_copy(
            src_ref=src,
            dst_ref=dst,
            send_sem=send_sems.at[step],
            recv_sem=recv_sems.at[step],
            device_id=partner(*pairs),
            device_id_type=MESH_ID,
        )
        copy.start()
        return copy

    lo, length, step = 0, o_ref.shape[0], 0
    for k, group in enumerate(halving_groups(bits, halvings)):
        source = x_ref if k == 0 else work
        flips = [group] if len(group) == 1 else [group[:1], group[1:], group]
        parts = 1 << len(group)
        piece = length // parts
        mine = 0
        for pair in group:
            mine = 2 * mine + bit_of(pair)
        copies = []
        for m, flip in enumerate(flips):
            theirs = 0
            for pair in group:
                flipped = bit_of(pair) + (1 - 2 * bit_of(pair)) * int(pair in flip)
                theirs = 2 * theirs + flipped
            start = pl.multiple_of(lo + theirs * piece, 8)
            copies.append(start_copy(step + m, flip, source.at[pl.ds(start, piece)], halve_bufs[k].at[m]))
        for copy in copies:
            copy.wait()
        keep = pl.multiple_of(lo + mine * piece, 8)
        total = source[pl.ds(keep, piece)]
        for m in range(len(flips)):
            total = total + halve_bufs[k][m]
        work[pl.ds(keep, piece)] = total
        lo, length, step = keep, piece, step + len(flips)
    slot = 0
    for group in groups:
        own = work.at[pl.ds(lo, length)]
        if len(group) == 1:
            exchange(step, group[0], own, double_buf.at[slot])
            work[pl.ds(lo, length)] = own[...] + double_buf[slot]
            slot, step = slot + 1, step + 1
            continue
        flips = [(group[0],), (group[1],), (group[0], group[1])]
        copies = [start_copy(step + m, f, own, double_buf.at[slot + m]) for m, f in enumerate(flips)]
        for copy in copies:
            copy.wait()
        near, far = double_buf[slot] + own[...], double_buf[slot + 1] + double_buf[slot + 2]
        work[pl.ds(lo, length)] = near + far
        slot, step = slot + 3, step + 3
    o_ref[pl.ds(lo, length)] = work[pl.ds(lo, length)]
    for group in reversed(halving_groups(bits, halvings)):
        flips = [group] if len(group) == 1 else [group[:1], group[1:], group]
        region = o_ref.at[pl.ds(lo, length)]
        copies = [start_copy(step + m, flip, region, region) for m, flip in enumerate(flips)]
        for copy in copies:
            copy.wait()
        mine = 0
        for pair in group:
            mine = 2 * mine + bit_of(pair)
        lo = pl.multiple_of(lo - mine * length, 8)
        length, step = length << len(group), step + len(flips)
    for copy in halo:
        copy.wait()


def allreduce(flat, pieces=(), halvings=HALVINGS):
    offsets = NEIGHBOURS[: len(pieces)]
    pieces = [p.reshape(-1, 128) for p in pieces]
    bits = mesh_bits()
    halvings = min(halvings, len(bits))
    rows = flat.shape[0]
    segment = rows >> halvings
    far = len(bits) - halvings
    slots = 3 * (far // 2) + far % 2
    steps = 2 * sum((1 << len(g)) - 1 for g in halving_groups(bits, halvings)) + slots
    scratch, length = [], rows
    for group in halving_groups(bits, halvings):
        length >>= len(group)
        scratch.append(pltpu.VMEM(((1 << len(group)) - 1, length, 128), jnp.float32))
    scratch += [
        pltpu.VMEM(flat.shape, jnp.float32),
        pltpu.VMEM((max(slots, 1), segment, 128), jnp.float32),
        pltpu.SemaphoreType.DMA((steps,)),
        pltpu.SemaphoreType.DMA((steps,)),
        pltpu.SemaphoreType.DMA((max(len(pieces), 1),)),
        pltpu.SemaphoreType.DMA((max(len(pieces), 1),)),
    ]
    vmem = pl.BlockSpec(memory_space=pltpu.VMEM)
    outs = pl.pallas_call(
        functools.partial(allreduce_kernel, bits, halvings, offsets),
        out_shape=[jax.ShapeDtypeStruct(flat.shape, jnp.float32)]
        + [jax.ShapeDtypeStruct(p.shape, p.dtype) for p in pieces],
        in_specs=[vmem] * (1 + len(pieces)),
        out_specs=[vmem] * (1 + len(pieces)),
        scratch_shapes=scratch,
        compiler_params=pltpu.CompilerParams(collective_id=0, has_side_effects=True),
    )(flat, *pieces)
    return outs[0], outs[1:]


def summed_gradients(local_conv, local_down, pieces, scale):
    sizes = (local_conv.size, local_down.size)
    flat = jnp.concatenate([local_conv.reshape(-1), local_down.reshape(-1)]) * scale
    unit = 128 * 8 << HALVINGS
    padded = -(-flat.size // unit) * unit
    flat = jnp.pad(flat, (0, padded - flat.size)).reshape(-1, 128)
    total, got = allreduce(flat, [as_rows(p) for p in pieces])
    total = total.reshape(-1)
    return (
        total[: sizes[0]].reshape(local_conv.shape),
        total[sizes[0] : sizes[0] + sizes[1]].reshape(local_down.shape),
        [from_rows(g, p.shape) for g, p in zip(got, pieces)],
    )


def body(features, conv_weight, down_weight, cotangent):
    channels, plane_count, row_count, breadth = features.shape
    out_channels = down_weight.shape[2]
    cell_count = plane_count * row_count * breadth * lax.axis_size("gz") * lax.axis_size("gy")
    grad_scale = 1.0 / math.sqrt(cell_count)
    columns = widen(framed(features, halo_swap(halo_pieces(features), 1)))
    preact = conv_taps(columns, conv_weight, features.shape)
    hidden = jax.nn.silu(preact).astype(jnp.bfloat16)
    blocks = hidden.reshape(channels, plane_count // 2, 2, row_count // 2, 2, breadth // 2, 2)
    down_split = down_weight.reshape(2, 2, out_channels, 2, channels)
    coarse = jnp.einsum(
        "aboei,iZaYbXe->oZYX", down_split, blocks, preferred_element_type=jnp.float32
    )
    section_out = coarse.reshape(out_channels, plane_count // 2, -1).astype(jnp.bfloat16)
    coarse_cot = cotangent.reshape(out_channels, plane_count // 2, row_count // 2, breadth // 2)
    hidden_grad = jnp.einsum(
        "aboei,oZYX->iZaYbXe", down_split, coarse_cot, preferred_element_type=jnp.float32
    )
    hidden_grad = hidden_grad.reshape(channels, plane_count, row_count, breadth)
    local_down = jnp.einsum(
        "oZYX,iZaYbXe->aboei", coarse_cot, blocks, preferred_element_type=jnp.float32
    )
    local_down = local_down.reshape(2, 2, out_channels, 2 * channels)
    gate_sig = jax.nn.sigmoid(preact)
    gate_grad = (hidden_grad * gate_sig * (1.0 + preact * (1.0 - gate_sig))).astype(jnp.bfloat16)
    kernel_rows = []
    for tap_z in range(3):
        row_list = []
        for tap_y in range(3):
            window = columns[:, tap_z : tap_z + plane_count, tap_y : tap_y + row_count]
            row_list.append(
                jnp.einsum("ozyx,jzyx->oj", gate_grad, window, preferred_element_type=jnp.float32)
            )
        kernel_rows.append(jnp.stack(row_list, axis=0))
    local_conv = jnp.stack(kernel_rows, axis=0)
    summed_conv, summed_down, got = summed_gradients(local_conv, local_down, halo_pieces(gate_grad), grad_scale)
    gate_columns = widen(framed(gate_grad, got))
    grad_field = conv_taps(gate_columns, transposed_weight(conv_weight), features.shape)
    return (section_out, grad_field, summed_conv, summed_down)


def solution(mesh):
    return jax.shard_map(
        body,
        mesh=mesh,
        in_specs=(P(None, "gz", "gy", None), P(), P(), P(None, "gz", "gy")),
        out_specs=(P(None, "gz", "gy"), P(None, "gz", "gy", None), P(), P()),
        check_vma=False,
    )
```

```python
import functools
import math

import jax
import jax.numpy as jnp
from jax import lax
from jax.experimental import pallas as pl
from jax.experimental.pallas import tpu as pltpu
from jax.sharding import PartitionSpec as P

MESH_ID = pl.DeviceIdType.MESH
BIT_ORDER = (
    (("gy", 0), ("gy", 0)),
    (("gy", 1), ("gz", 0)),
    (("gz", 0), ("gz", 3)),
    (("gz", 3), ("gy", 1)),
    (("gz", 1), ("gz", 4)),
    (("gz", 2), ("gy", 3)),
    (("gz", 4), ("gz", 1)),
    (("gy", 3), ("gz", 2)),
    (("gy", 2), ("gy", 2)),
)
HALVINGS = 4


def extended(cells, sides, width):
    for axis, dim in sides:
        count = lax.axis_size(axis)
        head = lax.slice_in_dim(cells, 0, width, axis=dim)
        tail = lax.slice_in_dim(cells, cells.shape[dim] - width, cells.shape[dim], axis=dim)
        cells = jnp.concatenate(
            [
                lax.ppermute(tail, axis, [(i, (i + 1) % count) for i in range(count)]),
                cells,
                lax.ppermute(head, axis, [((i + 1) % count, i) for i in range(count)]),
            ],
            axis=dim,
        )
    return cells


def widen(framed):
    return jnp.concatenate([jnp.roll(framed, 1 - tap_x, axis=3) for tap_x in range(3)], axis=0)


def fold_along(spread, channels):
    result = jnp.roll(spread[0:channels], -1, axis=3)
    result = result + spread[channels : 2 * channels]
    result = result + jnp.roll(spread[2 * channels : 3 * channels], 1, axis=3)
    return result


NEIGHBOURS = ((1, 0), (-1, 0), (0, 1), (0, -1), (1, 1), (1, -1), (-1, 1), (-1, -1))


def halo_kernel(offsets, *refs):
    count = len(offsets)
    sources, targets = refs[:count], refs[count : 2 * count]
    send_sems, recv_sems = refs[2 * count :]
    sizes = (lax.axis_size("gz"), lax.axis_size("gy"))
    here = (lax.axis_index("gz"), lax.axis_index("gy"))

    def device(dz, dy):
        return ((here[0] + dz + sizes[0]) % sizes[0], (here[1] + dy + sizes[1]) % sizes[1])

    barrier = pltpu.get_barrier_semaphore()
    for dz, dy in offsets:
        pl.semaphore_signal(barrier, inc=1, device_id=device(dz, dy), device_id_type=MESH_ID)
    pl.semaphore_wait(barrier, count)
    copies = []
    for i, (dz, dy) in enumerate(offsets):
        copy = pltpu.make_async_remote_copy(
            src_ref=sources[i],
            dst_ref=targets[i],
            send_sem=send_sems.at[i],
            recv_sem=recv_sems.at[i],
            device_id=device(dz, dy),
            device_id_type=MESH_ID,
        )
        copy.start()
        copies.append(copy)
    for copy in copies:
        copy.wait()


def halo_swap(pieces, collective_id):
    flat = [as_rows(p) for p in pieces]
    vmem = pl.BlockSpec(memory_space=pltpu.VMEM)
    got = pl.pallas_call(
        functools.partial(halo_kernel, NEIGHBOURS),
        out_shape=[jax.ShapeDtypeStruct(f.shape, f.dtype) for f in flat],
        in_specs=[vmem] * len(flat),
        out_specs=[vmem] * len(flat),
        scratch_shapes=[pltpu.SemaphoreType.DMA((len(flat),)), pltpu.SemaphoreType.DMA((len(flat),))],
        compiler_params=pltpu.CompilerParams(collective_id=collective_id, has_side_effects=True),
    )(*flat)
    return [from_rows(g, p.shape) for g, p in zip(got, pieces)]


def as_rows(piece):
    return jnp.transpose(piece, (1, 2, 0, 3)).reshape(-1, piece.shape[3])


def from_rows(rows, shape):
    channels, planes, lines, breadth = shape
    return jnp.transpose(rows.reshape(planes, lines, channels, breadth), (2, 0, 1, 3))


def ranges(shift, count, border):
    if shift == 1:
        return slice(border + count - 1, border + count)
    if shift == -1:
        return slice(border, border + 1)
    return slice(border, border + count)


def halo_pieces(cells):
    _, planes, rows, _ = cells.shape
    return [cells[:, ranges(dz, planes, 0), ranges(dy, rows, 0)] for dz, dy in NEIGHBOURS]


def framed(cells, received):
    got = dict(zip(NEIGHBOURS, received))
    lines = []
    for dz in (1, 0, -1):
        middle = cells if dz == 0 else got[(dz, 0)]
        lines.append(jnp.concatenate([got[(dz, 1)], middle, got[(dz, -1)]], axis=2))
    return jnp.concatenate(lines, axis=1)


def conv_taps(columns, weight, shape):
    _, planes, rows, _ = shape
    total = jnp.zeros(shape, jnp.float32)
    for tap_z in range(3):
        for tap_y in range(3):
            window = columns[:, tap_z : tap_z + planes, tap_y : tap_y + rows]
            total = total + jnp.einsum(
                "oj,jzyx->ozyx", weight[tap_z, tap_y], window, preferred_element_type=jnp.float32
            )
    return total


def transposed_weight(conv_weight):
    taps_z, taps_y, channels, width = conv_weight.shape
    split = conv_weight.reshape(taps_z, taps_y, channels, width // channels, channels)
    split = split[::-1, ::-1, :, ::-1, :]
    return jnp.transpose(split, (0, 1, 4, 3, 2)).reshape(taps_z, taps_y, channels, width)


def border_pieces(spread):
    _, planes, rows, _ = spread.shape
    planes, rows = planes - 2, rows - 2
    pieces = []
    for dz, dy in NEIGHBOURS:
        zs = slice(planes + 1, planes + 2) if dz == 1 else slice(0, 1) if dz == -1 else slice(1, planes + 1)
        ys = slice(rows + 1, rows + 2) if dy == 1 else slice(0, 1) if dy == -1 else slice(1, rows + 1)
        pieces.append(spread[:, zs, ys].astype(jnp.bfloat16))
    return pieces


def folded_grad(spread, got):
    _, planes, rows, _ = spread.shape
    planes, rows = planes - 2, rows - 2
    own = spread[:, 1 : planes + 1, 1 : rows + 1]
    for (dz, dy), piece in zip(NEIGHBOURS, got):
        own = own.at[:, ranges(-dz, planes, 0), ranges(-dy, rows, 0)].add(piece.astype(own.dtype))
    return own


def mesh_bits():
    sizes = {"gz": lax.axis_size("gz"), "gy": lax.axis_size("gy")}
    orders = [[pair[c] for pair in BIT_ORDER if (1 << pair[c][1]) < sizes[pair[c][0]]] for c in (0, 1)]
    return list(zip(*orders))


def halving_groups(bits, halvings):
    if halvings < 3:
        return [(pair,) for pair in bits[:halvings]]
    return [(pair,) for pair in bits[: halvings - 2]] + [tuple(bits[halvings - 2 : halvings])]


def allreduce_kernel(bits, halvings, offsets, x_ref, *refs):
    count = len(offsets)
    pieces, outs = refs[:count], refs[count : count + 2]
    landed = refs[count + 2 : 2 * count + 2]
    scratch, o_ref = refs[2 * count + 2 : -1], refs[-1]
    halve_bufs = scratch[: len(halving_groups(bits, halvings))]
    work, double_buf, send_sems, recv_sems, halo_send, halo_recv = scratch[len(halve_bufs) :]
    here = {"gz": lax.axis_index("gz"), "gy": lax.axis_index("gy")}
    sizes = {"gz": lax.axis_size("gz"), "gy": lax.axis_size("gy")}

    def neighbour(dz, dy):
        return ((here["gz"] + dz + sizes["gz"]) % sizes["gz"], (here["gy"] + dy + sizes["gy"]) % sizes["gy"])

    core = here["gy"] % 2

    def pick(pair):
        (axis0, b0), (axis1, b1) = pair
        a0, a1 = int(axis0 == "gy"), int(axis1 == "gy")
        return a0 + (a1 - a0) * core, (1 << b0) + ((1 << b1) - (1 << b0)) * core

    def bit_of(pair):
        which, weight = pick(pair)
        value = here["gz"] + (here["gy"] - here["gz"]) * which
        return (value // weight) % 2

    def partner(*pairs):
        device = [here["gz"], here["gy"]]
        for pair in pairs:
            which, weight = pick(pair)
            step = (1 - 2 * bit_of(pair)) * weight
            device = [device[0] + step * (1 - which), device[1] + step * which]
        return tuple(device)

    groups = [bits[i : i + 2] for i in range(halvings, len(bits), 2)]
    wide = [tuple(g) for g in groups + halving_groups(bits, halvings) if len(g) == 2]
    reach = [(pair,) for pair in bits] + wide

    barrier = pltpu.get_barrier_semaphore()
    for pairs in reach:
        pl.semaphore_signal(barrier, inc=1, device_id=partner(*pairs), device_id_type=MESH_ID)
    for dz, dy in offsets:
        pl.semaphore_signal(barrier, inc=1, device_id=neighbour(dz, dy), device_id_type=MESH_ID)
    pl.semaphore_wait(barrier, len(reach) + count)
    halo = []
    for i, (dz, dy) in enumerate(offsets):
        copy = pltpu.make_async_remote_copy(
            src_ref=pieces[i],
            dst_ref=landed[i],
            send_sem=halo_send.at[i],
            recv_sem=halo_recv.at[i],
            device_id=neighbour(dz, dy),
            device_id_type=MESH_ID,
        )
        copy.start()
        halo.append(copy)

    def exchange(step, pair, src, dst):
        start_copy(step, (pair,), src, dst).wait()

    def start_copy(step, pairs, src, dst):
        copy = pltpu.make_async_remote_copy(
            src_ref=src,
            dst_ref=dst,
            send_sem=send_sems.at[step],
            recv_sem=recv_sems.at[step],
            device_id=partner(*pairs),
            device_id_type=MESH_ID,
        )
        copy.start()
        return copy

    lo, length, step = 0, o_ref.shape[0], 0
    for k, group in enumerate(halving_groups(bits, halvings)):
        source = x_ref if k == 0 else work
        flips = [group] if len(group) == 1 else [group[:1], group[1:], group]
        parts = 1 << len(group)
        piece = length // parts
        mine = 0
        for pair in group:
            mine = 2 * mine + bit_of(pair)
        copies = []
        for m, flip in enumerate(flips):
            theirs = 0
            for pair in group:
                flipped = bit_of(pair) + (1 - 2 * bit_of(pair)) * int(pair in flip)
                theirs = 2 * theirs + flipped
            start = pl.multiple_of(lo + theirs * piece, 8)
            copies.append(start_copy(step + m, flip, source.at[pl.ds(start, piece)], halve_bufs[k].at[m]))
        for copy in copies:
            copy.wait()
        keep = pl.multiple_of(lo + mine * piece, 8)
        total = source[pl.ds(keep, piece)]
        for m in range(len(flips)):
            total = total + halve_bufs[k][m]
        work[pl.ds(keep, piece)] = total
        lo, length, step = keep, piece, step + len(flips)
    slot = 0
    for group in groups:
        own = work.at[pl.ds(lo, length)]
        if len(group) == 1:
            exchange(step, group[0], own, double_buf.at[slot])
            work[pl.ds(lo, length)] = own[...] + double_buf[slot]
            slot, step = slot + 1, step + 1
            continue
        flips = [(group[0],), (group[1],), (group[0], group[1])]
        copies = [start_copy(step + m, f, own, double_buf.at[slot + m]) for m, f in enumerate(flips)]
        for copy in copies:
            copy.wait()
        near, far = double_buf[slot] + own[...], double_buf[slot + 1] + double_buf[slot + 2]
        work[pl.ds(lo, length)] = near + far
        slot, step = slot + 3, step + 3
    o_ref[pl.ds(lo, length)] = work[pl.ds(lo, length)]
    for group in reversed(halving_groups(bits, halvings)):
        flips = [group] if len(group) == 1 else [group[:1], group[1:], group]
        region = o_ref.at[pl.ds(lo, length)]
        copies = [start_copy(step + m, flip, region, region) for m, flip in enumerate(flips)]
        for copy in copies:
            copy.wait()
        mine = 0
        for pair in group:
            mine = 2 * mine + bit_of(pair)
        lo = pl.multiple_of(lo - mine * length, 8)
        length, step = length << len(group), step + len(flips)
    for copy in halo:
        copy.wait()
    start = 0
    for out in outs:
        out[...] = o_ref[pl.ds(start, out.shape[0])]
        start += out.shape[0]


def allreduce(flat, splits, pieces=(), halvings=HALVINGS):
    offsets = NEIGHBOURS[: len(pieces)]
    pieces = [p.reshape(-1, 128) for p in pieces]
    bits = mesh_bits()
    halvings = min(halvings, len(bits))
    rows = flat.shape[0]
    segment = rows >> halvings
    far = len(bits) - halvings
    slots = 3 * (far // 2) + far % 2
    steps = 2 * sum((1 << len(g)) - 1 for g in halving_groups(bits, halvings)) + slots
    scratch, length = [], rows
    for group in halving_groups(bits, halvings):
        length >>= len(group)
        scratch.append(pltpu.VMEM(((1 << len(group)) - 1, length, 128), jnp.float32))
    scratch += [
        pltpu.VMEM(flat.shape, jnp.float32),
        pltpu.VMEM((max(slots, 1), segment, 128), jnp.float32),
        pltpu.SemaphoreType.DMA((steps,)),
        pltpu.SemaphoreType.DMA((steps,)),
        pltpu.SemaphoreType.DMA((max(len(pieces), 1),)),
        pltpu.SemaphoreType.DMA((max(len(pieces), 1),)),
        pltpu.VMEM(flat.shape, jnp.float32),
    ]
    vmem = pl.BlockSpec(memory_space=pltpu.VMEM)
    outs = pl.pallas_call(
        functools.partial(allreduce_kernel, bits, halvings, offsets),
        out_shape=[jax.ShapeDtypeStruct((rows_out, 128), jnp.float32) for rows_out in splits]
        + [jax.ShapeDtypeStruct(p.shape, p.dtype) for p in pieces],
        in_specs=[vmem] * (1 + len(pieces)),
        out_specs=[vmem] * (len(splits) + len(pieces)),
        scratch_shapes=scratch,
        compiler_params=pltpu.CompilerParams(collective_id=0, has_side_effects=True),
    )(flat, *pieces)
    return outs[: len(splits)], outs[len(splits) :]


def summed_gradients(local_conv, local_down, pieces, scale):
    sizes = (local_conv.size, local_down.size)
    flat = jnp.concatenate([local_conv.reshape(-1), local_down.reshape(-1)]) * scale
    unit = 128 * 8 << HALVINGS
    padded = -(-flat.size // unit) * unit
    flat = jnp.pad(flat, (0, padded - flat.size)).reshape(-1, 128)
    (conv_rows, down_rows), got = allreduce(flat, (sizes[0] // 128, sizes[1] // 128), [as_rows(p) for p in pieces])
    return (
        conv_rows.reshape(local_conv.shape),
        down_rows.reshape(local_down.shape),
        [from_rows(g, p.shape) for g, p in zip(got, pieces)],
    )


def body(features, conv_weight, down_weight, cotangent):
    channels, plane_count, row_count, breadth = features.shape
    out_channels = down_weight.shape[2]
    cell_count = plane_count * row_count * breadth * lax.axis_size("gz") * lax.axis_size("gy")
    grad_scale = 1.0 / math.sqrt(cell_count)
    columns = widen(framed(features, halo_swap(halo_pieces(features), 1)))
    preact = conv_taps(columns, conv_weight, features.shape)
    hidden = jax.nn.silu(preact).astype(jnp.bfloat16)
    blocks = hidden.reshape(channels, plane_count // 2, 2, row_count // 2, 2, breadth // 2, 2)
    down_split = down_weight.reshape(2, 2, out_channels, 2, channels)
    coarse = jnp.einsum(
        "aboei,iZaYbXe->oZYX", down_split, blocks, preferred_element_type=jnp.float32
    )
    section_out = coarse.reshape(out_channels, plane_count // 2, -1).astype(jnp.bfloat16)
    coarse_cot = cotangent.reshape(out_channels, plane_count // 2, row_count // 2, breadth // 2)
    hidden_grad = jnp.einsum(
        "aboei,oZYX->iZaYbXe", down_split, coarse_cot, preferred_element_type=jnp.float32
    )
    hidden_grad = hidden_grad.reshape(channels, plane_count, row_count, breadth)
    local_down = jnp.einsum(
        "oZYX,iZaYbXe->aboei", coarse_cot, blocks, preferred_element_type=jnp.float32
    )
    local_down = local_down.reshape(2, 2, out_channels, 2 * channels)
    gate_sig = jax.nn.sigmoid(preact)
    gate_grad = (hidden_grad * gate_sig * (1.0 + preact * (1.0 - gate_sig))).astype(jnp.bfloat16)
    kernel_rows = []
    for tap_z in range(3):
        row_list = []
        for tap_y in range(3):
            window = columns[:, tap_z : tap_z + plane_count, tap_y : tap_y + row_count]
            row_list.append(
                jnp.einsum("ozyx,jzyx->oj", gate_grad, window, preferred_element_type=jnp.float32)
            )
        kernel_rows.append(jnp.stack(row_list, axis=0))
    local_conv = jnp.stack(kernel_rows, axis=0)
    summed_conv, summed_down, got = summed_gradients(local_conv, local_down, halo_pieces(gate_grad), grad_scale)
    gate_columns = widen(framed(gate_grad, got))
    grad_field = conv_taps(gate_columns, transposed_weight(conv_weight), features.shape)
    return (section_out, grad_field, summed_conv, summed_down)


def solution(mesh):
    return jax.shard_map(
        body,
        mesh=mesh,
        in_specs=(P(None, "gz", "gy", None), P(), P(), P(None, "gz", "gy")),
        out_specs=(P(None, "gz", "gy"), P(None, "gz", "gy", None), P(), P()),
        check_vma=False,
    )
```

```python
import functools
import math

import jax
import jax.numpy as jnp
from jax import lax
from jax.experimental import pallas as pl
from jax.experimental.pallas import tpu as pltpu
from jax.sharding import PartitionSpec as P

MESH_ID = pl.DeviceIdType.MESH
BIT_ORDER = (
    (("gy", 0), ("gy", 0)),
    (("gy", 1), ("gz", 0)),
    (("gz", 0), ("gz", 3)),
    (("gz", 3), ("gy", 1)),
    (("gz", 1), ("gz", 4)),
    (("gz", 2), ("gy", 3)),
    (("gz", 4), ("gz", 1)),
    (("gy", 3), ("gz", 2)),
    (("gy", 2), ("gy", 2)),
)
HALVINGS = 4


def extended(cells, sides, width):
    for axis, dim in sides:
        count = lax.axis_size(axis)
        head = lax.slice_in_dim(cells, 0, width, axis=dim)
        tail = lax.slice_in_dim(cells, cells.shape[dim] - width, cells.shape[dim], axis=dim)
        cells = jnp.concatenate(
            [
                lax.ppermute(tail, axis, [(i, (i + 1) % count) for i in range(count)]),
                cells,
                lax.ppermute(head, axis, [((i + 1) % count, i) for i in range(count)]),
            ],
            axis=dim,
        )
    return cells


def widen(framed):
    return jnp.concatenate([jnp.roll(framed, 1 - tap_x, axis=3) for tap_x in range(3)], axis=0)


def fold_along(spread, channels):
    result = jnp.roll(spread[0:channels], -1, axis=3)
    result = result + spread[channels : 2 * channels]
    result = result + jnp.roll(spread[2 * channels : 3 * channels], 1, axis=3)
    return result


NEIGHBOURS = ((1, 0), (-1, 0), (0, 1), (0, -1), (1, 1), (1, -1), (-1, 1), (-1, -1))


def halo_kernel(offsets, *refs):
    count = len(offsets)
    sources, targets = refs[:count], refs[count : 2 * count]
    send_sems, recv_sems = refs[2 * count :]
    sizes = (lax.axis_size("gz"), lax.axis_size("gy"))
    here = (lax.axis_index("gz"), lax.axis_index("gy"))

    def device(dz, dy):
        return ((here[0] + dz + sizes[0]) % sizes[0], (here[1] + dy + sizes[1]) % sizes[1])

    barrier = pltpu.get_barrier_semaphore()
    for dz, dy in offsets:
        pl.semaphore_signal(barrier, inc=1, device_id=device(dz, dy), device_id_type=MESH_ID)
    pl.semaphore_wait(barrier, count)
    copies = []
    for i, (dz, dy) in enumerate(offsets):
        copy = pltpu.make_async_remote_copy(
            src_ref=sources[i],
            dst_ref=targets[i],
            send_sem=send_sems.at[i],
            recv_sem=recv_sems.at[i],
            device_id=device(dz, dy),
            device_id_type=MESH_ID,
        )
        copy.start()
        copies.append(copy)
    for copy in copies:
        copy.wait()


def halo_swap(pieces, collective_id):
    flat = [as_rows(p) for p in pieces]
    vmem = pl.BlockSpec(memory_space=pltpu.VMEM)
    got = pl.pallas_call(
        functools.partial(halo_kernel, NEIGHBOURS),
        out_shape=[jax.ShapeDtypeStruct(f.shape, f.dtype) for f in flat],
        in_specs=[vmem] * len(flat),
        out_specs=[vmem] * len(flat),
        scratch_shapes=[pltpu.SemaphoreType.DMA((len(flat),)), pltpu.SemaphoreType.DMA((len(flat),))],
        compiler_params=pltpu.CompilerParams(collective_id=collective_id, has_side_effects=True),
    )(*flat)
    return [from_rows(g, p.shape) for g, p in zip(got, pieces)]


def as_rows(piece):
    return jnp.transpose(piece, (1, 2, 0, 3)).reshape(-1, piece.shape[3])


def from_rows(rows, shape):
    channels, planes, lines, breadth = shape
    return jnp.transpose(rows.reshape(planes, lines, channels, breadth), (2, 0, 1, 3))


def ranges(shift, count, border):
    if shift == 1:
        return slice(border + count - 1, border + count)
    if shift == -1:
        return slice(border, border + 1)
    return slice(border, border + count)


def halo_pieces(cells):
    _, planes, rows, _ = cells.shape
    return [cells[:, ranges(dz, planes, 0), ranges(dy, rows, 0)] for dz, dy in NEIGHBOURS]


def framed(cells, received):
    got = dict(zip(NEIGHBOURS, received))
    lines = []
    for dz in (1, 0, -1):
        middle = cells if dz == 0 else got[(dz, 0)]
        lines.append(jnp.concatenate([got[(dz, 1)], middle, got[(dz, -1)]], axis=2))
    return jnp.concatenate(lines, axis=1)


def conv_taps(columns, weight, shape):
    _, planes, rows, _ = shape
    total = jnp.zeros(shape, jnp.float32)
    for tap_z in range(3):
        for tap_y in range(3):
            window = columns[:, tap_z : tap_z + planes, tap_y : tap_y + rows]
            total = total + jnp.einsum(
                "oj,jzyx->ozyx", weight[tap_z, tap_y], window, preferred_element_type=jnp.float32
            )
    return total


def transposed_weight(conv_weight):
    taps_z, taps_y, channels, width = conv_weight.shape
    split = conv_weight.reshape(taps_z, taps_y, channels, width // channels, channels)
    split = split[::-1, ::-1, :, ::-1, :]
    return jnp.transpose(split, (0, 1, 4, 3, 2)).reshape(taps_z, taps_y, channels, width)


def border_pieces(spread):
    _, planes, rows, _ = spread.shape
    planes, rows = planes - 2, rows - 2
    pieces = []
    for dz, dy in NEIGHBOURS:
        zs = slice(planes + 1, planes + 2) if dz == 1 else slice(0, 1) if dz == -1 else slice(1, planes + 1)
        ys = slice(rows + 1, rows + 2) if dy == 1 else slice(0, 1) if dy == -1 else slice(1, rows + 1)
        pieces.append(spread[:, zs, ys].astype(jnp.bfloat16))
    return pieces


def folded_grad(spread, got):
    _, planes, rows, _ = spread.shape
    planes, rows = planes - 2, rows - 2
    own = spread[:, 1 : planes + 1, 1 : rows + 1]
    for (dz, dy), piece in zip(NEIGHBOURS, got):
        own = own.at[:, ranges(-dz, planes, 0), ranges(-dy, rows, 0)].add(piece.astype(own.dtype))
    return own


def mesh_bits():
    sizes = {"gz": lax.axis_size("gz"), "gy": lax.axis_size("gy")}
    orders = [[pair[c] for pair in BIT_ORDER if (1 << pair[c][1]) < sizes[pair[c][0]]] for c in (0, 1)]
    return list(zip(*orders))


def halving_groups(bits, halvings):
    if halvings < 3:
        return [(pair,) for pair in bits[:halvings]]
    return [(pair,) for pair in bits[: halvings - 2]] + [tuple(bits[halvings - 2 : halvings])]


def allreduce_kernel(bits, halvings, offsets, x_ref, *refs):
    count = len(offsets)
    pieces, outs = refs[:count], refs[count : count + 2]
    landed = refs[count + 2 : 2 * count + 2]
    scratch, o_ref = refs[2 * count + 2 : -1], refs[-1]
    halve_bufs = scratch[: len(halving_groups(bits, halvings))]
    work, double_buf, send_sems, recv_sems, halo_send, halo_recv = scratch[len(halve_bufs) :]
    here = {"gz": lax.axis_index("gz"), "gy": lax.axis_index("gy")}
    sizes = {"gz": lax.axis_size("gz"), "gy": lax.axis_size("gy")}

    def neighbour(dz, dy):
        return ((here["gz"] + dz + sizes["gz"]) % sizes["gz"], (here["gy"] + dy + sizes["gy"]) % sizes["gy"])

    core = here["gy"] % 2

    def pick(pair):
        (axis0, b0), (axis1, b1) = pair
        a0, a1 = int(axis0 == "gy"), int(axis1 == "gy")
        return a0 + (a1 - a0) * core, (1 << b0) + ((1 << b1) - (1 << b0)) * core

    def bit_of(pair):
        which, weight = pick(pair)
        value = here["gz"] + (here["gy"] - here["gz"]) * which
        return (value // weight) % 2

    def partner(*pairs):
        device = [here["gz"], here["gy"]]
        for pair in pairs:
            which, weight = pick(pair)
            step = (1 - 2 * bit_of(pair)) * weight
            device = [device[0] + step * (1 - which), device[1] + step * which]
        return tuple(device)

    groups = [bits[i : i + 2] for i in range(halvings, len(bits), 2)]
    wide = [tuple(g) for g in groups + halving_groups(bits, halvings) if len(g) == 2]
    reach = [(pair,) for pair in bits] + wide

    barrier = pltpu.get_barrier_semaphore()
    for pairs in reach:
        pl.semaphore_signal(barrier, inc=1, device_id=partner(*pairs), device_id_type=MESH_ID)
    for dz, dy in offsets:
        pl.semaphore_signal(barrier, inc=1, device_id=neighbour(dz, dy), device_id_type=MESH_ID)
    pl.semaphore_wait(barrier, len(reach) + count)
    halo = []
    for i, (dz, dy) in enumerate(offsets):
        copy = pltpu.make_async_remote_copy(
            src_ref=pieces[i],
            dst_ref=landed[i],
            send_sem=halo_send.at[i],
            recv_sem=halo_recv.at[i],
            device_id=neighbour(dz, dy),
            device_id_type=MESH_ID,
        )
        copy.start()
        halo.append(copy)

    def exchange(step, pair, src, dst):
        start_copy(step, (pair,), src, dst).wait()

    def start_copy(step, pairs, src, dst):
        copy = pltpu.make_async_remote_copy(
            src_ref=src,
            dst_ref=dst,
            send_sem=send_sems.at[step],
            recv_sem=recv_sems.at[step],
            device_id=partner(*pairs),
            device_id_type=MESH_ID,
        )
        copy.start()
        return copy

    lo, length, step = 0, o_ref.shape[0], 0
    for k, group in enumerate(halving_groups(bits, halvings)):
        source = x_ref if k == 0 else work
        flips = [group] if len(group) == 1 else [group[:1], group[1:], group]
        parts = 1 << len(group)
        piece = length // parts
        mine = 0
        for pair in group:
            mine = 2 * mine + bit_of(pair)
        copies = []
        for m, flip in enumerate(flips):
            theirs = 0
            for pair in group:
                flipped = bit_of(pair) + (1 - 2 * bit_of(pair)) * int(pair in flip)
                theirs = 2 * theirs + flipped
            start = pl.multiple_of(lo + theirs * piece, 8)
            copies.append(start_copy(step + m, flip, source.at[pl.ds(start, piece)], halve_bufs[k].at[m]))
        for copy in copies:
            copy.wait()
        keep = pl.multiple_of(lo + mine * piece, 8)
        total = source[pl.ds(keep, piece)]
        for m in range(len(flips)):
            total = total + halve_bufs[k][m]
        work[pl.ds(keep, piece)] = total
        lo, length, step = keep, piece, step + len(flips)
    slot = 0
    for group in groups:
        own = work.at[pl.ds(lo, length)]
        if len(group) == 1:
            exchange(step, group[0], own, double_buf.at[slot])
            work[pl.ds(lo, length)] = own[...] + double_buf[slot]
            slot, step = slot + 1, step + 1
            continue
        flips = [(group[0],), (group[1],), (group[0], group[1])]
        copies = [start_copy(step + m, f, own, double_buf.at[slot + m]) for m, f in enumerate(flips)]
        for copy in copies:
            copy.wait()
        near, far = double_buf[slot] + own[...], double_buf[slot + 1] + double_buf[slot + 2]
        work[pl.ds(lo, length)] = near + far
        slot, step = slot + 3, step + 3
    o_ref[pl.ds(lo, length)] = work[pl.ds(lo, length)]
    for group in reversed(halving_groups(bits, halvings)):
        flips = [group] if len(group) == 1 else [group[:1], group[1:], group]
        region = o_ref.at[pl.ds(lo, length)]
        copies = [start_copy(step + m, flip, region, region) for m, flip in enumerate(flips)]
        for copy in copies:
            copy.wait()
        mine = 0
        for pair in group:
            mine = 2 * mine + bit_of(pair)
        lo = pl.multiple_of(lo - mine * length, 8)
        length, step = length << len(group), step + len(flips)
    for copy in halo:
        copy.wait()
    start = 0
    for out in outs:
        out[...] = o_ref[pl.ds(start, out.shape[0])]
        start += out.shape[0]


def allreduce(flat, splits, pieces=(), halvings=HALVINGS):
    offsets = NEIGHBOURS[: len(pieces)]
    pieces = [p.reshape(-1, 128) for p in pieces]
    bits = mesh_bits()
    halvings = min(halvings, len(bits))
    rows = flat.shape[0]
    segment = rows >> halvings
    far = len(bits) - halvings
    slots = 3 * (far // 2) + far % 2
    steps = 2 * sum((1 << len(g)) - 1 for g in halving_groups(bits, halvings)) + slots
    scratch, length = [], rows
    for group in halving_groups(bits, halvings):
        length >>= len(group)
        scratch.append(pltpu.VMEM(((1 << len(group)) - 1, length, 128), jnp.float32))
    scratch += [
        pltpu.VMEM(flat.shape, jnp.float32),
        pltpu.VMEM((max(slots, 1), segment, 128), jnp.float32),
        pltpu.SemaphoreType.DMA((steps,)),
        pltpu.SemaphoreType.DMA((steps,)),
        pltpu.SemaphoreType.DMA((max(len(pieces), 1),)),
        pltpu.SemaphoreType.DMA((max(len(pieces), 1),)),
        pltpu.VMEM(flat.shape, jnp.float32),
    ]
    vmem = pl.BlockSpec(memory_space=pltpu.VMEM)
    outs = pl.pallas_call(
        functools.partial(allreduce_kernel, bits, halvings, offsets),
        out_shape=[jax.ShapeDtypeStruct((rows_out, 128), jnp.float32) for rows_out in splits]
        + [jax.ShapeDtypeStruct(p.shape, p.dtype) for p in pieces],
        in_specs=[vmem] * (1 + len(pieces)),
        out_specs=[vmem] * (len(splits) + len(pieces)),
        scratch_shapes=scratch,
        compiler_params=pltpu.CompilerParams(collective_id=0, has_side_effects=True),
    )(flat, *pieces)
    return outs[: len(splits)], outs[len(splits) :]


def summed_gradients(local_conv, local_down, pieces, scale):
    sizes = (local_conv.size, local_down.size)
    flat = jnp.concatenate([local_conv.reshape(-1), local_down.reshape(-1)]) * scale
    unit = 128 * 8 << HALVINGS
    padded = -(-flat.size // unit) * unit
    flat = jnp.pad(flat, (0, padded - flat.size)).reshape(-1, 128)
    (conv_rows, down_rows), got = allreduce(flat, (sizes[0] // 128, sizes[1] // 128), [as_rows(p) for p in pieces])
    return (
        conv_rows.reshape(local_conv.shape),
        down_rows.reshape(local_down.shape),
        [from_rows(g, p.shape) for g, p in zip(got, pieces)],
    )


def body(features, conv_weight, down_weight, cotangent):
    channels, plane_count, row_count, breadth = features.shape
    out_channels = down_weight.shape[2]
    cell_count = plane_count * row_count * breadth * lax.axis_size("gz") * lax.axis_size("gy")
    grad_scale = 1.0 / math.sqrt(cell_count)
    received = halo_swap(halo_pieces(features), 1)
    received, down_weight, cotangent = lax.optimization_barrier((received, down_weight, cotangent))
    columns = widen(framed(features, received))
    preact = conv_taps(columns, conv_weight, features.shape)
    hidden = jax.nn.silu(preact).astype(jnp.bfloat16)
    blocks = hidden.reshape(channels, plane_count // 2, 2, row_count // 2, 2, breadth // 2, 2)
    down_split = down_weight.reshape(2, 2, out_channels, 2, channels)
    coarse = jnp.einsum(
        "aboei,iZaYbXe->oZYX", down_split, blocks, preferred_element_type=jnp.float32
    )
    section_out = coarse.reshape(out_channels, plane_count // 2, -1).astype(jnp.bfloat16)
    coarse_cot = cotangent.reshape(out_channels, plane_count // 2, row_count // 2, breadth // 2)
    hidden_grad = jnp.einsum(
        "aboei,oZYX->iZaYbXe", down_split, coarse_cot, preferred_element_type=jnp.float32
    )
    hidden_grad = hidden_grad.reshape(channels, plane_count, row_count, breadth)
    local_down = jnp.einsum(
        "oZYX,iZaYbXe->aboei", coarse_cot, blocks, preferred_element_type=jnp.float32
    )
    local_down = local_down.reshape(2, 2, out_channels, 2 * channels)
    gate_sig = jax.nn.sigmoid(preact)
    gate_grad = (hidden_grad * gate_sig * (1.0 + preact * (1.0 - gate_sig))).astype(jnp.bfloat16)
    kernel_rows = []
    for tap_z in range(3):
        row_list = []
        for tap_y in range(3):
            window = columns[:, tap_z : tap_z + plane_count, tap_y : tap_y + row_count]
            row_list.append(
                jnp.einsum("ozyx,jzyx->oj", gate_grad, window, preferred_element_type=jnp.float32)
            )
        kernel_rows.append(jnp.stack(row_list, axis=0))
    local_conv = jnp.stack(kernel_rows, axis=0)
    summed_conv, summed_down, got = summed_gradients(local_conv, local_down, halo_pieces(gate_grad), grad_scale)
    gate_columns = widen(framed(gate_grad, got))
    grad_field = conv_taps(gate_columns, transposed_weight(conv_weight), features.shape)
    return (section_out, grad_field, summed_conv, summed_down)


def solution(mesh):
    return jax.shard_map(
        body,
        mesh=mesh,
        in_specs=(P(None, "gz", "gy", None), P(), P(), P(None, "gz", "gy")),
        out_specs=(P(None, "gz", "gy"), P(None, "gz", "gy", None), P(), P()),
        check_vma=False,
    )
```
